32 devices in a mesh: section: 2 (over core), expert: 16 (over z, y, x).
Axes of the slice: x: 2, y: 2, z: 4, core: 2. Of those that a mesh axis runs over, the one named last changes fastest.
Arguments:
- block_input: bfloat16 [2, 8192, 768], P(None, 'expert'), may hold values from -6 to 6
- cotangent: bfloat16 [2, 8192, 768], P(None, 'expert'), may hold values from -6 to 6
- expert_ids: int32 [2, 2, 8192, 2], P(None, None, 'expert'), may hold values from 0 to 15, all different within a row; in each aligned block of 512 rows (0 to 511, 512 to 1023, ..., all dimensions but the last counted through in order) at most 68 rows name the same one
- qkv_weight: bfloat16 [2, 768, 2304], P('section'), may hold values from -0.21875 to 0.21875
- query_bias: float32 [2, 768], P('section'), may hold values from -4 to 4
- value_bias: float32 [2, 768], P('section'), may hold values from -1.5 to 1.5
- proj_weight: bfloat16 [2, 768, 768], P('section'), may hold values from -1.75 to 1.75
- proj_bias: float32 [2, 768], P('section'), may hold values from -4 to 4
- attn_gain: float32 [2, 768], P('section'), may hold values from 0.25 to 1.75
- ffn_gain: float32 [2, 768], P('section'), may hold values from 0.25 to 1.75
- router_weight: bfloat16 [2, 768, 16], P('section'), may hold values from -0.4375 to 0.4375
- in_weight: bfloat16 [2, 16, 768, 3072], P('section', 'expert'), may hold values from -0.21875 to 0.21875
- out_weight: bfloat16 [2, 16, 3072, 768], P('section', 'expert'), may hold values from -0.109375 to 0.109375
Outputs:
- section_out: bfloat16 [2, 2, 8192, 768], P('section', None, 'expert')
- section_grad: float32 [2, 2, 8192, 768], P('section', None, 'expert')
- grad_qkv: float32 [2, 768, 2304], P('section')
- grad_qbias: float32 [2, 768], P('section')
- grad_vbias: float32 [2, 768], P('section')
- grad_proj: float32 [2, 768, 768], P('section')
- grad_pbias: float32 [2, 768], P('section')
- grad_attngain: float32 [2, 768], P('section')
- grad_ffngain: float32 [2, 768], P('section')
- grad_router: float32 [2, 768, 16], P('section')
- grad_win: bfloat16 [2, 16, 768, 3072], P('section', 'expert')
- grad_wout: bfloat16 [2, 16, 3072, 768], P('section', 'expert')
The draws below stay inside these ranges and needn't reach their ends.
Inputs may be any that keep to these rules, and one draw needn't show every extreme that they name: `expert_ids`: A token's 2 ids differ. For each layer and micro-batch, among the choices of the 512 tokens of one device, no expert is named more than 68 times, a bound that some block reaches.
All inputs are finite; a program needn't handle non-finite values.
Results may differ from the reference program's by a relative error of at most 0.02.
Values may be sent and summed in bfloat16 or wider, within the bound.
A program may use at most 384 MiB of HBM per device.

```python
import math
import jax
import jax.numpy as jnp
import numpy as np
from jax import lax

D = 768
H = 12
HD = 64
FF = 3072
TOP = 2
SEQ = 512
MICRO = 2
TOK_DEV = 512
EXPERTS = 16
TOKENS = 8192
CAP = 68
N_EXPERT = 16


def shard_levels(key, shape, split, low, top_value):
    factor_of, own = 1.0, jax.random.fold_in(key, 6)
    for position, shards_of in split:
        heights = jnp.exp(jax.random.uniform(jax.random.fold_in(own, position), (shards_of,), jnp.float32, low / len(split), top_value / len(split)))
        factor_of = factor_of * jnp.repeat(heights, shape[position] // shards_of).reshape([-1 if axis == position else 1 for axis in range(len(shape))])
    return factor_of


def deal_out(stream_key, own, number, rows, amount, top, limit, lean):
    order = jax.random.permutation(stream_key, amount)
    heavy_load, common = load_shares(amount, rows * top, limit, lean, True), load_shares(amount, rows * top, limit, lean, False)
    places = jnp.arange(amount)

    def named(lengths, rotation):
        used = int((lengths > 0).sum())
        fixed = max(1, used // 4)
        shifted = fixed + (places - fixed + rotation * (used - fixed)) % max(1, amount - fixed)
        return jnp.zeros((amount,), jnp.int32).at[order[jnp.where(places < fixed, places, shifted)]].set(jnp.asarray(lengths, jnp.int32))

    lengths = jnp.where(number % 4 == 0, named(heavy_load, number // 4), named(common, number - number // 4 - 1))
    mixed = jax.random.permutation(jax.random.fold_in(own, 3), amount)
    donor, sink = mixed[0:amount // 2 * 2:2], mixed[1:amount // 2 * 2:2]
    room = jnp.minimum(lengths[donor] - 1, limit - lengths[sink]) // 2
    room = jnp.where((donor == order[0]) | (sink == order[0]) | (lengths[sink] == 0), 0, jnp.maximum(room, 0))
    shifted = jax.random.randint(jax.random.fold_in(own, 4), (amount // 2,), 0, 1 << 20) % (room + 1)
    lengths = lengths.at[donor].add(-shifted).at[sink].add(shifted)
    items = jnp.searchsorted(jnp.cumsum(lengths), jnp.arange(rows * top), side="right").astype(jnp.int32)
    table = items.reshape(top, rows).T
    table = table[jax.random.permutation(jax.random.fold_in(own, 1), rows)]
    rotation = jax.random.randint(jax.random.fold_in(own, 2), (rows, 1), 0, top)
    return jnp.take_along_axis(table, (jnp.arange(top)[None, :] + rotation) % top, axis=1)


def load_shares(count, total, limit, slope, full):
    weights = [(1 << 20) // math.isqrt(grade ** slope) + 1 for grade in range(1, count + 1)]
    largest = limit if full else min(limit, max(-(-total // count), total * weights[0] // sum(weights)))
    least = 1 if total - largest >= count - 1 else 0
    given, surplus = [largest] + [least] * (count - 1), total - largest - least * (count - 1)
    while surplus > 0:
        movable = [i for i in range(1, count) if given[i] < largest] or [i for i in range(1, count) if given[i] < limit]
        pool, budget = sum([weights[i] for i in movable]), surplus
        for i in movable:
            more = min(limit - given[i], max(1, budget * weights[i] // pool), surplus)
            given[i] = given[i] + more
            surplus = surplus - more
    return np.array(given)


def scatter_about(own_key, extent, deviation, reach, pieces=(), held_as=jnp.bfloat16):
    drawn = jax.random.normal(own_key, extent, jnp.float32) * deviation
    if len(pieces) > 0:
        drawn = shard_levels(own_key, extent, pieces, -0.22, 0.18) * drawn
    return jnp.clip(drawn, min=-reach, max=reach).astype(held_as)


def setup_inputs(seed: int = 0) -> dict:
    splits = jax.random.split(jax.random.key(seed), 14)
    block_input = scatter_about(splits[0], (MICRO, TOKENS, D), 1.0, 6.0, ((1, 16),))
    cotangent = scatter_about(splits[1], (MICRO, TOKENS, D), 1.0, 6.0, ((1, 16),))
    expert_ids_keys = jax.random.split(jax.random.fold_in(splits[2], 1), 2 * MICRO * TOKENS // TOK_DEV)
    expert_ids_turns = jax.random.permutation(jax.random.fold_in(splits[2], 3), 2 * MICRO * TOKENS // TOK_DEV)
    expert_ids = jax.vmap(lambda own, number: deal_out(jax.random.fold_in(splits[2], 2), own, number, TOK_DEV, EXPERTS, TOP, CAP, 2))(expert_ids_keys, expert_ids_turns).reshape((2, MICRO, TOKENS, TOP))
    qkv_weight = scatter_about(splits[3], (2, D, 3 * D), D ** -0.5, 0.21875, ((0, 2),))
    query_bias = scatter_about(splits[4], (2, D), 0.3, 4.0, ((0, 2),), jnp.float32)
    value_bias = scatter_about(splits[5], (2, D), 0.1, 1.5, ((0, 2),), jnp.float32)
    proj_weight = scatter_about(splits[6], (2, D, D), (D // 64) ** -0.5, 1.75, ((0, 2),))
    proj_bias = scatter_about(splits[7], (2, D), 0.3, 4.0, ((0, 2),), jnp.float32)
    attn_gain = jnp.clip(1.0 + 0.15 * jax.random.normal(splits[8], (2, D), jnp.float32), 0.25, 1.75)
    ffn_gain = jnp.clip(1.0 + 0.15 * jax.random.normal(splits[9], (2, D), jnp.float32), 0.25, 1.75)
    router_weight = scatter_about(splits[10], (2, D, EXPERTS), (D // 4) ** -0.5, 0.4375, ((0, 2),))
    in_weight = scatter_about(splits[11], (2, EXPERTS, D, FF), D ** -0.5, 0.21875, ((0, 2), (1, 16)))
    out_weight = scatter_about(splits[12], (2, EXPERTS, FF, D), FF ** -0.5, 0.109375, ((0, 2), (1, 16)))
    return dict(block_input=block_input, cotangent=cotangent, expert_ids=expert_ids, qkv_weight=qkv_weight, query_bias=query_bias, value_bias=value_bias, proj_weight=proj_weight, proj_bias=proj_bias, attn_gain=attn_gain, ffn_gain=ffn_gain, router_weight=router_weight, in_weight=in_weight, out_weight=out_weight)


HIGH = lax.Precision.HIGHEST
EPS = 1e-06
NEG = -1e+30

@jax.custom_vjp
def low(v):
    return lax.optimization_barrier(v.astype(jnp.bfloat16)).astype(jnp.float32)

@jax.custom_vjp
def low_back(v):
    return v

def reduced_precision_saved(v):
    return (low(v), None)

def low_pass(kept, grad):
    return (grad,)

def back_keep(v):
    return (v, None)

def back_low(kept, grad):
    return (low(grad),)
low.defvjp(reduced_precision_saved, low_pass)
low_back.defvjp(back_keep, back_low)

def norm_apply(field, scaling):
    return field * lax.rsqrt(lax.optimization_barrier(jnp.mean(field * field, axis=-1, keepdims=True)) + EPS) * scaling

def router_gates(logits, choose):
    probs_all = jax.nn.softmax(logits, axis=-1)
    picked = lax.optimization_barrier(jnp.sum(probs_all[:, None, :] * choose, axis=-1))
    return picked / lax.optimization_barrier(jnp.sum(picked, axis=-1, keepdims=True))

def attend_one(queries, key_rows, value_rows):
    scores = jnp.einsum('qhd,khd->hqk', queries, key_rows, precision=HIGH) * HD ** (-0.5)
    scores = low_back(scores)
    length = scores.shape[-1]
    causal = jnp.arange(length)[:, None] >= jnp.arange(length)[None, :]
    scores = jnp.where(causal[None], scores, NEG)
    weights = low(jax.nn.softmax(scores, axis=-1))
    return jnp.einsum('hqk,khd->qhd', weights, value_rows, precision=HIGH)

def expert_layer(routed, route_ids, gating, in_weight, out_weight):
    blocks = N_EXPERT
    per_block = routed.shape[0] // blocks
    flat_ids = route_ids.reshape(blocks, per_block * TOP)
    marked = (flat_ids[:, :, None] == jnp.arange(EXPERTS, dtype=jnp.int32)[None, None, :]).astype(jnp.int32)
    ranked = lax.optimization_barrier(jnp.sum(jnp.cumsum(marked, axis=1) * marked, axis=-1)) - 1
    slot_ids = (flat_ids * CAP + ranked).astype(jnp.int32)
    lane_ids = jnp.repeat(jnp.arange(blocks, dtype=jnp.int32)[:, None], per_block * TOP, axis=1)
    copies = low_back(jnp.repeat(routed.reshape(blocks, per_block, D), TOP, axis=1))
    buffer = jnp.zeros((blocks, EXPERTS * CAP, D), jnp.float32).at[lane_ids, slot_ids].set(copies)
    buffer = buffer.reshape(blocks, EXPERTS, CAP, D)
    hidden = low_back(jnp.einsum('necd,edf->necf', buffer, in_weight, precision=HIGH))
    active = low(jax.nn.gelu(hidden))
    result = low_back(low(jnp.einsum('necf,efd->necd', active, out_weight, precision=HIGH)))
    picked = result.reshape(blocks, EXPERTS * CAP, D)[lane_ids, slot_ids]
    picked = picked.reshape(blocks * per_block, TOP, D)
    return lax.optimization_barrier(jnp.sum(gating[:, :, None] * picked, axis=1))

def layer_apply(params, route_ids, inputs):
    qkv_w, qbias, vbias, proj_w, pbias, gain_attn, gain_ffn, router_w, win_all, wout_all = params
    tokens = inputs.shape[0]
    normed = low(norm_apply(inputs, gain_attn))
    packed = jnp.dot(normed, qkv_w, precision=HIGH)
    queries = low_back(low(packed[:, :D] + qbias))
    key_rows = low_back(low(packed[:, D:2 * D]))
    value_rows = low_back(low(packed[:, 2 * D:] + vbias))
    grid_shape = (tokens // SEQ, SEQ, H, HD)
    attended = lax.map(lambda trio: jax.checkpoint(attend_one)(*trio), (queries.reshape(grid_shape), key_rows.reshape(grid_shape), value_rows.reshape(grid_shape)))
    attended = low_back(low(attended.reshape(tokens, D)))
    branch = low_back(jnp.dot(attended, proj_w, precision=HIGH) + pbias)
    between_sections = inputs + branch
    routed = low(norm_apply(between_sections, gain_ffn))
    logits = jnp.dot(routed, router_w, precision=HIGH)
    choose = (route_ids[:, :, None] == jnp.arange(EXPERTS, dtype=jnp.int32)[None, None, :]).astype(jnp.float32)
    gating = router_gates(logits, choose)
    mixture = expert_layer(routed, route_ids, gating, win_all, wout_all)
    return between_sections + mixture

def reference(block_input, cotangent, expert_ids, qkv_weight, query_bias, value_bias, proj_weight, proj_bias, attn_gain, ffn_gain, router_weight, in_weight, out_weight):
    params = tuple((weight_set.astype(jnp.float32) for weight_set in (qkv_weight, query_bias, value_bias, proj_weight, proj_bias, attn_gain, ffn_gain, router_weight, in_weight, out_weight)))
    firsts = []
    seconds = []
    grads_in = []
    grads_mid = []
    totals = None
    for step_index in range(MICRO):

        def forward(weight_sets, inputs, probe_zero):
            first_out = layer_apply(tuple((weight_set[0] for weight_set in weight_sets)), expert_ids[0, step_index], inputs)
            handed = low(first_out)
            second = layer_apply(tuple((weight_set[1] for weight_set in weight_sets)), expert_ids[1, step_index], low_back(handed + probe_zero))
            return (second, handed)
        inputs = block_input[step_index].astype(jnp.float32)
        second, pullback, handed = jax.vjp(forward, params, inputs, jnp.zeros_like(inputs), has_aux=True)
        grad_params, grad_inputs, grad_probe = pullback(cotangent[step_index].astype(jnp.float32))
        if totals is None:
            totals = grad_params
        else:
            totals = jax.tree.map(jnp.add, totals, grad_params)
        firsts.append(handed)
        seconds.append(second)
        grads_in.append(grad_inputs)
        grads_mid.append(grad_probe)
    section_out = jnp.stack([jnp.stack(firsts), jnp.stack(seconds)]).astype(jnp.bfloat16)
    section_grad = jnp.stack([jnp.stack(grads_in), jnp.stack(grads_mid)])
    return (section_out, section_grad, totals[0], totals[1], totals[2], totals[3], totals[4], totals[5], totals[6], totals[7], totals[8].astype(jnp.bfloat16), totals[9].astype(jnp.bfloat16))
```

```python
import functools

import jax
import jax.numpy as jnp
from jax import lax
from jax.experimental import pallas as pl
from jax.experimental.pallas import tpu as pltpu
from jax.sharding import PartitionSpec as P

HD = 64
EPS = 1e-06
NEG = -1e30
BF = jnp.bfloat16
F32 = jnp.float32
HIGH = lax.Precision.HIGHEST
SWAP = [(0, 1), (1, 0)]
MESH = pl.DeviceIdType.MESH
NN = ((1,), (0,))
NT = ((1,), (1,))
TN = ((0,), (0,))
PLANES = 4
CHUNK = 512


def dot(a, b, dims, kind=F32, precision=None):
    return lax.dot_general(
        a, b, (dims, ((), ())), precision=precision, preferred_element_type=F32
    ).astype(kind)


def capacity_of(tokens, choices, experts):
    return tokens * choices // experts + max(1, tokens * choices // (16 * experts))


def inverse_rms(field):
    return lax.rsqrt(jnp.mean(field * field, axis=-1, keepdims=True) + EPS)


def norm_back(field, gain, grad):
    scale = inverse_rms(field)
    unit = field * scale
    grad_gain = jnp.sum(grad * unit, axis=0)
    scaled = grad * gain
    grad_field = scale * (scaled - unit * jnp.mean(scaled * unit, axis=-1, keepdims=True))
    return grad_field, grad_gain


def causal_scores(queries, key_rows):
    scores = jnp.einsum(
        "qhd,khd->hqk", queries, key_rows, preferred_element_type=F32
    ) * HD ** (-0.5)
    length = scores.shape[-1]
    causal = jnp.arange(length)[:, None] >= jnp.arange(length)[None, :]
    return jnp.where(causal[None], scores, NEG)


def attend_forward(queries, key_rows, value_rows):
    tokens, width = queries.shape
    shape = (tokens, width // HD, HD)
    scores = causal_scores(queries.reshape(shape), key_rows.reshape(shape))
    row_max = jnp.max(scores, axis=-1, keepdims=True)
    weights = jnp.exp(scores - row_max)
    row_total = jnp.sum(weights, axis=-1, keepdims=True)
    prob_low = (weights / row_total).astype(BF)
    attended = jnp.einsum(
        "hqk,khd->qhd", prob_low, value_rows.reshape(shape), preferred_element_type=F32
    )
    return (
        attended.astype(BF).reshape(tokens, width),
        row_max[..., 0] + jnp.log(row_total[..., 0]),
    )


def attend_backward(queries, key_rows, value_rows, log_total, grad_out):
    tokens, width = queries.shape
    shape = (tokens, width // HD, HD)
    queries, key_rows, value_rows, grad_out = (
        part.reshape(shape) for part in (queries, key_rows, value_rows, grad_out)
    )
    scores = causal_scores(queries, key_rows)
    weights = jnp.exp(scores - log_total[..., None])
    grad_probs = jnp.einsum("qhd,khd->hqk", grad_out, value_rows, preferred_element_type=F32)
    inner = jnp.sum(weights * grad_probs, axis=-1, keepdims=True)
    grad_scores = (weights * (grad_probs - inner)).astype(BF)
    grad_value = jnp.einsum(
        "hqk,qhd->khd", weights.astype(BF), grad_out, preferred_element_type=F32
    )
    grad_query = jnp.einsum(
        "hqk,khd->qhd", grad_scores, key_rows, preferred_element_type=F32
    ) * HD ** (-0.5)
    grad_key = jnp.einsum(
        "hqk,qhd->khd", grad_scores, queries, preferred_element_type=F32
    ) * HD ** (-0.5)
    return tuple(
        part.astype(BF).reshape(tokens, width) for part in (grad_query, grad_key, grad_value)
    )


def gelu_and_slope(hidden):
    root = 0.7978845608028654
    square = hidden * hidden
    bent = jnp.tanh(hidden * (root + (root * 0.044715) * square))
    half = 0.5 + 0.5 * bent
    slope = half + (0.5 * hidden) * (1.0 - bent * bent) * (root + (root * 0.134145) * square)
    return hidden * half, slope


def moe_kernel(experts, extra, ahead, back, *refs):
    refs = list(refs)

    def take(count):
        taken, refs[:count] = refs[:count], []
        return taken

    rows_in, grads_in, kept_in = [], [], []
    if ahead:
        rows_in = take(2)
    if back:
        grads_in = take(2)
    if back and not ahead:
        kept_in = take(2)
    win_hbm, wout_hbm = take(2)
    produced_out = take(2) if ahead else []
    kept_out = take(2) if ahead and not back else []
    returned_out = take(2) if back else []
    gwin_out, gwout_out = take(2) if back else (None, None)
    win, wout, weight_sem = take(3)
    if ahead:
        row_land, row_land_x, row_stage, row_stage_x, row_acc = take(5)
    if back:
        grad_land, grad_land_x, grad_stage, grad_stage_x, grad_acc, gwin, gwout = take(7)
        fold, fold_sem = take(2)
    send_sems, recv_sems, send_x_sems, recv_x_sems = take(4)

    per = experts // PLANES
    main = (rows_in or grads_in)[0].shape[1]
    ff = win.shape[1]
    chunks = ff // CHUNK
    me = lax.axis_index("expert")
    plane = me // per
    spot = me % per
    half, low = plane // 2, plane % 2
    order = [
        (1 - half) * 2 + low,
        (1 - half) * 2 + (1 - low),
        half * 2 + (1 - low),
        plane,
    ]

    barrier = pltpu.get_barrier_semaphore()

    def greet(step, carry):
        pl.semaphore_signal(
            barrier, inc=1, device_id={"expert": (me + step) % experts}, device_id_type=MESH
        )
        return carry

    load_in = pltpu.make_async_copy(win_hbm, win, weight_sem.at[0])
    load_out = pltpu.make_async_copy(wout_hbm, wout, weight_sem.at[1])
    load_in.start()
    load_out.start()
    lax.fori_loop(1, experts, greet, 0)
    pl.semaphore_wait(barrier, experts - 1)

    def send(source, target, lane, peer, to_plane):
        pltpu.make_async_remote_copy(
            src_ref=source.at[peer],
            dst_ref=target.at[me],
            send_sem=send_sems.at[lane],
            recv_sem=recv_sems.at[lane, plane],
            device_id={"expert": peer},
            device_id_type=MESH,
        ).start()

    def send_x(source, target, lane, peer):
        pltpu.make_async_remote_copy(
            src_ref=source.at[peer],
            dst_ref=target.at[me],
            send_sem=send_x_sems.at[lane],
            recv_sem=recv_x_sems.at[lane],
            device_id={"expert": peer},
            device_id_type=MESH,
        ).start()

    def own(source, target, sem):
        pltpu.make_async_copy(source.at[me], target.at[me], sem).start()

    def send_all_x(pairs):
        def one(step, carry):
            for source, target, lane in pairs:
                send_x(source, target, lane, (me + step) % experts)
            return carry

        lax.fori_loop(1, experts, one, 0)
        for source, target, lane in pairs:
            own(source, target, recv_x_sems.at[lane])

    def send_plane(pairs, to_plane, is_own):
        def one(step, carry):
            for source, target, lane in pairs:
                send(source, target, lane, to_plane * per + (spot + step) % per, to_plane)
            return carry

        lax.fori_loop(1 if is_own else 0, per, one, 0)
        if is_own:
            for source, target, lane in pairs:
                own(source, target, recv_sems.at[lane, plane])

    def wait_plane(target, lane, from_plane):
        part = target.at[pl.ds(from_plane * per, per)]
        pltpu.make_async_copy(part, part, recv_sems.at[lane, from_plane]).wait()

    def wait_x(target, lane):
        pltpu.make_async_copy(target, target, recv_x_sems.at[lane]).wait()

    def wait_sent(source, lane):
        part = source.at[pl.ds(0, experts - 1)]
        pltpu.make_async_copy(part, part, send_sems.at[lane]).wait()

    def wait_sent_x(source, lane):
        part = source.at[pl.ds(0, experts - 1)]
        pltpu.make_async_copy(part, part, send_x_sems.at[lane]).wait()

    first_pairs, first_x = [], []
    if ahead:
        first_pairs.append((rows_in[0], row_land, 0))
        first_x.append((rows_in[1], row_land_x, 0))
    if back:
        first_pairs.append((grads_in[0], grad_land, 1))
        first_x.append((grads_in[1], grad_land_x, 1))
    send_all_x(first_x)
    for at, to_plane in enumerate(order):
        send_plane(first_pairs, to_plane, at == 3)

    tall = experts * 16
    tile_rows = lax.broadcasted_iota(jnp.int32, (experts * extra, tall), 0)
    tile_cols = lax.broadcasted_iota(jnp.int32, (experts * extra, tall), 1)
    parts = win.shape[0] // 256
    picks = [
        (tile_cols == (tile_rows // extra) * 16 + q * extra + tile_rows % extra).astype(BF)
        for q in range(parts)
    ]

    def gather_x(landed):
        flat = landed[...].reshape(tall, 256)
        return jnp.concatenate([dot(pick, flat, NN, BF) for pick in picks], axis=1)

    def spread_x(values):
        total = dot(picks[0], values[:, :256], TN)
        for q in range(1, parts):
            total += dot(picks[q], values[:, q * 256 : (q + 1) * 256], TN)
        return total.astype(BF).reshape(experts, 16, 256)

    def run(rows, grads, is_first):
        count = (rows if rows is not None else grads).shape[0]

        def one(step, carry):
            cols = pl.ds(pl.multiple_of(step * CHUNK, CHUNK), CHUNK)
            wide = win[:, cols]
            deep = wout[cols, :]
            active, slope = gelu_and_slope(dot(rows, wide, NN))
            active = active.astype(BF)
            if ahead:
                row_acc[pl.ds(0, count)] += dot(active, deep, NN)
            if back:
                grad_hidden = (dot(grads, deep, NT) * slope).astype(BF)
                grad_acc[pl.ds(0, count)] += dot(grad_hidden, wide, NT)
                term_in = dot(rows, grad_hidden, TN)
                term_out = dot(active, grads, TN)
                if is_first:
                    gwin[:, cols] = term_in
                    gwout[cols, :] = term_out
                else:
                    gwin[:, cols] += term_in
                    gwout[cols, :] += term_out
            return carry

        if ahead:
            row_acc[pl.ds(0, count)] = jnp.zeros((count, row_acc.shape[1]), F32)
        if back:
            grad_acc[pl.ds(0, count)] = jnp.zeros((count, grad_acc.shape[1]), F32)
        lax.fori_loop(0, chunks, one, 0)

    last_pairs, last_x = [], []
    if ahead:
        last_pairs.append((row_stage, produced_out[0], 2))
        last_x.append((row_stage_x, produced_out[1], 2))
        wait_x(row_land_x, 0)
    if back:
        last_pairs.append((grad_stage, returned_out[0], 3))
        last_x.append((grad_stage_x, returned_out[1], 3))
        wait_x(grad_land_x, 1)
    load_in.wait()
    load_out.wait()

    few = experts * extra
    if ahead:
        rows_x = gather_x(row_land_x)
        if kept_out:
            kept_out[1][...] = rows_x
    else:
        rows_x = kept_in[1][...]
    grads_x = gather_x(grad_land_x) if back else None
    run(rows_x, grads_x, True)
    if ahead:
        row_stage_x[...] = spread_x(row_acc[pl.ds(0, few)].astype(BF))
    if back:
        grad_stage_x[...] = spread_x(grad_acc[pl.ds(0, few)].astype(BF))
    send_all_x(last_x)

    width = win.shape[0]
    block = per * main
    for at in (3, 0, 1, 2):
        from_plane = order[at]
        places = pl.ds(from_plane * per, per)
        rows = grads = None
        if ahead:
            wait_plane(row_land, 0, from_plane)
            rows = row_land[places].reshape(block, width)
            if kept_out:
                kept_out[0][places] = row_land[places]
        else:
            rows = kept_in[0][places].reshape(block, width)
        if back:
            wait_plane(grad_land, 1, from_plane)
            grads = grad_land[places].reshape(block, width)
        run(rows, grads, False)
        if ahead:
            row_stage[places] = row_acc[...].astype(BF).reshape(per, main, width)
        if back:
            grad_stage[places] = grad_acc[...].astype(BF).reshape(per, main, width)
        send_plane(last_pairs, from_plane, at == 3)

    if back:
        for at in range(chunks):
            slot = at % 2
            span = slice(at * CHUNK, (at + 1) * CHUNK)
            if at >= 2:
                pltpu.make_async_copy(
                    fold.at[slot], gwin_out.at[:, span], fold_sem.at[slot]
                ).wait()
            fold[slot] = gwin[:, span].astype(BF)
            pltpu.make_async_copy(fold.at[slot], gwin_out.at[:, span], fold_sem.at[slot]).start()
        for slot in range(2):
            pltpu.make_async_copy(
                fold.at[slot], gwin_out.at[:, slice(0, CHUNK)], fold_sem.at[slot]
            ).wait()
        rows_of = ff // 6
        for at in range(6):
            span = slice(at * rows_of, (at + 1) * rows_of)
            wout[span, :] = gwout[span, :].astype(BF)
            pltpu.make_async_copy(wout.at[span, :], gwout_out.at[span, :], weight_sem.at[1]).start()
        pltpu.make_async_copy(wout, gwout_out, weight_sem.at[1]).wait()

    for source, target, lane in first_pairs:
        wait_sent(source, lane)
    for source, target, lane in first_x + last_x:
        wait_sent_x(source, lane)
    for source, target, lane in last_pairs:
        wait_sent(source, lane)
        for from_plane in range(PLANES):
            wait_plane(target, lane, from_plane)
    for source, target, lane in last_x:
        wait_x(target, lane)


def moe(ahead, back, collective, extra, rows, grads, kept, win, wout):
    lead = rows if ahead else grads
    experts, main, width = lead[0].shape
    ff = win.shape[1]
    few = experts * extra
    per = experts // PLANES
    block = per * main
    tall = jax.ShapeDtypeStruct((experts, main, width), BF)
    small = jax.ShapeDtypeStruct((experts, 16, 256), BF)
    vmem = pl.BlockSpec(memory_space=pltpu.VMEM)
    hbm = pl.BlockSpec(memory_space=pl.ANY)
    operands, in_specs = [], []
    for pair in (rows if ahead else (), grads if back else (), kept if back and not ahead else ()):
        operands += list(pair)
        in_specs += [vmem] * len(pair)
    operands += [win, wout]
    in_specs += [hbm, hbm]
    out_shape, out_specs = [], []
    if ahead:
        out_shape += [tall, small]
        out_specs += [vmem, vmem]
        if not back:
            out_shape += [tall, jax.ShapeDtypeStruct((few, width), BF)]
            out_specs += [vmem, vmem]
    if back:
        out_shape += [tall, small]
        out_specs += [vmem, vmem]
        out_shape += [
            jax.ShapeDtypeStruct((width, ff), BF),
            jax.ShapeDtypeStruct((ff, width), BF),
        ]
        out_specs += [hbm, hbm]
    scratch = [
        pltpu.VMEM((width, ff), BF),
        pltpu.VMEM((ff, width), BF),
        pltpu.SemaphoreType.DMA((2,)),
    ]
    work = [
        pltpu.VMEM((experts, main, width), BF),
        pltpu.VMEM((experts, 16, 256), BF),
        pltpu.VMEM((experts, main, width), BF),
        pltpu.VMEM((experts, 16, 256), BF),
        pltpu.VMEM((max(block, few), width), F32),
    ]
    if ahead:
        scratch += work
    if back:
        scratch += work + [
            pltpu.VMEM((width, ff), F32),
            pltpu.VMEM((ff, width), F32),
            pltpu.VMEM((2, width, CHUNK), BF),
            pltpu.SemaphoreType.DMA((2,)),
        ]
    scratch += [
        pltpu.SemaphoreType.DMA((4,)),
        pltpu.SemaphoreType.DMA((4, PLANES)),
        pltpu.SemaphoreType.DMA((4,)),
        pltpu.SemaphoreType.DMA((4,)),
    ]
    return pl.pallas_call(
        functools.partial(moe_kernel, experts, extra, ahead, back),
        out_shape=out_shape,
        in_specs=in_specs,
        out_specs=out_specs,
        scratch_shapes=scratch,
        compiler_params=pltpu.CompilerParams(
            collective_id=collective, has_side_effects=True, vmem_limit_bytes=60 * 2**20
        ),
        name="moe_%d%d" % (ahead, back),
    )(*operands)


def route_plan(route_ids, experts, capacity):
    tokens = route_ids.shape[0]
    main = capacity // 16 * 16
    extra = capacity - main
    lanes = jnp.arange(experts, dtype=jnp.int32)[None, :]
    first = (route_ids[:, 0:1] == lanes).astype(F32)
    second = (route_ids[:, 1:2] == lanes).astype(F32)
    places = jnp.arange(tokens, dtype=jnp.int32)
    earlier = (places[:, None] > places[None, :]).astype(BF)
    counts = dot(earlier, (first + second).astype(BF), NN)
    row = jnp.arange(experts * main, dtype=jnp.int32)[:, None]
    row_x = jnp.arange(experts * 16, dtype=jnp.int32)[:, None]
    place, place_x = [], []
    for j, hot in enumerate((first, second)):
        rank = jnp.sum(counts * hot, axis=-1).astype(jnp.int32)
        slot = jnp.where(rank < main, route_ids[:, j] * main + rank, -1)
        slot_x = jnp.where(rank < main, -experts * 16, route_ids[:, j] * 16 + rank - main)
        place.append((row == slot[None, :]).astype(BF))
        place_x.append(
            [(row_x == slot_x[None, :] + q * extra).astype(BF) for q in range(16 // extra)]
        )
    return first, second, place, place_x


def pack(plan, experts, values0, values1=None):
    _, _, place, place_x = plan
    width = values0.shape[1]
    if values1 is None:
        main = dot(place[0] + place[1], values0, NN)
    else:
        main = dot(place[0], values0, NN) + dot(place[1], values1, NN)
    small = 0.0
    for q in range(width // 256):
        part = slice(q * 256, (q + 1) * 256)
        if values1 is None:
            small += dot(place_x[0][q] + place_x[1][q], values0[:, part], NN)
        else:
            small += dot(place_x[0][q], values0[:, part], NN)
            small += dot(place_x[1][q], values1[:, part], NN)
    return main.astype(BF).reshape(experts, -1, width), small.astype(BF).reshape(experts, 16, 256)


def unpack(place, place_x, main, small, width):
    main = main.reshape(-1, width)
    small = small.reshape(-1, 256)
    tail = [dot(place_x[q], small, TN) for q in range(width // 256)]
    return dot(place, main, TN) + jnp.concatenate(tail, axis=1)


def layer_attend(current, plan, weights):
    qkv, qbias, vbias, proj, pbias, gain_attn, gain_ffn, router, win, wout = weights
    first, second = plan[:2]
    width = current.shape[1]
    normed = (current * inverse_rms(current) * gain_attn).astype(BF)
    packed = dot(normed, qkv, NN)
    queries = (packed[:, :width] + qbias).astype(BF)
    key_rows = packed[:, width : 2 * width].astype(BF)
    value_rows = (packed[:, 2 * width :] + vbias).astype(BF)
    attended, log_total = attend_forward(queries, key_rows, value_rows)
    middle = current + (dot(attended, proj, NN) + pbias)
    routed = (middle * inverse_rms(middle) * gain_ffn).astype(BF)
    logits = dot(routed, router, NN)
    gap = jnp.sum(logits * (first - second), axis=-1, keepdims=True)
    gate0, gate1 = jax.nn.sigmoid(gap), jax.nn.sigmoid(-gap)
    return (
        current, normed, queries, key_rows, value_rows, log_total, attended, middle, routed,
        gate0, gate1,
    )


def layer_combine(kept, plan, produced):
    middle, gate0, gate1 = kept[7], kept[9], kept[10]
    _, _, place, place_x = plan
    width = middle.shape[1]
    combined = [
        unpack(place[j], place_x[j], produced[0], produced[1], width).astype(BF) for j in range(2)
    ]
    outputs = middle + (gate0 * combined[0].astype(F32) + gate1 * combined[1].astype(F32))
    return outputs, combined


def layer_grads(seed, kept, plan, experts):
    gate0, gate1 = kept[9], kept[10]
    return pack(plan, experts, (gate0 * seed).astype(BF), (gate1 * seed).astype(BF))


def layer_backward(seed, kept, combined, returned, plan, weights):
    qkv, qbias, vbias, proj, pbias, gain_attn, gain_ffn, router, win, wout = weights
    first, second, place, place_x = plan
    (
        current, normed, queries, key_rows, value_rows, log_total, attended, middle, routed,
        gate0, gate1,
    ) = kept
    combined0, combined1 = combined
    width = middle.shape[1]
    grad_gap = gate0 * gate1 * jnp.sum(
        seed * (combined0.astype(F32) - combined1.astype(F32)), axis=-1, keepdims=True
    )
    grad_logits = grad_gap * (first - second)
    grad_router = dot(grad_logits, routed.astype(F32), TN, precision=HIGH)
    both_x = [one + two for one, two in zip(place_x[0], place_x[1])]
    grad_routed = unpack(place[0] + place[1], both_x, returned[0], returned[1], width) + dot(
        grad_logits, router.astype(F32), NT, precision=HIGH
    )
    grad_middle, grad_gain_ffn = norm_back(middle, gain_ffn, grad_routed)
    grad_middle = grad_middle + seed
    grad_branch = grad_middle.astype(BF)
    grad_pbias = jnp.sum(grad_branch.astype(F32), axis=0)
    grad_proj = dot(attended, grad_branch, TN, BF)
    grad_attended = dot(grad_branch, proj, NT, BF)
    grad_query, grad_key, grad_value = attend_backward(
        queries, key_rows, value_rows, log_total, grad_attended
    )
    grad_packed = jnp.concatenate([grad_query, grad_key, grad_value], axis=1)
    grad_qbias = jnp.sum(grad_query.astype(F32), axis=0)
    grad_vbias = jnp.sum(grad_value.astype(F32), axis=0)
    grad_qkv = [dot(normed, part, TN, BF) for part in (grad_query, grad_key, grad_value)]
    grad_normed = dot(grad_packed, qkv, NT)
    grad_current, grad_gain_attn = norm_back(current, gain_attn, grad_normed)
    grad_current = grad_current + grad_middle
    small = jnp.concatenate(
        [
            jnp.stack([grad_qbias, grad_vbias, grad_pbias, grad_gain_attn, grad_gain_ffn]),
            grad_router,
        ]
    )
    small = jnp.pad(small, ((0, -small.shape[0] % 32), (0, 0)))
    shared = jnp.concatenate(grad_qkv + [grad_proj, small.astype(BF)])
    return grad_current, shared


def reduce_shared(shared, section):
    half = shared.shape[0] // 2
    own = lax.dynamic_slice_in_dim(shared, section * half, half, 0)
    other = lax.dynamic_slice_in_dim(shared, (1 - section) * half, half, 0)
    other = lax.ppermute(other, "section", SWAP)
    return lax.psum((own.astype(F32) + other.astype(F32)).astype(BF), "expert")


def both(own, other, is_first):
    return jnp.where(is_first, own, other), jnp.where(is_first, other, own)


def shards(
    block_input, cotangent, expert_ids, qkv_weight, query_bias, value_bias, proj_weight,
    proj_bias, attn_gain, ffn_gain, router_weight, in_weight, out_weight,
):
    section = lax.axis_index("section")
    is_first = section == 0
    width = block_input.shape[2]
    experts = router_weight.shape[2]
    tokens = block_input.shape[1]
    capacity = capacity_of(tokens, expert_ids.shape[3], experts)
    extra = capacity % 16

    def gathered(array):
        return lax.all_gather(array, "section", axis=0, tiled=True)

    vectors = gathered(
        jnp.stack([query_bias, value_bias, proj_bias, attn_gain, ffn_gain], axis=1)
    )
    qkv_all, proj_all, router_all = (
        gathered(part) for part in (qkv_weight, proj_weight, router_weight)
    )
    win_all, wout_all = gathered(in_weight), gathered(out_weight)
    layers = [
        (
            qkv_all[l], vectors[l, 0], vectors[l, 1], proj_all[l], vectors[l, 2], vectors[l, 3],
            vectors[l, 4], router_all[l], win_all[l, 0], wout_all[l, 0],
        )
        for l in range(2)
    ]
    rows = lax.dynamic_index_in_dim(block_input, section, 0, keepdims=False)
    seed = lax.dynamic_index_in_dim(cotangent, section, 0, keepdims=False)
    ids = lax.dynamic_index_in_dim(expert_ids, section, 1, keepdims=False)
    plans = [route_plan(ids[l], experts, capacity) for l in range(2)]

    kept0 = layer_attend(rows.astype(F32), plans[0], layers[0])
    done0 = moe(
        True, False, 0, extra, pack(plans[0], experts, kept0[8]), None, None, *layers[0][8:]
    )
    out0, combined0 = layer_combine(kept0, plans[0], done0[:2])
    out0 = out0.astype(BF)
    seed = seed.astype(F32)
    kept1 = layer_attend(out0.astype(F32), plans[1], layers[1])
    done1 = moe(
        True, True, 1, extra, pack(plans[1], experts, kept1[8]),
        layer_grads(seed, kept1, plans[1], experts), None, *layers[1][8:]
    )
    win1, wout1 = done1[4:]
    out1, combined1 = layer_combine(kept1, plans[1], done1[:2])
    out1 = out1.astype(BF)
    out_other = lax.ppermute(jnp.where(is_first, out1, out0), "section", SWAP)
    section_out = jnp.stack(both(jnp.where(is_first, out0, out1), out_other, is_first))

    grad1, shared1 = layer_backward(seed, kept1, combined1, done1[2:4], plans[1], layers[1])
    grad1 = grad1.astype(BF)
    up, down = [(0, 1)], [(1, 0)]
    win1_other = lax.ppermute(win1, "section", up)
    wout1_other = lax.ppermute(wout1, "section", up)
    grad1_other = lax.ppermute(grad1, "section", up)
    total1 = reduce_shared(shared1, section)
    total1_other = lax.ppermute(total1, "section", up)

    seed0 = grad1.astype(F32)
    back0 = moe(
        False, True, 2, extra, None, layer_grads(seed0, kept0, plans[0], experts), done0[2:4],
        *layers[0][8:]
    )
    win0, wout0 = back0[2:]
    grad0, shared0 = layer_backward(seed0, kept0, combined0, back0[:2], plans[0], layers[0])
    win0_other = lax.ppermute(win0, "section", down)
    wout0_other = lax.ppermute(wout0, "section", down)
    grad0_other = lax.ppermute(grad0, "section", down)
    shared0, total1 = lax.optimization_barrier((shared0, total1))
    total0 = reduce_shared(shared0, section)
    total0_other = lax.ppermute(total0, "section", down)

    section_grad = jnp.stack(
        [
            jnp.where(is_first, grad0, grad1_other.astype(F32)),
            jnp.where(is_first, grad0_other, grad1.astype(F32)),
        ]
    )

    def summed(first, first_other, second, second_other):
        return jnp.where(
            is_first,
            first.astype(F32) + first_other.astype(F32),
            second.astype(F32) + second_other.astype(F32),
        ).astype(BF)

    grad_win = summed(win0, win0_other, win1, win1_other)
    grad_wout = summed(wout0, wout0_other, wout1, wout1_other)
    total = jnp.concatenate(
        [
            jnp.where(is_first, total0, total1_other),
            jnp.where(is_first, total0_other, total1),
        ]
    ).astype(F32)
    grad_qkv = jnp.concatenate([total[i * width : (i + 1) * width] for i in range(3)], axis=1)
    grad_proj = total[3 * width : 4 * width]
    small = total[4 * width : 4 * width + 5 + experts]
    return (
        section_out[None],
        section_grad[None],
        grad_qkv[None],
        small[0][None],
        small[1][None],
        grad_proj[None],
        small[2][None],
        small[3][None],
        small[4][None],
        small[5:].T[None],
        grad_win[None, None],
        grad_wout[None, None],
    )


def solution(mesh):
    vector, matrix = P("section", None), P("section", None, None)
    expert = P("section", "expert", None, None)
    rows = P("section", None, "expert", None)
    return jax.shard_map(
        shards,
        mesh=mesh,
        in_specs=(
            P(None, "expert", None),
            P(None, "expert", None),
            P(None, None, "expert", None),
            matrix, vector, vector, matrix, vector, vector, vector, matrix, expert, expert,
        ),
        out_specs=(
            rows, rows, matrix, vector, vector, matrix, vector, vector, vector, matrix,
            expert, expert,
        ),
        check_vma=False,
    )
```

```python
import functools

import jax
import jax.numpy as jnp
from jax import lax
from jax.experimental import pallas as pl
from jax.experimental.pallas import tpu as pltpu
from jax.sharding import PartitionSpec as P

HD = 64
EPS = 1e-06
NEG = -1e30
BF = jnp.bfloat16
F32 = jnp.float32
HIGH = lax.Precision.HIGHEST
SWAP = [(0, 1), (1, 0)]
MESH = pl.DeviceIdType.MESH
NN = ((1,), (0,))
NT = ((1,), (1,))
TN = ((0,), (0,))
PLANES = 4
CHUNK = 512


def dot(a, b, dims, kind=F32, precision=None):
    return lax.dot_general(
        a, b, (dims, ((), ())), precision=precision, preferred_element_type=F32
    ).astype(kind)


def capacity_of(tokens, choices, experts):
    return tokens * choices // experts + max(1, tokens * choices // (16 * experts))


def inverse_rms(field):
    return lax.rsqrt(jnp.mean(field * field, axis=-1, keepdims=True) + EPS)


def norm_back(field, gain, grad):
    scale = inverse_rms(field)
    unit = field * scale
    grad_gain = jnp.sum(grad * unit, axis=0)
    scaled = grad * gain
    grad_field = scale * (scaled - unit * jnp.mean(scaled * unit, axis=-1, keepdims=True))
    return grad_field, grad_gain


def causal_scores(queries, key_rows):
    scores = jnp.einsum(
        "qhd,khd->hqk", queries, key_rows, preferred_element_type=F32
    ) * HD ** (-0.5)
    length = scores.shape[-1]
    causal = jnp.arange(length)[:, None] >= jnp.arange(length)[None, :]
    return jnp.where(causal[None], scores, NEG)


def attend_forward(queries, key_rows, value_rows):
    tokens, width = queries.shape
    shape = (tokens, width // HD, HD)
    scores = causal_scores(queries.reshape(shape), key_rows.reshape(shape))
    row_max = jnp.max(scores, axis=-1, keepdims=True)
    weights = jnp.exp(scores - row_max)
    row_total = jnp.sum(weights, axis=-1, keepdims=True)
    prob_low = (weights / row_total).astype(BF)
    attended = jnp.einsum(
        "hqk,khd->qhd", prob_low, value_rows.reshape(shape), preferred_element_type=F32
    )
    return (
        attended.astype(BF).reshape(tokens, width),
        row_max[..., 0] + jnp.log(row_total[..., 0]),
    )


def attend_backward(queries, key_rows, value_rows, log_total, grad_out):
    tokens, width = queries.shape
    shape = (tokens, width // HD, HD)
    queries, key_rows, value_rows, grad_out = (
        part.reshape(shape) for part in (queries, key_rows, value_rows, grad_out)
    )
    scores = causal_scores(queries, key_rows)
    weights = jnp.exp(scores - log_total[..., None])
    grad_probs = jnp.einsum("qhd,khd->hqk", grad_out, value_rows, preferred_element_type=F32)
    inner = jnp.sum(weights * grad_probs, axis=-1, keepdims=True)
    grad_scores = (weights * (grad_probs - inner)).astype(BF)
    grad_value = jnp.einsum(
        "hqk,qhd->khd", weights.astype(BF), grad_out, preferred_element_type=F32
    )
    grad_query = jnp.einsum(
        "hqk,khd->qhd", grad_scores, key_rows, preferred_element_type=F32
    ) * HD ** (-0.5)
    grad_key = jnp.einsum(
        "hqk,qhd->khd", grad_scores, queries, preferred_element_type=F32
    ) * HD ** (-0.5)
    return tuple(
        part.astype(BF).reshape(tokens, width) for part in (grad_query, grad_key, grad_value)
    )


def gelu_and_slope(hidden):
    root = 0.7978845608028654
    square = hidden * hidden
    bent = jnp.tanh(hidden * (root + (root * 0.044715) * square))
    half = 0.5 + 0.5 * bent
    slope = half + (0.5 * hidden) * (1.0 - bent * bent) * (root + (root * 0.134145) * square)
    return hidden * half, slope


def moe_kernel(experts, extra, layer, ahead, back, *refs):
    refs = list(refs)

    def take(count):
        taken, refs[:count] = refs[:count], []
        return taken

    rows_in, grads_in, kept_in = [], [], []
    if ahead:
        rows_in = take(2)
    if back:
        grads_in = take(2)
    if back and not ahead:
        kept_in = take(2)
    own_weights, other_weights = take(2), take(2)
    if kept_in:
        take(2)
    produced_out = take(2) if ahead else []
    kept_out = take(2) if ahead and not back else []
    returned_out = take(2) if back else []
    gwin_out, gwout_out = take(2) if back else (None, None)
    win, wout, weight_sem = take(3)
    if ahead:
        row_land, row_land_x, row_stage, row_stage_x, row_acc = take(5)
    if back:
        grad_land, grad_land_x, grad_stage, grad_stage_x, grad_acc, gwin, gwout = take(7)
        fold, fold_sem = take(2)
    send_sems, recv_sems, send_x_sems, recv_x_sems = take(4)

    per = experts // PLANES
    main = (rows_in or grads_in)[0].shape[1]
    ff = win.shape[1]
    chunks = ff // CHUNK
    me = lax.axis_index("expert")
    plane = me // per
    spot = me % per
    half, low = plane // 2, plane % 2
    order = [
        (1 - half) * 2 + low,
        (1 - half) * 2 + (1 - low),
        half * 2 + (1 - low),
        plane,
    ]

    barrier = pltpu.get_barrier_semaphore()

    def greet(step, carry):
        pl.semaphore_signal(
            barrier, inc=1, device_id={"expert": (me + step) % experts}, device_id_type=MESH
        )
        return carry

    if back:
        gwin_out, gwout_out = gwin_out.at[layer], gwout_out.at[layer]

    def load(weights):
        pltpu.make_async_copy(weights[0], win, weight_sem.at[0]).start()
        pltpu.make_async_copy(weights[1], wout, weight_sem.at[1]).start()

    section = lax.axis_index("section")
    pl.when(section == layer)(lambda: load(own_weights))
    pl.when(section != layer)(lambda: load(other_weights))
    lax.fori_loop(1, experts, greet, 0)
    pl.semaphore_wait(barrier, experts - 1)

    def send(source, target, lane, peer, to_plane):
        pltpu.make_async_remote_copy(
            src_ref=source.at[peer],
            dst_ref=target.at[me],
            send_sem=send_sems.at[lane],
            recv_sem=recv_sems.at[lane, plane],
            device_id={"expert": peer},
            device_id_type=MESH,
        ).start()

    def send_x(source, target, lane, peer):
        pltpu.make_async_remote_copy(
            src_ref=source.at[peer],
            dst_ref=target.at[me],
            send_sem=send_x_sems.at[lane],
            recv_sem=recv_x_sems.at[lane],
            device_id={"expert": peer},
            device_id_type=MESH,
        ).start()

    def own(source, target, sem):
        pltpu.make_async_copy(source.at[me], target.at[me], sem).start()

    def send_all_x(pairs):
        def one(step, carry):
            for source, target, lane in pairs:
                send_x(source, target, lane, (me + step) % experts)
            return carry

        lax.fori_loop(1, experts, one, 0)
        for source, target, lane in pairs:
            own(source, target, recv_x_sems.at[lane])

    def send_plane(pairs, to_plane, is_own):
        def one(step, carry):
            for source, target, lane in pairs:
                send(source, target, lane, to_plane * per + (spot + step) % per, to_plane)
            return carry

        lax.fori_loop(1 if is_own else 0, per, one, 0)
        if is_own:
            for source, target, lane in pairs:
                own(source, target, recv_sems.at[lane, plane])

    def wait_plane(target, lane, from_plane):
        part = target.at[pl.ds(from_plane * per, per)]
        pltpu.make_async_copy(part, part, recv_sems.at[lane, from_plane]).wait()

    def wait_x(target, lane):
        pltpu.make_async_copy(target, target, recv_x_sems.at[lane]).wait()

    def wait_sent(source, lane):
        part = source.at[pl.ds(0, experts - 1)]
        pltpu.make_async_copy(part, part, send_sems.at[lane]).wait()

    def wait_sent_x(source, lane):
        part = source.at[pl.ds(0, experts - 1)]
        pltpu.make_async_copy(part, part, send_x_sems.at[lane]).wait()

    first_pairs, first_x = [], []
    if ahead:
        first_pairs.append((rows_in[0], row_land, 0))
        first_x.append((rows_in[1], row_land_x, 0))
    if back:
        first_pairs.append((grads_in[0], grad_land, 1))
        first_x.append((grads_in[1], grad_land_x, 1))
    send_all_x(first_x)
    for at, to_plane in enumerate(order):
        send_plane(first_pairs, to_plane, at == 3)

    tall = experts * 16
    tile_rows = lax.broadcasted_iota(jnp.int32, (experts * extra, tall), 0)
    tile_cols = lax.broadcasted_iota(jnp.int32, (experts * extra, tall), 1)
    parts = win.shape[0] // 256
    picks = [
        (tile_cols == (tile_rows // extra) * 16 + q * extra + tile_rows % extra).astype(BF)
        for q in range(parts)
    ]

    def gather_x(landed):
        flat = landed[...].reshape(tall, 256)
        return jnp.concatenate([dot(pick, flat, NN, BF) for pick in picks], axis=1)

    def spread_x(values):
        total = dot(picks[0], values[:, :256], TN)
        for q in range(1, parts):
            total += dot(picks[q], values[:, q * 256 : (q + 1) * 256], TN)
        return total.astype(BF).reshape(experts, 16, 256)

    def run(rows, grads, is_first):
        count = (rows if rows is not None else grads).shape[0]

        def one(step, carry):
            cols = pl.ds(pl.multiple_of(step * CHUNK, CHUNK), CHUNK)
            wide = win[:, cols]
            deep = wout[cols, :]
            active, slope = gelu_and_slope(dot(rows, wide, NN))
            active = active.astype(BF)
            if ahead:
                row_acc[pl.ds(0, count)] += dot(active, deep, NN)
            if back:
                grad_hidden = (dot(grads, deep, NT) * slope).astype(BF)
                grad_acc[pl.ds(0, count)] += dot(grad_hidden, wide, NT)
                term_in = dot(rows, grad_hidden, TN)
                term_out = dot(active, grads, TN)
                if is_first:
                    gwin[:, cols] = term_in
                    gwout[cols, :] = term_out
                else:
                    gwin[:, cols] += term_in
                    gwout[cols, :] += term_out
            return carry

        if ahead:
            row_acc[pl.ds(0, count)] = jnp.zeros((count, row_acc.shape[1]), F32)
        if back:
            grad_acc[pl.ds(0, count)] = jnp.zeros((count, grad_acc.shape[1]), F32)
        lax.fori_loop(0, chunks, one, 0)

    last_pairs, last_x = [], []
    if ahead:
        last_pairs.append((row_stage, produced_out[0], 2))
        last_x.append((row_stage_x, produced_out[1], 2))
        wait_x(row_land_x, 0)
    if back:
        last_pairs.append((grad_stage, returned_out[0], 3))
        last_x.append((grad_stage_x, returned_out[1], 3))
        wait_x(grad_land_x, 1)
    pltpu.make_async_copy(win, win, weight_sem.at[0]).wait()
    pltpu.make_async_copy(wout, wout, weight_sem.at[1]).wait()

    few = experts * extra
    if ahead:
        rows_x = gather_x(row_land_x)
        if kept_out:
            kept_out[1][...] = rows_x
    else:
        rows_x = kept_in[1][...]
    grads_x = gather_x(grad_land_x) if back else None
    run(rows_x, grads_x, True)
    if ahead:
        row_stage_x[...] = spread_x(row_acc[pl.ds(0, few)].astype(BF))
    if back:
        grad_stage_x[...] = spread_x(grad_acc[pl.ds(0, few)].astype(BF))
    send_all_x(last_x)

    width = win.shape[0]
    block = per * main
    for at in (3, 0, 1, 2):
        from_plane = order[at]
        places = pl.ds(from_plane * per, per)
        rows = grads = None
        if ahead:
            wait_plane(row_land, 0, from_plane)
            rows = row_land[places].reshape(block, width)
            if kept_out:
                kept_out[0][places] = row_land[places]
        else:
            rows = kept_in[0][places].reshape(block, width)
        if back:
            wait_plane(grad_land, 1, from_plane)
            grads = grad_land[places].reshape(block, width)
        run(rows, grads, False)
        if ahead:
            row_stage[places] = row_acc[...].astype(BF).reshape(per, main, width)
        if back:
            grad_stage[places] = grad_acc[...].astype(BF).reshape(per, main, width)
        send_plane(last_pairs, from_plane, at == 3)

    if back:
        for at in range(chunks):
            slot = at % 2
            span = slice(at * CHUNK, (at + 1) * CHUNK)
            if at >= 2:
                pltpu.make_async_copy(
                    fold.at[slot], gwin_out.at[:, span], fold_sem.at[slot]
                ).wait()
            fold[slot] = gwin[:, span].astype(BF)
            pltpu.make_async_copy(fold.at[slot], gwin_out.at[:, span], fold_sem.at[slot]).start()
        for slot in range(2):
            pltpu.make_async_copy(
                fold.at[slot], gwin_out.at[:, slice(0, CHUNK)], fold_sem.at[slot]
            ).wait()
        rows_of = ff // 6
        for at in range(6):
            span = slice(at * rows_of, (at + 1) * rows_of)
            wout[span, :] = gwout[span, :].astype(BF)
            pltpu.make_async_copy(wout.at[span, :], gwout_out.at[span, :], weight_sem.at[1]).start()
        pltpu.make_async_copy(wout, gwout_out, weight_sem.at[1]).wait()

    for source, target, lane in first_pairs:
        wait_sent(source, lane)
    for source, target, lane in first_x + last_x:
        wait_sent_x(source, lane)
    for source, target, lane in last_pairs:
        wait_sent(source, lane)
        for from_plane in range(PLANES):
            wait_plane(target, lane, from_plane)
    for source, target, lane in last_x:
        wait_x(target, lane)


def moe(ahead, back, collective, extra, layer, rows, grads, kept, own, other, stacked=()):
    lead = rows if ahead else grads
    experts, main, width = lead[0].shape
    ff = own[0].shape[1]
    few = experts * extra
    per = experts // PLANES
    block = per * main
    tall = jax.ShapeDtypeStruct((experts, main, width), BF)
    small = jax.ShapeDtypeStruct((experts, 16, 256), BF)
    vmem = pl.BlockSpec(memory_space=pltpu.VMEM)
    hbm = pl.BlockSpec(memory_space=pl.ANY)
    operands, in_specs = [], []
    for pair in (rows if ahead else (), grads if back else (), kept if back and not ahead else ()):
        operands += list(pair)
        in_specs += [vmem] * len(pair)
    operands += [*own, *other, *stacked]
    in_specs += [hbm] * (4 + len(stacked))
    out_shape, out_specs = [], []
    if ahead:
        out_shape += [tall, small]
        out_specs += [vmem, vmem]
        if not back:
            out_shape += [tall, jax.ShapeDtypeStruct((few, width), BF)]
            out_specs += [vmem, vmem]
    if back:
        out_shape += [tall, small]
        out_specs += [vmem, vmem]
        out_shape += [
            jax.ShapeDtypeStruct((2, width, ff), BF),
            jax.ShapeDtypeStruct((2, ff, width), BF),
        ]
        out_specs += [hbm, hbm]
    aliases = {}
    if stacked:
        last = len(operands) - 2
        aliases = {last: len(out_shape) - 2, last + 1: len(out_shape) - 1}
    scratch = [
        pltpu.VMEM((width, ff), BF),
        pltpu.VMEM((ff, width), BF),
        pltpu.SemaphoreType.DMA((2,)),
    ]
    work = [
        pltpu.VMEM((experts, main, width), BF),
        pltpu.VMEM((experts, 16, 256), BF),
        pltpu.VMEM((experts, main, width), BF),
        pltpu.VMEM((experts, 16, 256), BF),
        pltpu.VMEM((max(block, few), width), F32),
    ]
    if ahead:
        scratch += work
    if back:
        scratch += work + [
            pltpu.VMEM((width, ff), F32),
            pltpu.VMEM((ff, width), F32),
            pltpu.VMEM((2, width, CHUNK), BF),
            pltpu.SemaphoreType.DMA((2,)),
        ]
    scratch += [
        pltpu.SemaphoreType.DMA((4,)),
        pltpu.SemaphoreType.DMA((4, PLANES)),
        pltpu.SemaphoreType.DMA((4,)),
        pltpu.SemaphoreType.DMA((4,)),
    ]
    return pl.pallas_call(
        functools.partial(moe_kernel, experts, extra, layer, ahead, back),
        out_shape=out_shape,
        in_specs=in_specs,
        out_specs=out_specs,
        scratch_shapes=scratch,
        input_output_aliases=aliases,
        cost_estimate=pl.CostEstimate(
            flops=(4 * ahead + 6 * back) * experts * main * width * ff,
            bytes_accessed=40 * 2**20 * (ahead + back),
            transcendentals=0,
        ),
        compiler_params=pltpu.CompilerParams(
            collective_id=collective, has_side_effects=True, vmem_limit_bytes=60 * 2**20
        ),
        name="moe_%d%d" % (ahead, back),
    )(*operands)


def pieces_of(experts, rows):
    return 4 if rows % (64 * experts) == 0 else 3


def merge_kernel(
    experts, main0, main1, small0, small1, wins, wouts, total, total_small, land_in, land_out,
    own, mate, land1, land2, acc, own_s, mate_s, land1_s, land2_s,
    load_sems, mate_send, mate_recv, mate_recv_s, wide_send, wide_recv,
    send_sems, send_s_sems, rs1, rs1_s, rs2, rs2_s, ag2, ag2_s, ag1, ag1_s,
):
    per = experts // PLANES
    me = lax.axis_index("expert")
    section = lax.axis_index("section")
    plane, spot = me // per, me % per
    rows, rows_s = own.shape[0], own_s.shape[0]
    pieces = pieces_of(experts, rows)
    size = rows // pieces
    step_rows = 48 if size % (48 * experts) == 0 else 16
    partner = {"section": 1 - section}

    barrier = pltpu.get_barrier_semaphore()

    def greet(target):
        pl.semaphore_signal(barrier, inc=1, device_id=target, device_id_type=MESH)

    greet(partner)

    def greet_plane(step, carry):
        greet({"expert": plane * per + (spot + step) % per})
        return carry

    def greet_column(step, carry):
        greet({"expert": ((plane + step) % PLANES) * per + spot})
        return carry

    lax.fori_loop(1, per, greet_plane, 0)
    lax.fori_loop(1, PLANES, greet_column, 0)
    pl.semaphore_wait(barrier, per + PLANES - 1)

    def remote(source, target, send, recv, where):
        pltpu.make_async_remote_copy(
            src_ref=source, dst_ref=target, send_sem=send, recv_sem=recv,
            device_id=where, device_id_type=MESH,
        ).start()

    def wait(part, sem):
        pltpu.make_async_copy(part, part, sem).wait()

    def at(start, size):
        return pl.ds(pl.multiple_of(start, 16), size)

    in_plane = lambda j: plane * per + j
    in_column = lambda j: j * per + spot
    by_plane = (per, spot, in_plane, PLANES, plane, in_column)
    by_column = (PLANES, plane, in_column, per, spot, in_plane)
    parts = [(p, p * size) + (by_column if p == 1 else by_plane) for p in range(pieces)]
    lows = [0]
    for part in parts:
        lows.append(lows[-1] + size // part[2])

    def begin(own_main, own_small, other_main, other_small):
        pltpu.make_async_copy(own_main, own, load_sems.at[0]).start()
        pltpu.make_async_copy(own_small, own_s, load_sems.at[1]).start()
        remote(other_small, mate_s, mate_send.at[1], mate_recv_s.at[0], partner)
        for p, base, n1, i1, _, _, _, _ in parts:
            block = size // n1

            def hand(step, carry):
                j = (i1 + step) % n1
                part = at(base + j * block, block)
                remote(other_main.at[part], mate.at[part], mate_send.at[0],
                       mate_recv.at[p, j], partner)
                return carry

            lax.fori_loop(1, n1 + 1, hand, 0)

    pl.when(section == 0)(lambda: begin(main0, small0, main1, small1))
    pl.when(section == 1)(lambda: begin(main1, small1, main0, small0))
    remote(wins.at[1 - section], land_in, wide_send.at[0], wide_recv.at[0], partner)
    remote(wouts.at[1 - section], land_out, wide_send.at[1], wide_recv.at[1], partner)
    wait(own, load_sems.at[0])
    wait(own_s, load_sems.at[1])
    wait(mate_s, mate_recv_s.at[0])
    own_s[...] += mate_s[...]

    def stage1(part):
        p, base, n1, i1, peer1, _, _, _ = part
        block, block_s = size // n1, rows_s // n1

        def out1(step, carry):
            j = (i1 + step) % n1
            wait(mate.at[at(base + j * block, block)], mate_recv.at[p, j])

            def fold(step, carry):
                part = at(base + j * block + step * step_rows, step_rows)
                own[part] = (own[part].astype(F32) + mate[part].astype(F32)).astype(BF)
                return carry

            lax.fori_loop(0, block // step_rows, fold, 0)
            where = {"expert": peer1(j)}
            remote(own.at[at(base + j * block, block)], land1.at[at(base + i1 * block, block)],
                   send_sems.at[p, 0], rs1.at[p, i1], where)
            if p == 0:
                remote(own_s.at[at(j * block_s, block_s)], land1_s.at[at(i1 * block_s, block_s)],
                       send_s_sems.at[0], rs1_s.at[i1], where)
            return carry

        lax.fori_loop(1, n1, out1, 0)

    def stage2(part):
        p, base, n1, i1, _, n2, i2, peer2 = part
        block, block_s = size // n1, rows_s // n1
        sub, sub_s = size // (n1 * n2), rows_s // (n1 * n2)
        low = lows[p]
        wait(mate.at[at(base + i1 * block, block)], mate_recv.at[p, i1])

        def in1(step, carry):
            j = (i1 + step) % n1
            wait(land1.at[at(base + j * block, block)], rs1.at[p, j])
            if p == 0:
                wait(land1_s.at[at(j * block_s, block_s)], rs1_s.at[j])
            return carry

        lax.fori_loop(1, n1, in1, 0)

        def sum1(k):
            def one(step, carry):
                place = k * sub + step * step_rows
                part = at(base + i1 * block + place, step_rows)
                value = own[part].astype(F32) + mate[part].astype(F32)

                def add(other, value):
                    far = at(base + ((i1 + other) % n1) * block + place, step_rows)
                    return value + land1[far].astype(F32)

                value = lax.fori_loop(1, n1, add, value)
                own[part] = value.astype(BF)
                acc[at(low + place, step_rows)] = value
                return carry

            lax.fori_loop(0, sub // step_rows, one, 0)
            if p == 0:
                part = at(i1 * block_s + k * sub_s, sub_s)

                def add_s(other, value):
                    far = at(((i1 + other) % n1) * block_s + k * sub_s, sub_s)
                    return value + land1_s[far]

                own_s[part] = lax.fori_loop(1, n1, add_s, own_s[part])

        def out2(step, carry):
            k = (i2 + step) % n2
            sum1(k)
            where = {"expert": peer2(k)}
            remote(own.at[at(base + i1 * block + k * sub, sub)],
                   land2.at[at(low + i2 * sub, sub)], send_sems.at[p, 1], rs2.at[p, i2], where)
            if p == 0:
                remote(own_s.at[at(i1 * block_s + k * sub_s, sub_s)],
                       land2_s.at[at(i2 * sub_s, sub_s)], send_s_sems.at[1], rs2_s.at[i2], where)
            return carry

        lax.fori_loop(1, n2, out2, 0)
        sum1(i2)

    def stage3(part):
        p, base, n1, i1, _, n2, i2, peer2 = part
        block, block_s = size // n1, rows_s // n1
        sub, sub_s = size // (n1 * n2), rows_s // (n1 * n2)
        low = lows[p]

        def in2(step, carry):
            k = (i2 + step) % n2
            wait(land2.at[at(low + k * sub, sub)], rs2.at[p, k])
            if p == 0:
                wait(land2_s.at[at(k * sub_s, sub_s)], rs2_s.at[k])
            return carry

        lax.fori_loop(1, n2, in2, 0)

        def sum2(step, carry):
            place = step * step_rows
            value = acc[at(low + i2 * sub + place, step_rows)]

            def add(other, value):
                far = at(low + ((i2 + other) % n2) * sub + place, step_rows)
                return value + land2[far].astype(F32)

            value = lax.fori_loop(1, n2, add, value)
            total[at(base + i1 * block + i2 * sub + place, step_rows)] = value.astype(BF)
            return carry

        lax.fori_loop(0, sub // step_rows, sum2, 0)
        home = at(base + i1 * block + i2 * sub, sub)
        home_s = at(i1 * block_s + i2 * sub_s, sub_s)
        if p == 0:

            def add2_s(other, value):
                return value + land2_s[at(((i2 + other) % n2) * sub_s, sub_s)]

            total_small[home_s] = lax.fori_loop(1, n2, add2_s, own_s[home_s])

        def share2(step, carry):
            where = {"expert": peer2((i2 + step) % n2)}
            remote(total.at[home], total.at[home], send_sems.at[p, 2], ag2.at[p, i2], where)
            if p == 0:
                remote(total_small.at[home_s], total_small.at[home_s], send_s_sems.at[2],
                       ag2_s.at[i2], where)
            return carry

        lax.fori_loop(1, n2, share2, 0)

    def stage4(part):
        p, base, n1, i1, peer1, n2, i2, _ = part
        block, block_s = size // n1, rows_s // n1
        sub, sub_s = size // (n1 * n2), rows_s // (n1 * n2)

        def share1(step, carry):
            k = (i2 + step) % n2
            home = at(base + i1 * block + k * sub, sub)
            home_s = at(i1 * block_s + k * sub_s, sub_s)

            @pl.when(step > 0)
            def _():
                wait(total.at[home], ag2.at[p, k])
                if p == 0:
                    wait(total_small.at[home_s], ag2_s.at[k])

            def one(jump, carry):
                where = {"expert": peer1((i1 + jump) % n1)}
                remote(total.at[home], total.at[home], send_sems.at[p, 3], ag1.at[p, i1], where)
                if p == 0:
                    remote(total_small.at[home_s], total_small.at[home_s], send_s_sems.at[3],
                           ag1_s.at[i1], where)
                return carry

            lax.fori_loop(1, n1, one, 0)
            return carry

        lax.fori_loop(0, n2, share1, 0)

    order = [(1, 0), (1, 1), (1, 2), (2, 0), (1, 3), (2, 1), (2, 2), (3, 0), (2, 3), (3, 1),
             (3, 2), (4, 0), (3, 3), (4, 1), (4, 2), (4, 3)]
    stages = (None, stage1, stage2, stage3, stage4)
    for stage, p in order:
        if p < pieces:
            stages[stage](parts[p])
    for p, base, n1, i1, _, n2, _, _ in parts:
        block, block_s = size // n1, rows_s // n1
        sub, sub_s = size // (n1 * n2), rows_s // (n1 * n2)

        def in_last(step, carry):
            j = (i1 + step) % n1
            wait(total.at[at(base + j * block, block)], ag1.at[p, j])
            if p == 0:
                wait(total_small.at[at(j * block_s, block_s)], ag1_s.at[j])
            return carry

        lax.fori_loop(1, n1, in_last, 0)
        for lane, count, count_s in (
            (0, (n1 - 1) * block, (n1 - 1) * block_s),
            (1, (n2 - 1) * sub, (n2 - 1) * sub_s),
            (2, (n2 - 1) * sub, (n2 - 1) * sub_s),
            (3, (n1 - 1) * block, (n1 - 1) * block_s),
        ):
            wait(own.at[pl.ds(0, count)], send_sems.at[p, lane])
            if p == 0:
                wait(own_s.at[pl.ds(0, count_s)], send_s_sems.at[lane])
    wait(mate, mate_send.at[0])
    wait(mate_s, mate_send.at[1])
    wait(land_in, wide_send.at[0])
    wait(land_out, wide_send.at[1])
    wait(land_in, wide_recv.at[0])
    wait(land_out, wide_recv.at[1])


def merge(experts, mains, smalls, wins, wouts):
    rows, width = mains[0].shape
    rows_s = smalls[0].shape[0]
    per = experts // PLANES
    most, least = max(per, PLANES), min(per, PLANES)
    pieces = pieces_of(experts, rows)
    seconds = (pieces - 1) * (rows // pieces // per) + rows // pieces // PLANES
    vmem = pl.BlockSpec(memory_space=pltpu.VMEM)
    hbm = pl.BlockSpec(memory_space=pl.ANY)
    sems = lambda *shape: pltpu.SemaphoreType.DMA(shape)
    return pl.pallas_call(
        functools.partial(merge_kernel, experts),
        out_shape=[
            jax.ShapeDtypeStruct((rows, width), BF),
            jax.ShapeDtypeStruct((rows_s, 128), F32),
            jax.ShapeDtypeStruct(wins.shape[1:], BF),
            jax.ShapeDtypeStruct(wouts.shape[1:], BF),
        ],
        in_specs=[hbm] * 6,
        out_specs=[vmem, vmem, hbm, hbm],
        scratch_shapes=[
            pltpu.VMEM((rows, width), BF),
            pltpu.VMEM((rows, width), BF),
            pltpu.VMEM((rows, width), BF),
            pltpu.VMEM((seconds, width), BF),
            pltpu.VMEM((seconds, width), F32),
            pltpu.VMEM((rows_s, 128), F32),
            pltpu.VMEM((rows_s, 128), F32),
            pltpu.VMEM((rows_s, 128), F32),
            pltpu.VMEM((rows_s // per, 128), F32),
            sems(2), sems(2), sems(pieces, most), sems(1), sems(2), sems(2),
            sems(pieces, 4), sems(4), sems(pieces, most), sems(most), sems(pieces, most), sems(most),
            sems(pieces, most), sems(most), sems(pieces, most), sems(most),
        ],
        compiler_params=pltpu.CompilerParams(
            collective_id=3, has_side_effects=True, vmem_limit_bytes=60 * 2**20
        ),
        name="merge",
    )(*mains, *smalls, wins, wouts)


def route_plan(route_ids, experts, capacity):
    tokens = route_ids.shape[0]
    main = capacity // 16 * 16
    extra = capacity - main
    lanes = jnp.arange(experts, dtype=jnp.int32)[None, :]
    first = (route_ids[:, 0:1] == lanes).astype(F32)
    second = (route_ids[:, 1:2] == lanes).astype(F32)
    places = jnp.arange(tokens, dtype=jnp.int32)
    earlier = (places[:, None] > places[None, :]).astype(BF)
    counts = dot(earlier, (first + second).astype(BF), NN)
    row = jnp.arange(experts * main, dtype=jnp.int32)[:, None]
    row_x = jnp.arange(experts * 16, dtype=jnp.int32)[:, None]
    place, place_x = [], []
    for j, hot in enumerate((first, second)):
        rank = jnp.sum(counts * hot, axis=-1).astype(jnp.int32)
        slot = jnp.where(rank < main, route_ids[:, j] * main + rank, -1)
        slot_x = jnp.where(rank < main, -experts * 16, route_ids[:, j] * 16 + rank - main)
        place.append((row == slot[None, :]).astype(BF))
        place_x.append(
            [(row_x == slot_x[None, :] + q * extra).astype(BF) for q in range(16 // extra)]
        )
    return first, second, place, place_x


def pack(plan, experts, values0, values1=None):
    _, _, place, place_x = plan
    width = values0.shape[1]
    if values1 is None:
        main = dot(place[0] + place[1], values0, NN)
    else:
        main = dot(place[0], values0, NN) + dot(place[1], values1, NN)
    small = 0.0
    for q in range(width // 256):
        part = slice(q * 256, (q + 1) * 256)
        if values1 is None:
            small += dot(place_x[0][q] + place_x[1][q], values0[:, part], NN)
        else:
            small += dot(place_x[0][q], values0[:, part], NN)
            small += dot(place_x[1][q], values1[:, part], NN)
    return main.astype(BF).reshape(experts, -1, width), small.astype(BF).reshape(experts, 16, 256)


def unpack(place, place_x, main, small, width):
    main = main.reshape(-1, width)
    small = small.reshape(-1, 256)
    tail = [dot(place_x[q], small, TN) for q in range(width // 256)]
    return dot(place, main, TN) + jnp.concatenate(tail, axis=1)


def layer_attend(current, plan, weights):
    qkv, qbias, vbias, proj, pbias, gain_attn, gain_ffn, router = weights
    first, second = plan[:2]
    width = current.shape[1]
    normed = (current * inverse_rms(current) * gain_attn).astype(BF)
    packed = dot(normed, qkv, NN)
    queries = (packed[:, :width] + qbias).astype(BF)
    key_rows = packed[:, width : 2 * width].astype(BF)
    value_rows = (packed[:, 2 * width :] + vbias).astype(BF)
    attended, log_total = attend_forward(queries, key_rows, value_rows)
    middle = current + (dot(attended, proj, NN) + pbias)
    routed = (middle * inverse_rms(middle) * gain_ffn).astype(BF)
    logits = dot(routed, router, NN)
    gap = jnp.sum(logits * (first - second), axis=-1, keepdims=True)
    gate0, gate1 = jax.nn.sigmoid(gap), jax.nn.sigmoid(-gap)
    return (
        current, normed, queries, key_rows, value_rows, log_total, attended, middle, routed,
        gate0, gate1,
    )


def layer_combine(kept, plan, produced):
    middle, gate0, gate1 = kept[7], kept[9], kept[10]
    _, _, place, place_x = plan
    width = middle.shape[1]
    combined = [
        unpack(place[j], place_x[j], produced[0], produced[1], width).astype(BF) for j in range(2)
    ]
    outputs = middle + (gate0 * combined[0].astype(F32) + gate1 * combined[1].astype(F32))
    return outputs, combined


def layer_grads(seed, kept, plan, experts):
    gate0, gate1 = kept[9], kept[10]
    return pack(plan, experts, (gate0 * seed).astype(BF), (gate1 * seed).astype(BF))


def layer_backward(seed, kept, combined, returned, plan, weights):
    qkv, qbias, vbias, proj, pbias, gain_attn, gain_ffn, router = weights
    first, second, place, place_x = plan
    (
        current, normed, queries, key_rows, value_rows, log_total, attended, middle, routed,
        gate0, gate1,
    ) = kept
    combined0, combined1 = combined
    width = middle.shape[1]
    experts = router.shape[1]
    grad_gap = gate0 * gate1 * jnp.sum(
        seed * (combined0.astype(F32) - combined1.astype(F32)), axis=-1, keepdims=True
    )
    grad_logits = grad_gap * (first - second)
    grad_router = dot(grad_logits, routed.astype(F32), TN, precision=HIGH)
    both_x = [one + two for one, two in zip(place_x[0], place_x[1])]
    grad_routed = unpack(place[0] + place[1], both_x, returned[0], returned[1], width) + dot(
        grad_logits, router.astype(F32), NT, precision=HIGH
    )
    grad_middle, grad_gain_ffn = norm_back(middle, gain_ffn, grad_routed)
    grad_middle = grad_middle + seed
    grad_branch = grad_middle.astype(BF)
    grad_pbias = jnp.sum(grad_branch.astype(F32), axis=0)
    grad_proj = dot(attended, grad_branch, TN, BF)
    grad_attended = dot(grad_branch, proj, NT, BF)
    grad_query, grad_key, grad_value = attend_backward(
        queries, key_rows, value_rows, log_total, grad_attended
    )
    grad_packed = jnp.concatenate([grad_query, grad_key, grad_value], axis=1)
    grad_qbias = jnp.sum(grad_query.astype(F32), axis=0)
    grad_vbias = jnp.sum(grad_value.astype(F32), axis=0)
    grad_qkv = [dot(normed, part, TN, BF) for part in (grad_query, grad_key, grad_value)]
    grad_normed = dot(grad_packed, qkv, NT)
    grad_current, grad_gain_attn = norm_back(current, gain_attn, grad_normed)
    grad_current = grad_current + grad_middle
    small = jnp.concatenate(
        [
            jnp.stack([grad_qbias, grad_vbias, grad_pbias, grad_gain_attn, grad_gain_ffn]),
            grad_router,
        ]
    ).reshape(-1, 128)
    small = jnp.pad(small, ((0, -small.shape[0] % (16 * experts)), (0, 0)))
    return grad_current, jnp.concatenate(grad_qkv + [grad_proj]), small


def both(own, other, is_first):
    return jnp.where(is_first, own, other), jnp.where(is_first, other, own)


def shards(
    block_input, cotangent, expert_ids, qkv_weight, query_bias, value_bias, proj_weight,
    proj_bias, attn_gain, ffn_gain, router_weight, in_weight, out_weight,
):
    section = lax.axis_index("section")
    is_first = section == 0
    width = block_input.shape[2]
    experts = router_weight.shape[2]
    tokens = block_input.shape[1]
    capacity = capacity_of(tokens, expert_ids.shape[3], experts)
    extra = capacity % 16

    def swapped(array):
        return lax.ppermute(array, "section", SWAP)

    vectors = jnp.concatenate([query_bias, value_bias, proj_bias, attn_gain, ffn_gain])
    shared = [qkv_weight[0], vectors, proj_weight[0], router_weight[0]]
    shared_other = [swapped(part) for part in shared]
    own_experts = (in_weight[0, 0], out_weight[0, 0])
    other_experts = tuple(swapped(part) for part in own_experts)
    layers = []
    for l in range(2):
        qkv, vector, proj, router = (
            jnp.where(section == l, own, other) for own, other in zip(shared, shared_other)
        )
        layers.append((qkv, vector[0], vector[1], proj, vector[2], vector[3], vector[4], router))
    rows = lax.dynamic_index_in_dim(block_input, section, 0, keepdims=False)
    seed = lax.dynamic_index_in_dim(cotangent, section, 0, keepdims=False)
    ids = lax.dynamic_index_in_dim(expert_ids, section, 1, keepdims=False)
    plans = [route_plan(ids[l], experts, capacity) for l in range(2)]

    kept0 = layer_attend(rows.astype(F32), plans[0], layers[0])
    done0 = moe(
        True, False, 0, extra, 0, pack(plans[0], experts, kept0[8]), None, None, own_experts,
        other_experts,
    )
    out0, combined0 = layer_combine(kept0, plans[0], done0[:2])
    out0 = out0.astype(BF)
    seed = seed.astype(F32)
    kept1 = layer_attend(out0.astype(F32), plans[1], layers[1])
    done1 = moe(
        True, True, 1, extra, 1, pack(plans[1], experts, kept1[8]),
        layer_grads(seed, kept1, plans[1], experts), None, own_experts, other_experts,
    )
    out1, combined1 = layer_combine(kept1, plans[1], done1[:2])
    out1 = out1.astype(BF)
    out_other = swapped(jnp.where(is_first, out1, out0))
    own_out = jnp.where(is_first, out0, out1)
    section_out = jnp.stack(both(own_out, out_other, is_first))

    grad1, main1, small1 = layer_backward(
        seed, kept1, combined1, done1[2:4], plans[1], layers[1]
    )
    grad1 = grad1.astype(BF)
    seed0 = grad1.astype(F32)
    back0 = moe(
        False, True, 2, extra, 0, None, layer_grads(seed0, kept0, plans[0], experts), done0[2:4],
        own_experts, other_experts, done1[4:],
    )
    grad0, main0, small0 = layer_backward(
        seed0, kept0, combined0, back0[:2], plans[0], layers[0]
    )
    grad1_other = lax.ppermute(grad1, "section", [(0, 1)])
    grad0_other = lax.ppermute(grad0, "section", [(1, 0)])
    section_grad = jnp.stack(
        [
            jnp.where(is_first, grad0, grad1_other.astype(F32)),
            jnp.where(is_first, grad0_other, grad1.astype(F32)),
        ]
    )
    total, small, land_in, land_out = merge(
        experts, (main0, main1), (small0, small1), back0[2], back0[3]
    )

    def summed(terms, landed):
        own = lax.dynamic_index_in_dim(terms, section, 0, keepdims=False)
        return (own.astype(F32) + landed.astype(F32)).astype(BF)

    grad_win = summed(back0[2], land_in)
    grad_wout = summed(back0[3], land_out)
    total = total.astype(F32)
    grad_qkv = jnp.concatenate([total[i * width : (i + 1) * width] for i in range(3)], axis=1)
    grad_proj = total[3 * width : 4 * width]
    small = small[: (5 + experts) * width // 128].reshape(5 + experts, width)
    return (
        section_out[None],
        section_grad[None],
        grad_qkv[None],
        small[0][None],
        small[1][None],
        grad_proj[None],
        small[2][None],
        small[3][None],
        small[4][None],
        small[5:].T[None],
        grad_win[None, None],
        grad_wout[None, None],
    )


def solution(mesh):
    vector, matrix = P("section", None), P("section", None, None)
    expert = P("section", "expert", None, None)
    rows = P("section", None, "expert", None)
    return jax.shard_map(
        shards,
        mesh=mesh,
        in_specs=(
            P(None, "expert", None),
            P(None, "expert", None),
            P(None, None, "expert", None),
            matrix, vector, vector, matrix, vector, vector, vector, matrix, expert, expert,
        ),
        out_specs=(
            rows, rows, matrix, vector, vector, matrix, vector, vector, vector, matrix,
            expert, expert,
        ),
        check_vma=False,
    )
```

```python
import functools

import jax
import jax.numpy as jnp
from jax import lax
from jax.experimental import pallas as pl
from jax.experimental.pallas import tpu as pltpu
from jax.sharding import PartitionSpec as P

HD = 64
EPS = 1e-06
NEG = -1e30
BF = jnp.bfloat16
F32 = jnp.float32
HIGH = lax.Precision.HIGHEST
SWAP = [(0, 1), (1, 0)]
MESH = pl.DeviceIdType.MESH
NN = ((1,), (0,))
NT = ((1,), (1,))
TN = ((0,), (0,))
PLANES = 4
CHUNK = 512


def dot(a, b, dims, kind=F32, precision=None):
    return lax.dot_general(
        a, b, (dims, ((), ())), precision=precision, preferred_element_type=F32
    ).astype(kind)


def capacity_of(tokens, choices, experts):
    return tokens * choices // experts + max(1, tokens * choices // (16 * experts))


def inverse_rms(field):
    return lax.rsqrt(jnp.mean(field * field, axis=-1, keepdims=True) + EPS)


def norm_back(field, gain, grad):
    scale = inverse_rms(field)
    unit = field * scale
    grad_gain = jnp.sum(grad * unit, axis=0)
    scaled = grad * gain
    grad_field = scale * (scaled - unit * jnp.mean(scaled * unit, axis=-1, keepdims=True))
    return grad_field, grad_gain


def causal_weights(scores, place, block):
    length = scores.shape[0]
    keys = lax.broadcasted_iota(jnp.int32, scores.shape, 0)
    queries = lax.broadcasted_iota(jnp.int32, scores.shape, 1) + place * block
    return jnp.where(keys <= queries, scores * HD ** (-0.5), NEG)


def attend_kernel(
    current_ref, qkv_ref, proj_ref, vectors_ref, normed_ref, queries_ref, keys_ref, values_ref,
    log_ref, attended_ref, middle_ref, routed_ref,
):
    tokens, width = normed_ref.shape
    block = tokens // 2
    qbias, vbias, pbias, gain_attn, gain_ffn = (vectors_ref[l : l + 1] for l in range(5))
    current = current_ref[...].astype(F32)
    normed = (current * inverse_rms(current) * gain_attn).astype(BF)
    normed_ref[...] = normed
    for at in range(0, width, 256):
        span = slice(at, at + 256)
        queries_ref[:, span] = (dot(normed, qkv_ref[:, span], NN) + qbias[:, span]).astype(BF)
        keys_ref[:, span] = dot(normed, qkv_ref[:, width + at : width + at + 256], NN, BF)
        values_ref[:, span] = (
            dot(normed, qkv_ref[:, 2 * width + at : 2 * width + at + 256], NN) + vbias[:, span]
        ).astype(BF)
    lane = lax.broadcasted_iota(jnp.int32, (1, 2 * HD), 1)

    def pair(step, carry):
        span = pl.ds(pl.multiple_of(step * 2 * HD, 2 * HD), 2 * HD)
        for place in range(2):
            rows = slice(place * block, (place + 1) * block)
            reach = slice(0, (place + 1) * block)
            total = jnp.zeros((block, 2 * HD), F32)
            for side in range(2):
                mine = (lane // HD) == side
                queries = jnp.where(mine, queries_ref[rows, span], 0.0).astype(BF)
                scores = causal_weights(dot(keys_ref[reach, span], queries, NT), place, block)
                top = jnp.max(scores, axis=0, keepdims=True)
                weights = jnp.exp(scores - top)
                amount = jnp.sum(weights, axis=0, keepdims=True)
                log_ref[step, side : side + 1, rows] = top + jnp.log(amount)
                probs = (weights * (1.0 / amount)).astype(BF)
                values = jnp.where(mine, values_ref[reach, span], 0.0).astype(BF)
                total += dot(probs, values, TN)
            attended_ref[rows, span] = total.astype(BF)
        return carry

    lax.fori_loop(0, width // (2 * HD), pair, 0)
    middle = current + (dot(attended_ref[...], proj_ref[...], NN) + pbias)
    middle_ref[...] = middle
    routed_ref[...] = (middle * inverse_rms(middle) * gain_ffn).astype(BF)


def attend(current, qkv, proj, vectors):
    tokens, width = current.shape
    low = jax.ShapeDtypeStruct((tokens, width), BF)
    vmem = pl.BlockSpec(memory_space=pltpu.VMEM)
    return pl.pallas_call(
        attend_kernel,
        out_shape=[
            low, low, low, low, jax.ShapeDtypeStruct((width // (2 * HD), 2, tokens), F32), low,
            jax.ShapeDtypeStruct((tokens, width), F32), low,
        ],
        in_specs=[vmem] * 4,
        out_specs=[vmem] * 8,
        compiler_params=pltpu.CompilerParams(vmem_limit_bytes=48 * 2**20),
        cost_estimate=pl.CostEstimate(
            flops=8 * tokens * width * width + 4 * tokens * tokens * width * 4,
            bytes_accessed=16 * 2**20, transcendentals=12 * tokens * tokens,
        ),
        name="attend",
    )(current, qkv, proj, vectors)


def attend_back_kernel(
    current_ref, normed_ref, queries_ref, keys_ref, values_ref, log_ref, attended_ref,
    grad_middle_ref, qkv_ref, proj_ref, vectors_ref, grad_current_ref, main_ref, sums_ref,
    grad_attended, grad_queries, grad_keys, grad_values, total_keys, total_values,
):
    tokens, width = normed_ref.shape
    block = tokens // 2
    grad_branch = grad_middle_ref[...].astype(BF)
    sums_ref[2:3] = jnp.sum(grad_branch.astype(F32), axis=0, keepdims=True)
    grad_attended[...] = dot(grad_branch, proj_ref[...], NT, BF)
    for at in range(0, width, 256):
        span = slice(at, at + 256)
        main_ref[3 * width : 4 * width, span] = dot(
            attended_ref[...], grad_middle_ref[:, span].astype(BF), TN, BF
        )
    lane = lax.broadcasted_iota(jnp.int32, (1, 2 * HD), 1)

    def pair(step, carry):
        span = pl.ds(pl.multiple_of(step * 2 * HD, 2 * HD), 2 * HD)
        for place in range(2):
            rows = slice(place * block, (place + 1) * block)
            reach = slice(0, (place + 1) * block)
            total = jnp.zeros((block, 2 * HD), F32)
            term_keys = term_values = 0.0
            for side in range(2):
                mine = (lane // HD) == side
                queries = jnp.where(mine, queries_ref[rows, span], 0.0).astype(BF)
                grads = jnp.where(mine, grad_attended[rows, span], 0.0).astype(BF)
                scores = causal_weights(dot(keys_ref[reach, span], queries, NT), place, block)
                weights = jnp.exp(scores - log_ref[step, side : side + 1, rows])
                grad_probs = dot(values_ref[reach, span], grads, NT)
                inner = jnp.sum(weights * grad_probs, axis=0, keepdims=True)
                grad_scores = (weights * (grad_probs - inner)).astype(BF)
                keys = jnp.where(mine, keys_ref[reach, span], 0.0).astype(BF)
                total += dot(grad_scores, keys, TN)
                term_values += dot(weights.astype(BF), grads, NN)
                term_keys += dot(grad_scores, queries, NN)
            grad_queries[rows, span] = (total * HD ** (-0.5)).astype(BF)
            if place == 0:
                total_keys[...] = term_keys
                total_values[...] = term_values
            else:
                term_keys = jnp.concatenate(
                    [term_keys[:block] + total_keys[...], term_keys[block:]]
                )
                term_values = jnp.concatenate(
                    [term_values[:block] + total_values[...], term_values[block:]]
                )
                grad_keys[:, span] = (term_keys * HD ** (-0.5)).astype(BF)
                grad_values[:, span] = term_values.astype(BF)
        return carry

    lax.fori_loop(0, width // (2 * HD), pair, 0)
    sums_ref[0:1] = jnp.sum(grad_queries[...].astype(F32), axis=0, keepdims=True)
    sums_ref[1:2] = jnp.sum(grad_values[...].astype(F32), axis=0, keepdims=True)
    grad_normed = jnp.zeros((tokens, width), F32)
    for which, grads in enumerate((grad_queries, grad_keys, grad_values)):
        for at in range(0, width, 256):
            main_ref[which * width : (which + 1) * width, at : at + 256] = dot(
                normed_ref[...], grads[:, at : at + 256], TN, BF
            )
        grad_normed += dot(grads[...], qkv_ref[:, which * width : (which + 1) * width], NT)
    current = current_ref[...].astype(F32)
    scale = inverse_rms(current)
    unit = current * scale
    sums_ref[3:4] = jnp.sum(grad_normed * unit, axis=0, keepdims=True)
    scaled = grad_normed * vectors_ref[3:4]
    grad_current_ref[...] = grad_middle_ref[...] + scale * (
        scaled - unit * jnp.mean(scaled * unit, axis=-1, keepdims=True)
    )


def attend_back(current, kept, grad_middle, qkv, proj, vectors):
    normed, queries, keys, values, log_total, attended = kept
    tokens, width = normed.shape
    vmem = pl.BlockSpec(memory_space=pltpu.VMEM)
    return pl.pallas_call(
        attend_back_kernel,
        out_shape=[
            jax.ShapeDtypeStruct((tokens, width), F32),
            jax.ShapeDtypeStruct((4 * width, width), BF),
            jax.ShapeDtypeStruct((4, width), F32),
        ],
        in_specs=[vmem] * 11,
        out_specs=[vmem] * 3,
        scratch_shapes=[pltpu.VMEM((tokens, width), BF)] * 4
        + [pltpu.VMEM((tokens // 2, 2 * HD), F32)] * 2,
        compiler_params=pltpu.CompilerParams(vmem_limit_bytes=48 * 2**20),
        cost_estimate=pl.CostEstimate(
            flops=16 * tokens * width * width + 10 * tokens * tokens * width * 4,
            bytes_accessed=24 * 2**20, transcendentals=12 * tokens * tokens,
        ),
        name="attend_back",
    )(
        current, normed, queries, keys, values, log_total, attended, grad_middle, qkv, proj,
        vectors,
    )


def gelu_and_slope(hidden):
    root = 0.7978845608028654
    square = hidden * hidden
    bent = jnp.tanh(hidden * (root + (root * 0.044715) * square))
    half = 0.5 + 0.5 * bent
    slope = half + (0.5 * hidden) * (1.0 - bent * bent) * (root + (root * 0.134145) * square)
    return hidden * half, slope


def moe_kernel(experts, extra, layer, ahead, back, *refs):
    refs = list(refs)

    def take(count):
        taken, refs[:count] = refs[:count], []
        return taken

    rows_in, grads_in, kept_in = [], [], []
    if ahead:
        rows_in = take(2)
    if back:
        grads_in = take(2)
    if back and not ahead:
        kept_in = take(2)
    own_weights, other_weights = take(2), take(2)
    if kept_in:
        take(2)
    produced_out = take(2) if ahead else []
    kept_out = take(2) if ahead and not back else []
    returned_out = take(2) if back else []
    gwin_out, gwout_out = take(2) if back else (None, None)
    win, wout, weight_sem = take(3)
    if ahead:
        row_land, row_land_x, row_stage, row_stage_x, row_acc = take(5)
    if back:
        grad_land, grad_land_x, grad_stage, grad_stage_x, grad_acc, gwin, gwout = take(7)
        fold, fold_sem = take(2)
    send_sems, recv_sems, send_x_sems, recv_x_sems = take(4)
    takes_turns = ahead and not back
    turn = take(1)[0] if takes_turns else None

    per = experts // PLANES
    main = (rows_in or grads_in)[0].shape[1]
    ff = win.shape[1]
    chunks = ff // CHUNK
    me = lax.axis_index("expert")
    plane = me // per
    spot = me % per
    half, low = plane // 2, plane % 2
    order = [
        (1 - half) * 2 + low,
        (1 - half) * 2 + (1 - low),
        half * 2 + (1 - low),
        plane,
    ]

    barrier = pltpu.get_barrier_semaphore()

    def greet(step, carry):
        pl.semaphore_signal(
            barrier, inc=1, device_id={"expert": (me + step) % experts}, device_id_type=MESH
        )
        return carry

    if back:
        gwin_out, gwout_out = gwin_out.at[layer], gwout_out.at[layer]

    def load(weights):
        pltpu.make_async_copy(weights[0], win, weight_sem.at[0]).start()
        pltpu.make_async_copy(weights[1], wout, weight_sem.at[1]).start()

    section = lax.axis_index("section")
    pl.when(section == layer)(lambda: load(own_weights))
    pl.when(section != layer)(lambda: load(other_weights))
    lax.fori_loop(1, experts, greet, 0)
    if takes_turns:
        pl.semaphore_signal(
            barrier, inc=1, device_id={"section": 1 - section}, device_id_type=MESH
        )
        pl.semaphore_wait(barrier, experts)
        pl.when(section == 1)(lambda: pl.semaphore_wait(turn, 1))
    else:
        pl.semaphore_wait(barrier, experts - 1)

    def send(source, target, lane, peer, to_plane):
        pltpu.make_async_remote_copy(
            src_ref=source.at[peer],
            dst_ref=target.at[me],
            send_sem=send_sems.at[lane],
            recv_sem=recv_sems.at[lane, plane],
            device_id={"expert": peer},
            device_id_type=MESH,
        ).start()

    def send_x(source, target, lane, peer):
        pltpu.make_async_remote_copy(
            src_ref=source.at[peer],
            dst_ref=target.at[me],
            send_sem=send_x_sems.at[lane],
            recv_sem=recv_x_sems.at[lane],
            device_id={"expert": peer},
            device_id_type=MESH,
        ).start()

    def own(source, target, sem):
        pltpu.make_async_copy(source.at[me], target.at[me], sem).start()

    def send_all_x(pairs):
        def one(step, carry):
            for source, target, lane in pairs:
                send_x(source, target, lane, (me + step) % experts)
            return carry

        lax.fori_loop(1, experts, one, 0)
        for source, target, lane in pairs:
            own(source, target, recv_x_sems.at[lane])

    def send_plane(pairs, to_plane, is_own):
        def one(step, carry):
            for source, target, lane in pairs:
                send(source, target, lane, to_plane * per + (spot + step) % per, to_plane)
            return carry

        lax.fori_loop(1 if is_own else 0, per, one, 0)
        if is_own:
            for source, target, lane in pairs:
                own(source, target, recv_sems.at[lane, plane])

    def wait_plane(target, lane, from_plane):
        part = target.at[pl.ds(from_plane * per, per)]
        pltpu.make_async_copy(part, part, recv_sems.at[lane, from_plane]).wait()

    def wait_x(target, lane):
        pltpu.make_async_copy(target, target, recv_x_sems.at[lane]).wait()

    def wait_sent(source, lane):
        part = source.at[pl.ds(0, experts - 1)]
        pltpu.make_async_copy(part, part, send_sems.at[lane]).wait()

    def wait_sent_x(source, lane):
        part = source.at[pl.ds(0, experts - 1)]
        pltpu.make_async_copy(part, part, send_x_sems.at[lane]).wait()

    first_pairs, first_x = [], []
    if ahead:
        first_pairs.append((rows_in[0], row_land, 0))
        first_x.append((rows_in[1], row_land_x, 0))
    if back:
        first_pairs.append((grads_in[0], grad_land, 1))
        first_x.append((grads_in[1], grad_land_x, 1))
    send_all_x(first_x)
    for at, to_plane in enumerate(order):
        send_plane(first_pairs, to_plane, at == 3)

    tall = experts * 16
    tile_rows = lax.broadcasted_iota(jnp.int32, (experts * extra, tall), 0)
    tile_cols = lax.broadcasted_iota(jnp.int32, (experts * extra, tall), 1)
    parts = win.shape[0] // 256
    picks = [
        (tile_cols == (tile_rows // extra) * 16 + q * extra + tile_rows % extra).astype(BF)
        for q in range(parts)
    ]

    def gather_x(landed):
        flat = landed[...].reshape(tall, 256)
        return jnp.concatenate([dot(pick, flat, NN, BF) for pick in picks], axis=1)

    def spread_x(values):
        total = dot(picks[0], values[:, :256], TN)
        for q in range(1, parts):
            total += dot(picks[q], values[:, q * 256 : (q + 1) * 256], TN)
        return total.astype(BF).reshape(experts, 16, 256)

    def run(rows, grads, is_first):
        count = (rows if rows is not None else grads).shape[0]

        def one(step, carry):
            cols = pl.ds(pl.multiple_of(step * CHUNK, CHUNK), CHUNK)
            wide = win[:, cols]
            deep = wout[cols, :]
            active, slope = gelu_and_slope(dot(rows, wide, NN))
            active = active.astype(BF)
            if ahead:
                row_acc[pl.ds(0, count)] += dot(active, deep, NN)
            if back:
                grad_hidden = (dot(grads, deep, NT) * slope).astype(BF)
                grad_acc[pl.ds(0, count)] += dot(grad_hidden, wide, NT)
                term_in = dot(rows, grad_hidden, TN)
                term_out = dot(active, grads, TN)
                if is_first:
                    gwin[:, cols] = term_in
                    gwout[cols, :] = term_out
                else:
                    gwin[:, cols] += term_in
                    gwout[cols, :] += term_out
            return carry

        if ahead:
            row_acc[pl.ds(0, count)] = jnp.zeros((count, row_acc.shape[1]), F32)
        if back:
            grad_acc[pl.ds(0, count)] = jnp.zeros((count, grad_acc.shape[1]), F32)
        lax.fori_loop(0, chunks, one, 0)

    last_pairs, last_x = [], []
    if ahead:
        last_pairs.append((row_stage, produced_out[0], 2))
        last_x.append((row_stage_x, produced_out[1], 2))
        wait_x(row_land_x, 0)
    if back:
        last_pairs.append((grad_stage, returned_out[0], 3))
        last_x.append((grad_stage_x, returned_out[1], 3))
        wait_x(grad_land_x, 1)
    pltpu.make_async_copy(win, win, weight_sem.at[0]).wait()
    pltpu.make_async_copy(wout, wout, weight_sem.at[1]).wait()

    few = experts * extra
    if ahead:
        rows_x = gather_x(row_land_x)
        if kept_out:
            kept_out[1][...] = rows_x
    else:
        rows_x = kept_in[1][...]
    grads_x = gather_x(grad_land_x) if back else None
    run(rows_x, grads_x, True)
    if ahead:
        row_stage_x[...] = spread_x(row_acc[pl.ds(0, few)].astype(BF))
    if back:
        grad_stage_x[...] = spread_x(grad_acc[pl.ds(0, few)].astype(BF))
    send_all_x(last_x)

    width = win.shape[0]
    block = per * main
    for at in (3, 0, 1, 2):
        from_plane = order[at]
        places = pl.ds(from_plane * per, per)
        rows = grads = None
        if ahead:
            wait_plane(row_land, 0, from_plane)
            rows = row_land[places].reshape(block, width)
            if kept_out:
                kept_out[0][places] = row_land[places]
        else:
            rows = kept_in[0][places].reshape(block, width)
        if back:
            wait_plane(grad_land, 1, from_plane)
            grads = grad_land[places].reshape(block, width)
        run(rows, grads, False)
        if ahead:
            row_stage[places] = row_acc[...].astype(BF).reshape(per, main, width)
        if back:
            grad_stage[places] = grad_acc[...].astype(BF).reshape(per, main, width)
        send_plane(last_pairs, from_plane, at == 3)

    if takes_turns:
        pl.when(section == 0)(
            lambda: pl.semaphore_signal(
                turn, inc=1, device_id={"section": 1 - section}, device_id_type=MESH
            )
        )
    if back:
        for at in range(chunks):
            slot = at % 2
            span = slice(at * CHUNK, (at + 1) * CHUNK)
            if at >= 2:
                pltpu.make_async_copy(
                    fold.at[slot], gwin_out.at[:, span], fold_sem.at[slot]
                ).wait()
            fold[slot] = gwin[:, span].astype(BF)
            pltpu.make_async_copy(fold.at[slot], gwin_out.at[:, span], fold_sem.at[slot]).start()
        for slot in range(2):
            pltpu.make_async_copy(
                fold.at[slot], gwin_out.at[:, slice(0, CHUNK)], fold_sem.at[slot]
            ).wait()
        rows_of = ff // 6
        for at in range(6):
            span = slice(at * rows_of, (at + 1) * rows_of)
            wout[span, :] = gwout[span, :].astype(BF)
            pltpu.make_async_copy(wout.at[span, :], gwout_out.at[span, :], weight_sem.at[1]).start()
        pltpu.make_async_copy(wout, gwout_out, weight_sem.at[1]).wait()

    for source, target, lane in first_pairs:
        wait_sent(source, lane)
    for source, target, lane in first_x + last_x:
        wait_sent_x(source, lane)
    for source, target, lane in last_pairs:
        wait_sent(source, lane)
        for from_plane in range(PLANES):
            wait_plane(target, lane, from_plane)
    for source, target, lane in last_x:
        wait_x(target, lane)


def moe(ahead, back, collective, extra, layer, rows, grads, kept, own, other, stacked=()):
    lead = rows if ahead else grads
    experts, main, width = lead[0].shape
    ff = own[0].shape[1]
    few = experts * extra
    per = experts // PLANES
    block = per * main
    tall = jax.ShapeDtypeStruct((experts, main, width), BF)
    small = jax.ShapeDtypeStruct((experts, 16, 256), BF)
    vmem = pl.BlockSpec(memory_space=pltpu.VMEM)
    hbm = pl.BlockSpec(memory_space=pl.ANY)
    operands, in_specs = [], []
    for pair in (rows if ahead else (), grads if back else (), kept if back and not ahead else ()):
        operands += list(pair)
        in_specs += [vmem] * len(pair)
    operands += [*own, *other, *stacked]
    in_specs += [hbm] * (4 + len(stacked))
    out_shape, out_specs = [], []
    if ahead:
        out_shape += [tall, small]
        out_specs += [vmem, vmem]
        if not back:
            out_shape += [tall, jax.ShapeDtypeStruct((few, width), BF)]
            out_specs += [vmem, vmem]
    if back:
        out_shape += [tall, small]
        out_specs += [vmem, vmem]
        out_shape += [
            jax.ShapeDtypeStruct((2, width, ff), BF),
            jax.ShapeDtypeStruct((2, ff, width), BF),
        ]
        out_specs += [hbm, hbm]
    aliases = {}
    if stacked:
        last = len(operands) - 2
        aliases = {last: len(out_shape) - 2, last + 1: len(out_shape) - 1}
    scratch = [
        pltpu.VMEM((width, ff), BF),
        pltpu.VMEM((ff, width), BF),
        pltpu.SemaphoreType.DMA((2,)),
    ]
    work = [
        pltpu.VMEM((experts, main, width), BF),
        pltpu.VMEM((experts, 16, 256), BF),
        pltpu.VMEM((experts, main, width), BF),
        pltpu.VMEM((experts, 16, 256), BF),
        pltpu.VMEM((max(block, few), width), F32),
    ]
    if ahead:
        scratch += work
    if back:
        scratch += work + [
            pltpu.VMEM((width, ff), F32),
            pltpu.VMEM((ff, width), F32),
            pltpu.VMEM((2, width, CHUNK), BF),
            pltpu.SemaphoreType.DMA((2,)),
        ]
    scratch += [
        pltpu.SemaphoreType.DMA((4,)),
        pltpu.SemaphoreType.DMA((4, PLANES)),
        pltpu.SemaphoreType.DMA((4,)),
        pltpu.SemaphoreType.DMA((4,)),
    ]
    if ahead and not back:
        scratch.append(pltpu.SemaphoreType.REGULAR)
    return pl.pallas_call(
        functools.partial(moe_kernel, experts, extra, layer, ahead, back),
        out_shape=out_shape,
        in_specs=in_specs,
        out_specs=out_specs,
        scratch_shapes=scratch,
        input_output_aliases=aliases,
        cost_estimate=pl.CostEstimate(
            flops=(4 * ahead + 6 * back) * experts * main * width * ff,
            bytes_accessed=40 * 2**20 * (ahead + back),
            transcendentals=0,
        ),
        compiler_params=pltpu.CompilerParams(
            collective_id=collective, has_side_effects=True, vmem_limit_bytes=60 * 2**20
        ),
        name="moe_%d%d" % (ahead, back),
    )(*operands)


def pieces_of(experts, rows):
    return 4 if rows % (64 * experts) == 0 else 3


def merge_kernel(
    experts, main0, main1, small0, small1, out0, out1, grad0, grad1, wins, wouts,
    total, total_small, land_in, land_out, section_out, section_grad,
    own, mate, land1, land2, acc, own_s, mate_s, land1_s, land2_s,
    load_sems, mate_send, mate_recv, mate_recv_s, wide_send, wide_recv, hand_load,
    send_sems, send_s_sems, rs1, rs1_s, rs2, rs2_s, ag2, ag2_s, ag1, ag1_s,
):
    per = experts // PLANES
    me = lax.axis_index("expert")
    section = lax.axis_index("section")
    plane, spot = me // per, me % per
    rows, rows_s = own.shape[0], own_s.shape[0]
    pieces = pieces_of(experts, rows)
    size = rows // pieces
    step_rows = 48 if size % (48 * experts) == 0 else 16
    partner = {"section": 1 - section}

    barrier = pltpu.get_barrier_semaphore()

    def greet(target):
        pl.semaphore_signal(barrier, inc=1, device_id=target, device_id_type=MESH)

    greet(partner)

    def greet_plane(step, carry):
        greet({"expert": plane * per + (spot + step) % per})
        return carry

    def greet_column(step, carry):
        greet({"expert": ((plane + step) % PLANES) * per + spot})
        return carry

    lax.fori_loop(1, per, greet_plane, 0)
    lax.fori_loop(1, PLANES, greet_column, 0)
    pl.semaphore_wait(barrier, per + PLANES - 1)

    def remote(source, target, send, recv, where):
        pltpu.make_async_remote_copy(
            src_ref=source, dst_ref=target, send_sem=send, recv_sem=recv,
            device_id=where, device_id_type=MESH,
        ).start()

    def wait(part, sem):
        pltpu.make_async_copy(part, part, sem).wait()

    def at(start, size):
        return pl.ds(pl.multiple_of(start, 16), size)

    in_plane = lambda j: plane * per + j
    in_column = lambda j: j * per + spot
    by_plane = (per, spot, in_plane, PLANES, plane, in_column)
    by_column = (PLANES, plane, in_column, per, spot, in_plane)
    parts = [(p, p * size) + (by_column if p == 1 else by_plane) for p in range(pieces)]
    lows = [0]
    for part in parts:
        lows.append(lows[-1] + size // part[2])

    def begin(own_main, own_small, own_hand, other_main, other_small, other_hand):
        pltpu.make_async_copy(own_main, own, load_sems.at[0]).start()
        pltpu.make_async_copy(own_small, own_s, load_sems.at[1]).start()
        remote(other_small, mate_s, mate_send.at[1], mate_recv_s.at[0], partner)
        for p, base, n1, i1, _, _, _, _ in parts:
            block = size // n1

            def hand(step, carry):
                j = (i1 + step) % n1
                part = at(base + j * block, block)
                remote(other_main.at[part], mate.at[part], mate_send.at[0],
                       mate_recv.at[p, j], partner)
                return carry

            lax.fori_loop(1, n1 + 1, hand, 0)
        for lane, target in enumerate((section_out, section_grad)):
            mine = target.at[section]
            pltpu.make_async_copy(own_hand[lane], mine, hand_load.at[lane]).start()
            remote(
                other_hand[lane], mine, wide_send.at[2 + lane], wide_recv.at[2 + lane], partner
            )

    first = (main0, small0, (out0, grad0))
    second = (main1, small1, (out1, grad1))
    pl.when(section == 0)(lambda: begin(*first, *second))
    pl.when(section == 1)(lambda: begin(*second, *first))
    remote(wins.at[1 - section], land_in, wide_send.at[0], wide_recv.at[0], partner)
    remote(wouts.at[1 - section], land_out, wide_send.at[1], wide_recv.at[1], partner)
    wait(own, load_sems.at[0])
    wait(own_s, load_sems.at[1])
    wait(mate_s, mate_recv_s.at[0])
    own_s[...] += mate_s[...]

    def stage1(part):
        p, base, n1, i1, peer1, _, _, _ = part
        block, block_s = size // n1, rows_s // n1

        def out1(step, carry):
            j = (i1 + step) % n1
            wait(mate.at[at(base + j * block, block)], mate_recv.at[p, j])

            def fold(step, carry):
                part = at(base + j * block + step * step_rows, step_rows)
                own[part] = (own[part].astype(F32) + mate[part].astype(F32)).astype(BF)
                return carry

            lax.fori_loop(0, block // step_rows, fold, 0)
            where = {"expert": peer1(j)}
            remote(own.at[at(base + j * block, block)], land1.at[at(base + i1 * block, block)],
                   send_sems.at[p, 0], rs1.at[p, i1], where)
            if p == 0:
                remote(own_s.at[at(j * block_s, block_s)], land1_s.at[at(i1 * block_s, block_s)],
                       send_s_sems.at[0], rs1_s.at[i1], where)
            return carry

        lax.fori_loop(1, n1, out1, 0)

    def stage2(part):
        p, base, n1, i1, _, n2, i2, peer2 = part
        block, block_s = size // n1, rows_s // n1
        sub, sub_s = size // (n1 * n2), rows_s // (n1 * n2)
        low = lows[p]
        wait(mate.at[at(base + i1 * block, block)], mate_recv.at[p, i1])

        def in1(step, carry):
            j = (i1 + step) % n1
            wait(land1.at[at(base + j * block, block)], rs1.at[p, j])
            if p == 0:
                wait(land1_s.at[at(j * block_s, block_s)], rs1_s.at[j])
            return carry

        lax.fori_loop(1, n1, in1, 0)

        def sum1(k):
            def one(step, carry):
                place = k * sub + step * step_rows
                part = at(base + i1 * block + place, step_rows)
                value = own[part].astype(F32) + mate[part].astype(F32)

                def add(other, value):
                    far = at(base + ((i1 + other) % n1) * block + place, step_rows)
                    return value + land1[far].astype(F32)

                value = lax.fori_loop(1, n1, add, value)
                own[part] = value.astype(BF)
                acc[at(low + place, step_rows)] = value
                return carry

            lax.fori_loop(0, sub // step_rows, one, 0)
            if p == 0:
                part = at(i1 * block_s + k * sub_s, sub_s)

                def add_s(other, value):
                    far = at(((i1 + other) % n1) * block_s + k * sub_s, sub_s)
                    return value + land1_s[far]

                own_s[part] = lax.fori_loop(1, n1, add_s, own_s[part])

        def out2(step, carry):
            k = (i2 + step) % n2
            sum1(k)
            where = {"expert": peer2(k)}
            remote(own.at[at(base + i1 * block + k * sub, sub)],
                   land2.at[at(low + i2 * sub, sub)], send_sems.at[p, 1], rs2.at[p, i2], where)
            if p == 0:
                remote(own_s.at[at(i1 * block_s + k * sub_s, sub_s)],
                       land2_s.at[at(i2 * sub_s, sub_s)], send_s_sems.at[1], rs2_s.at[i2], where)
            return carry

        lax.fori_loop(1, n2, out2, 0)
        sum1(i2)

    def stage3(part):
        p, base, n1, i1, _, n2, i2, peer2 = part
        block, block_s = size // n1, rows_s // n1
        sub, sub_s = size // (n1 * n2), rows_s // (n1 * n2)
        low = lows[p]

        def in2(step, carry):
            k = (i2 + step) % n2
            wait(land2.at[at(low + k * sub, sub)], rs2.at[p, k])
            if p == 0:
                wait(land2_s.at[at(k * sub_s, sub_s)], rs2_s.at[k])
            return carry

        lax.fori_loop(1, n2, in2, 0)

        def sum2(step, carry):
            place = step * step_rows
            value = acc[at(low + i2 * sub + place, step_rows)]

            def add(other, value):
                far = at(low + ((i2 + other) % n2) * sub + place, step_rows)
                return value + land2[far].astype(F32)

            value = lax.fori_loop(1, n2, add, value)
            total[at(base + i1 * block + i2 * sub + place, step_rows)] = value.astype(BF)
            return carry

        lax.fori_loop(0, sub // step_rows, sum2, 0)
        home = at(base + i1 * block + i2 * sub, sub)
        home_s = at(i1 * block_s + i2 * sub_s, sub_s)
        if p == 0:

            def add2_s(other, value):
                return value + land2_s[at(((i2 + other) % n2) * sub_s, sub_s)]

            total_small[home_s] = lax.fori_loop(1, n2, add2_s, own_s[home_s])

        def share2(step, carry):
            where = {"expert": peer2((i2 + step) % n2)}
            remote(total.at[home], total.at[home], send_sems.at[p, 2], ag2.at[p, i2], where)
            if p == 0:
                remote(total_small.at[home_s], total_small.at[home_s], send_s_sems.at[2],
                       ag2_s.at[i2], where)
            return carry

        lax.fori_loop(1, n2, share2, 0)

    def stage4(part):
        p, base, n1, i1, peer1, n2, i2, _ = part
        block, block_s = size // n1, rows_s // n1
        sub, sub_s = size // (n1 * n2), rows_s // (n1 * n2)

        def share1(step, carry):
            k = (i2 + step) % n2
            home = at(base + i1 * block + k * sub, sub)
            home_s = at(i1 * block_s + k * sub_s, sub_s)

            @pl.when(step > 0)
            def _():
                wait(total.at[home], ag2.at[p, k])
                if p == 0:
                    wait(total_small.at[home_s], ag2_s.at[k])

            def one(jump, carry):
                where = {"expert": peer1((i1 + jump) % n1)}
                remote(total.at[home], total.at[home], send_sems.at[p, 3], ag1.at[p, i1], where)
                if p == 0:
                    remote(total_small.at[home_s], total_small.at[home_s], send_s_sems.at[3],
                           ag1_s.at[i1], where)
                return carry

            lax.fori_loop(1, n1, one, 0)
            return carry

        lax.fori_loop(0, n2, share1, 0)

    order = [(1, 0), (1, 1), (1, 2), (2, 0), (1, 3), (2, 1), (2, 2), (3, 0), (2, 3), (3, 1),
             (3, 2), (4, 0), (3, 3), (4, 1), (4, 2), (4, 3)]
    stages = (None, stage1, stage2, stage3, stage4)
    for stage, p in order:
        if p < pieces:
            stages[stage](parts[p])
    for p, base, n1, i1, _, n2, _, _ in parts:
        block, block_s = size // n1, rows_s // n1
        sub, sub_s = size // (n1 * n2), rows_s // (n1 * n2)

        def in_last(step, carry):
            j = (i1 + step) % n1
            wait(total.at[at(base + j * block, block)], ag1.at[p, j])
            if p == 0:
                wait(total_small.at[at(j * block_s, block_s)], ag1_s.at[j])
            return carry

        lax.fori_loop(1, n1, in_last, 0)
        for lane, count, count_s in (
            (0, (n1 - 1) * block, (n1 - 1) * block_s),
            (1, (n2 - 1) * sub, (n2 - 1) * sub_s),
            (2, (n2 - 1) * sub, (n2 - 1) * sub_s),
            (3, (n1 - 1) * block, (n1 - 1) * block_s),
        ):
            wait(own.at[pl.ds(0, count)], send_sems.at[p, lane])
            if p == 0:
                wait(own_s.at[pl.ds(0, count_s)], send_s_sems.at[lane])
    wait(mate, mate_send.at[0])
    wait(mate_s, mate_send.at[1])
    wait(land_in, wide_send.at[0])
    wait(land_out, wide_send.at[1])
    wait(land_in, wide_recv.at[0])
    wait(land_out, wide_recv.at[1])
    for lane, target in enumerate((section_out, section_grad)):
        wait(target.at[section], hand_load.at[lane])
        wait(target.at[section], wide_send.at[2 + lane])
        wait(target.at[1 - section], wide_recv.at[2 + lane])


def merge(experts, mains, smalls, outs, grads, wins, wouts):
    rows, width = mains[0].shape
    rows_s = smalls[0].shape[0]
    per = experts // PLANES
    most, least = max(per, PLANES), min(per, PLANES)
    pieces = pieces_of(experts, rows)
    seconds = (pieces - 1) * (rows // pieces // per) + rows // pieces // PLANES
    vmem = pl.BlockSpec(memory_space=pltpu.VMEM)
    hbm = pl.BlockSpec(memory_space=pl.ANY)
    sems = lambda *shape: pltpu.SemaphoreType.DMA(shape)
    return pl.pallas_call(
        functools.partial(merge_kernel, experts),
        out_shape=[
            jax.ShapeDtypeStruct((rows, width), BF),
            jax.ShapeDtypeStruct((rows_s, 128), F32),
            jax.ShapeDtypeStruct(wins.shape[1:], BF),
            jax.ShapeDtypeStruct(wouts.shape[1:], BF),
            jax.ShapeDtypeStruct((2, *outs[0].shape), BF),
            jax.ShapeDtypeStruct((2, *grads[0].shape), F32),
        ],
        in_specs=[hbm] * 10,
        out_specs=[vmem, vmem, hbm, hbm, hbm, hbm],
        scratch_shapes=[
            pltpu.VMEM((rows, width), BF),
            pltpu.VMEM((rows, width), BF),
            pltpu.VMEM((rows, width), BF),
            pltpu.VMEM((seconds, width), BF),
            pltpu.VMEM((seconds, width), F32),
            pltpu.VMEM((rows_s, 128), F32),
            pltpu.VMEM((rows_s, 128), F32),
            pltpu.VMEM((rows_s, 128), F32),
            pltpu.VMEM((rows_s // per, 128), F32),
            sems(2), sems(2), sems(pieces, most), sems(1), sems(4), sems(4), sems(2),
            sems(pieces, 4), sems(4), sems(pieces, most), sems(most), sems(pieces, most), sems(most),
            sems(pieces, most), sems(most), sems(pieces, most), sems(most),
        ],
        compiler_params=pltpu.CompilerParams(
            collective_id=3, has_side_effects=True, vmem_limit_bytes=60 * 2**20
        ),
        name="merge",
    )(*mains, *smalls, *outs, *grads, wins, wouts)


def route_plan(route_ids, experts, capacity):
    tokens = route_ids.shape[0]
    main = capacity // 16 * 16
    extra = capacity - main
    lanes = jnp.arange(experts, dtype=jnp.int32)[None, :]
    first = (route_ids[:, 0:1] == lanes).astype(F32)
    second = (route_ids[:, 1:2] == lanes).astype(F32)
    places = jnp.arange(tokens, dtype=jnp.int32)
    earlier = (places[:, None] > places[None, :]).astype(BF)
    counts = dot(earlier, (first + second).astype(BF), NN)
    row = jnp.arange(experts * main, dtype=jnp.int32)[:, None]
    row_x = jnp.arange(experts * 16, dtype=jnp.int32)[:, None]
    place, place_x = [], []
    for j, hot in enumerate((first, second)):
        rank = jnp.sum(counts * hot, axis=-1).astype(jnp.int32)
        slot = jnp.where(rank < main, route_ids[:, j] * main + rank, -1)
        slot_x = jnp.where(rank < main, -experts * 16, route_ids[:, j] * 16 + rank - main)
        place.append((row == slot[None, :]).astype(BF))
        place_x.append(
            [(row_x == slot_x[None, :] + q * extra).astype(BF) for q in range(16 // extra)]
        )
    return first, second, place, place_x


def pack(plan, experts, values0, values1=None):
    _, _, place, place_x = plan
    width = values0.shape[1]
    if values1 is None:
        main = dot(place[0] + place[1], values0, NN)
    else:
        main = dot(place[0], values0, NN) + dot(place[1], values1, NN)
    small = 0.0
    for q in range(width // 256):
        part = slice(q * 256, (q + 1) * 256)
        if values1 is None:
            small += dot(place_x[0][q] + place_x[1][q], values0[:, part], NN)
        else:
            small += dot(place_x[0][q], values0[:, part], NN)
            small += dot(place_x[1][q], values1[:, part], NN)
    return main.astype(BF).reshape(experts, -1, width), small.astype(BF).reshape(experts, 16, 256)


def unpack(place, place_x, main, small, width):
    main = main.reshape(-1, width)
    small = small.reshape(-1, 256)
    tail = [dot(place_x[q], small, TN) for q in range(width // 256)]
    return dot(place, main, TN) + jnp.concatenate(tail, axis=1)


def layer_attend(current, plan, weights):
    qkv, proj, router, vectors = weights
    first, second = plan[:2]
    *kept, middle, routed = attend(current, qkv, proj, vectors)
    logits = dot(routed, router, NN)
    gap = jnp.sum(logits * (first - second), axis=-1, keepdims=True)
    gate0, gate1 = jax.nn.sigmoid(gap), jax.nn.sigmoid(-gap)
    return current, kept, middle, routed, gate0, gate1


def layer_combine(kept, plan, produced):
    middle, gate0, gate1 = kept[2], kept[4], kept[5]
    _, _, place, place_x = plan
    width = middle.shape[1]
    combined = [
        unpack(place[j], place_x[j], produced[0], produced[1], width).astype(BF) for j in range(2)
    ]
    outputs = middle + (gate0 * combined[0].astype(F32) + gate1 * combined[1].astype(F32))
    return outputs, combined


def layer_grads(seed, kept, plan, experts):
    gate0, gate1 = kept[4], kept[5]
    return pack(plan, experts, (gate0 * seed).astype(BF), (gate1 * seed).astype(BF))


def layer_backward(seed, kept, combined, returned, plan, weights):
    qkv, proj, router, vectors = weights
    first, second, place, place_x = plan
    current, inner, middle, routed, gate0, gate1 = kept
    combined0, combined1 = combined
    width = middle.shape[1]
    experts = router.shape[1]
    grad_gap = gate0 * gate1 * jnp.sum(
        seed * (combined0.astype(F32) - combined1.astype(F32)), axis=-1, keepdims=True
    )
    grad_logits = grad_gap * (first - second)
    grad_router = dot(grad_logits, routed.astype(F32), TN, precision=HIGH)
    both_x = [one + two for one, two in zip(place_x[0], place_x[1])]
    grad_routed = unpack(place[0] + place[1], both_x, returned[0], returned[1], width) + dot(
        grad_logits, router.astype(F32), NT, precision=HIGH
    )
    grad_middle, grad_gain_ffn = norm_back(middle, vectors[4], grad_routed)
    grad_middle = grad_middle + seed
    grad_current, main, sums = attend_back(
        current, inner, grad_middle, qkv, proj, vectors
    )
    small = jnp.concatenate([sums, grad_gain_ffn[None], grad_router]).reshape(-1, 128)
    small = jnp.pad(small, ((0, -small.shape[0] % (16 * experts)), (0, 0)))
    return grad_current, main, small


def finish_kernel(
    which_ref, win_ref, land_in_ref, wout_ref, land_out_ref, q_ref, k_ref, v_ref, p_ref,
    gwin_ref, gwout_ref, gqkv_ref, gproj_ref,
):
    gwin_ref[...] = (win_ref[0].astype(F32) + land_in_ref[...].astype(F32)).astype(BF)
    gwout_ref[...] = (wout_ref[0].astype(F32) + land_out_ref[...].astype(F32)).astype(BF)
    width = gproj_ref.shape[1]
    for at, part in enumerate((q_ref, k_ref, v_ref)):
        gqkv_ref[:, at * width : (at + 1) * width] = part[...].astype(F32)
    gproj_ref[...] = p_ref[...].astype(F32)


def finish(section, wins, land_in, wouts, land_out, total):
    _, width, ff = wins.shape
    steps = 12
    low, tall = width // steps, ff // steps
    shared = [
        pl.BlockSpec((low, width), functools.partial(lambda k, i, s: (k * steps + i, 0), k))
        for k in range(4)
    ]
    return pl.pallas_call(
        finish_kernel,
        grid_spec=pltpu.PrefetchScalarGridSpec(
            num_scalar_prefetch=1,
            grid=(steps,),
            in_specs=[
                pl.BlockSpec((1, low, ff), lambda i, s: (s[0], i, 0)),
                pl.BlockSpec((low, ff), lambda i, s: (i, 0)),
                pl.BlockSpec((1, tall, width), lambda i, s: (s[0], i, 0)),
                pl.BlockSpec((tall, width), lambda i, s: (i, 0)),
                *shared,
            ],
            out_specs=[
                pl.BlockSpec((low, ff), lambda i, s: (i, 0)),
                pl.BlockSpec((tall, width), lambda i, s: (i, 0)),
                pl.BlockSpec((low, 3 * width), lambda i, s: (i, 0)),
                pl.BlockSpec((low, width), lambda i, s: (i, 0)),
            ],
        ),
        out_shape=[
            jax.ShapeDtypeStruct((width, ff), BF),
            jax.ShapeDtypeStruct((ff, width), BF),
            jax.ShapeDtypeStruct((width, 3 * width), F32),
            jax.ShapeDtypeStruct((width, width), F32),
        ],
        compiler_params=pltpu.CompilerParams(vmem_limit_bytes=32 * 2**20),
        name="finish",
    )(section.reshape(1).astype(jnp.int32), wins, land_in, wouts, land_out, *[total] * 4)


def shards(
    block_input, cotangent, expert_ids, qkv_weight, query_bias, value_bias, proj_weight,
    proj_bias, attn_gain, ffn_gain, router_weight, in_weight, out_weight,
):
    section = lax.axis_index("section")
    width = block_input.shape[2]
    experts = router_weight.shape[2]
    tokens = block_input.shape[1]
    capacity = capacity_of(tokens, expert_ids.shape[3], experts)
    extra = capacity % 16

    def swapped(array):
        return lax.ppermute(array, "section", SWAP)

    vectors = jnp.concatenate([query_bias, value_bias, proj_bias, attn_gain, ffn_gain])
    shared = [qkv_weight[0], vectors, proj_weight[0], router_weight[0]]
    shared_other = [swapped(part) for part in shared]
    own_experts = (in_weight[0, 0], out_weight[0, 0])
    other_experts = tuple(swapped(part) for part in own_experts)
    layers = []
    for l in range(2):
        qkv, vector, proj, router = (
            jnp.where(section == l, own, other) for own, other in zip(shared, shared_other)
        )
        layers.append((qkv, proj, router, vector))
    rows = lax.dynamic_index_in_dim(block_input, section, 0, keepdims=False)
    seed = lax.dynamic_index_in_dim(cotangent, section, 0, keepdims=False)
    ids = lax.dynamic_index_in_dim(expert_ids, section, 1, keepdims=False)
    plans = [route_plan(ids[l], experts, capacity) for l in range(2)]

    kept0 = layer_attend(rows, plans[0], layers[0])
    done0 = moe(
        True, False, 0, extra, 0, pack(plans[0], experts, kept0[3]), None, None, own_experts,
        other_experts,
    )
    out0, combined0 = layer_combine(kept0, plans[0], done0[:2])
    out0 = out0.astype(BF)
    seed = seed.astype(F32)
    kept1 = layer_attend(out0, plans[1], layers[1])
    done1 = moe(
        True, True, 1, extra, 1, pack(plans[1], experts, kept1[3]),
        layer_grads(seed, kept1, plans[1], experts), None, own_experts, other_experts,
    )
    out1, combined1 = layer_combine(kept1, plans[1], done1[:2])
    out1 = out1.astype(BF)

    grad1, main1, small1 = layer_backward(
        seed, kept1, combined1, done1[2:4], plans[1], layers[1]
    )
    grad1 = grad1.astype(BF)
    seed0 = grad1.astype(F32)
    back0 = moe(
        False, True, 2, extra, 0, None, layer_grads(seed0, kept0, plans[0], experts), done0[2:4],
        own_experts, other_experts, done1[4:],
    )
    grad0, main0, small0 = layer_backward(
        seed0, kept0, combined0, back0[:2], plans[0], layers[0]
    )
    total, small, land_in, land_out, section_out, section_grad = merge(
        experts, (main0, main1), (small0, small1), (out0, out1), (grad0, seed0), back0[2],
        back0[3],
    )
    grad_win, grad_wout, grad_qkv, grad_proj = finish(
        section, back0[2], land_in, back0[3], land_out, total
    )
    small = small[: (5 + experts) * width // 128].reshape(5 + experts, width)
    return (
        section_out[None],
        section_grad[None],
        grad_qkv[None],
        small[0][None],
        small[1][None],
        grad_proj[None],
        small[2][None],
        small[3][None],
        small[4][None],
        small[5:].T[None],
        grad_win[None, None],
        grad_wout[None, None],
    )


def solution(mesh):
    vector, matrix = P("section", None), P("section", None, None)
    expert = P("section", "expert", None, None)
    rows = P("section", None, "expert", None)
    return jax.shard_map(
        shards,
        mesh=mesh,
        in_specs=(
            P(None, "expert", None),
            P(None, "expert", None),
            P(None, None, "expert", None),
            matrix, vector, vector, matrix, vector, vector, vector, matrix, expert, expert,
        ),
        out_specs=(
            rows, rows, matrix, vector, vector, matrix, vector, vector, vector, matrix,
            expert, expert,
        ),
        check_vma=False,
    )
```

```python
import functools

import jax
import jax.numpy as jnp
from jax import lax
from jax.experimental import pallas as pl
from jax.experimental.pallas import tpu as pltpu
from jax.sharding import PartitionSpec as P

HD = 64
EPS = 1e-06
NEG = -1e30
BF = jnp.bfloat16
F32 = jnp.float32
HIGH = lax.Precision.HIGHEST
SWAP = [(0, 1), (1, 0)]
MESH = pl.DeviceIdType.MESH
NN = ((1,), (0,))
NT = ((1,), (1,))
TN = ((0,), (0,))
PLANES = 4
CHUNK = 512


def dot(a, b, dims, kind=F32, precision=None):
    return lax.dot_general(
        a, b, (dims, ((), ())), precision=precision, preferred_element_type=F32
    ).astype(kind)


def capacity_of(tokens, choices, experts):
    return tokens * choices // experts + max(1, tokens * choices // (16 * experts))


def inverse_rms(field):
    return lax.rsqrt(jnp.mean(field * field, axis=-1, keepdims=True) + EPS)


def places_of(route_ids, experts, capacity):
    tokens = route_ids.shape[0]
    main = capacity // 16 * 16
    lanes = jnp.arange(experts, dtype=jnp.int32)[None, :]
    hots = [(route_ids[:, j : j + 1] == lanes).astype(F32) for j in range(2)]
    spots = jnp.arange(tokens, dtype=jnp.int32)
    earlier = (spots[:, None] > spots[None, :]).astype(BF)
    counts = dot(earlier, (hots[0] + hots[1]).astype(BF), NN)
    slots, slots_x = [], []
    for j, hot in enumerate(hots):
        rank = jnp.sum(counts * hot, axis=-1).astype(jnp.int32)
        slots.append(jnp.where(rank < main, route_ids[:, j] * main + rank, -1))
        slots_x.append(
            jnp.where(rank < main, -experts * 16, route_ids[:, j] * 16 + rank - main)
        )
    table = jnp.stack(slots + slots_x + [route_ids[:, 0], route_ids[:, 1]] * 2, axis=1)
    return table, table.T


def pack_into(main_ref, small_ref, across, extra, values):
    experts, main, width = main_ref.shape
    tokens = across.shape[1]
    tall = 256
    each = tall // main

    def hot(rows, slot):
        return (rows == across[slot : slot + 1]).astype(BF)

    def one(step, carry):
        rows = lax.broadcasted_iota(jnp.int32, (tall, tokens), 0) + step * tall
        if len(values) == 1:
            total = dot(hot(rows, 0) + hot(rows, 1), values[0], NN)
        else:
            total = dot(hot(rows, 0), values[0], NN) + dot(hot(rows, 1), values[1], NN)
        main_ref[pl.ds(step * each, each)] = total.astype(BF).reshape(each, main, width)
        return carry

    lax.fori_loop(0, experts * main // tall, one, 0)

    def one_x(step, carry):
        rows = lax.broadcasted_iota(jnp.int32, (tall, tokens), 0) + step * tall
        total = 0.0
        for q in range(width // 256):
            span = slice(q * 256, (q + 1) * 256)
            hots = [hot(rows - q * extra, 2), hot(rows - q * extra, 3)]
            if len(values) == 1:
                total += dot(hots[0] + hots[1], values[0][:, span], NN)
            else:
                total += dot(hots[0], values[0][:, span], NN)
                total += dot(hots[1], values[1][:, span], NN)
        small_ref[pl.ds(step * (tall // 16), tall // 16)] = total.astype(BF).reshape(
            tall // 16, 16, 256
        )
        return carry

    lax.fori_loop(0, experts * 16 // tall, one_x, 0)


def unpack_from(main_ref, small_ref, down, extra, slots):
    experts, main, width = main_ref.shape
    tokens = down.shape[0]
    lanes = lax.broadcasted_iota(jnp.int32, (tokens, experts * main), 1)
    hot = sum((lanes == down[:, j : j + 1]).astype(BF) for j in slots)
    total = dot(hot, main_ref[...].reshape(experts * main, width), NN)
    lanes = lax.broadcasted_iota(jnp.int32, (tokens, experts * 16), 1)
    small = small_ref[...].reshape(experts * 16, 256)
    tail = [
        dot(sum((lanes - q * extra == down[:, 2 + j : 3 + j]).astype(BF) for j in slots), small, NN)
        for q in range(width // 256)
    ]
    return total + jnp.concatenate(tail, axis=1)


def signs_down(down):
    lanes = lax.broadcasted_iota(jnp.int32, (down.shape[0], 128), 1)
    return (lanes == down[:, 4:5]).astype(F32) - (lanes == down[:, 5:6]).astype(F32)


def causal_weights(scores, place, block):
    length = scores.shape[0]
    keys = lax.broadcasted_iota(jnp.int32, scores.shape, 0)
    queries = lax.broadcasted_iota(jnp.int32, scores.shape, 1) + place * block
    return jnp.where(keys <= queries, scores * HD ** (-0.5), NEG)


def load_shared(layer, own, other, qkv_ref, proj_ref, sems):
    section = lax.axis_index("section")

    def load(pair):
        pltpu.make_async_copy(pair[0], qkv_ref, sems.at[0]).start()
        pltpu.make_async_copy(pair[1], proj_ref, sems.at[1]).start()

    pl.when(section == layer)(lambda: load(own))
    pl.when(section != layer)(lambda: load(other))
    return [
        pltpu.make_async_copy(ref, ref, sems.at[at]) for at, ref in enumerate((qkv_ref, proj_ref))
    ]


def attend_kernel(layer, extra, chained, *refs):
    refs = list(refs)

    def take(count):
        taken, refs[:count] = refs[:count], []
        return taken

    own_qkv, own_proj, other_qkv, other_proj = take(4)
    vectors_ref, router_ref, down_ref, across_ref = take(4)
    if chained:
        before_ref, before_gates_ref, before_down_ref, back_ref, back_x_ref, seed_ref = take(6)
    else:
        (current_ref,) = take(1)
    normed_ref, queries_ref, keys_ref, values_ref, log_ref, attended_ref = take(6)
    middle_ref, routed_ref, gates_ref, rows_ref, rows_x_ref = take(5)
    if chained:
        current_ref, apart_ref, grads_ref, grads_x_ref = take(4)
    qkv_ref, proj_ref, sems = take(3)
    loads = load_shared(
        layer, (own_qkv, own_proj), (other_qkv, other_proj), qkv_ref, proj_ref, sems
    )
    if chained:
        down = before_down_ref[...]
        gates = before_gates_ref[...]
        one = unpack_from(back_ref, back_x_ref, down, extra, (0,))
        two = unpack_from(back_ref, back_x_ref, down, extra, (1,))
        apart_ref[...] = one - two
        current_ref[...] = (
            before_ref[...] + (gates[:, 0:1] * one + gates[:, 1:2] * two)
        ).astype(BF)
    tokens, width = normed_ref.shape
    block = tokens // 2
    qbias, vbias, pbias, gain_attn, gain_ffn = (vectors_ref[l : l + 1] for l in range(5))
    current = current_ref[...].astype(F32)
    normed = (current * inverse_rms(current) * gain_attn).astype(BF)
    normed_ref[...] = normed
    loads[0].wait()
    for at in range(0, width, 256):
        span = slice(at, at + 256)
        queries_ref[:, span] = (dot(normed, qkv_ref[:, span], NN) + qbias[:, span]).astype(BF)
        keys_ref[:, span] = dot(normed, qkv_ref[:, width + at : width + at + 256], NN, BF)
        values_ref[:, span] = (
            dot(normed, qkv_ref[:, 2 * width + at : 2 * width + at + 256], NN) + vbias[:, span]
        ).astype(BF)
    lane = lax.broadcasted_iota(jnp.int32, (1, 2 * HD), 1)

    def pair(step, carry):
        span = pl.ds(pl.multiple_of(step * 2 * HD, 2 * HD), 2 * HD)
        for place in range(2):
            rows = slice(place * block, (place + 1) * block)
            reach = slice(0, (place + 1) * block)
            total = jnp.zeros((block, 2 * HD), F32)
            for side in range(2):
                mine = (lane // HD) == side
                queries = jnp.where(mine, queries_ref[rows, span], 0.0).astype(BF)
                scores = causal_weights(dot(keys_ref[reach, span], queries, NT), place, block)
                top = jnp.max(scores, axis=0, keepdims=True)
                weights = jnp.exp(scores - top)
                amount = jnp.sum(weights, axis=0, keepdims=True)
                log_ref[step, side : side + 1, rows] = top + jnp.log(amount)
                probs = (weights * (1.0 / amount)).astype(BF)
                values = jnp.where(mine, values_ref[reach, span], 0.0).astype(BF)
                total += dot(probs, values, TN)
            attended_ref[rows, span] = total.astype(BF)
        return carry

    lax.fori_loop(0, width // (2 * HD), pair, 0)
    loads[1].wait()
    middle = current_ref[...].astype(F32) + (dot(attended_ref[...], proj_ref[...], NN) + pbias)
    middle_ref[...] = middle
    routed = (middle * inverse_rms(middle) * gain_ffn).astype(BF)
    routed_ref[...] = routed
    logits = dot(routed, router_ref[...], NN)
    gap = jnp.sum(logits * signs_down(down_ref[...]), axis=-1, keepdims=True)
    gate0, gate1 = jax.nn.sigmoid(gap), jax.nn.sigmoid(-gap)
    gates_ref[:, 0:1] = gate0
    gates_ref[:, 1:2] = gate1
    across = across_ref[...]
    pack_into(rows_ref, rows_x_ref, across, extra, [routed])
    if chained:
        seed = seed_ref[...].astype(F32)
        pack_into(
            grads_ref, grads_x_ref, across, extra,
            [(gate0 * seed).astype(BF), (gate1 * seed).astype(BF)],
        )


def shared_scratch(width):
    return [
        pltpu.VMEM((width, 3 * width), BF),
        pltpu.VMEM((width, width), BF),
        pltpu.SemaphoreType.DMA((2,)),
    ]


def attend(layer, extra, experts, main, weights, current=None, chain=None):
    own, other, router, vectors, down, across = weights
    tokens, width = (current if chain is None else chain[0]).shape
    low = jax.ShapeDtypeStruct((tokens, width), BF)
    wide = jax.ShapeDtypeStruct((tokens, width), F32)
    rows = [
        jax.ShapeDtypeStruct((experts, main, width), BF),
        jax.ShapeDtypeStruct((experts, 16, 256), BF),
    ]
    out_shape = [low, low, low, low]
    out_shape += [jax.ShapeDtypeStruct((width // (2 * HD), 2, tokens), F32), low, wide, low]
    out_shape += [jax.ShapeDtypeStruct((tokens, 2), F32), *rows]
    if chain is not None:
        out_shape += [low, wide, *rows]
    vmem = pl.BlockSpec(memory_space=pltpu.VMEM)
    hbm = pl.BlockSpec(memory_space=pl.ANY)
    operands = (current,) if chain is None else chain
    return pl.pallas_call(
        functools.partial(attend_kernel, layer, extra, chain is not None),
        out_shape=out_shape,
        in_specs=[hbm] * 4 + [vmem] * (4 + len(operands)),
        out_specs=[vmem] * len(out_shape),
        scratch_shapes=shared_scratch(width),
        compiler_params=pltpu.CompilerParams(vmem_limit_bytes=58 * 2**20),
        cost_estimate=pl.CostEstimate(
            flops=8 * tokens * width * width + 4 * tokens * tokens * width * 4,
            bytes_accessed=16 * 2**20, transcendentals=12 * tokens * tokens,
        ),
        name="attend",
    )(*own, *other, vectors, router, down, across, *operands)


def attend_back_kernel(layer, extra, last, *refs):
    refs = list(refs)

    def take(count):
        taken, refs[:count] = refs[:count], []
        return taken

    own_qkv, own_proj, other_qkv, other_proj = take(4)
    vectors_ref, router_ref, down_ref, across_ref = take(4)
    current_ref, normed_ref, queries_ref, keys_ref, values_ref, log_ref, attended_ref = take(7)
    middle_ref, routed_ref, gates_ref, seed_ref, back_ref, back_x_ref = take(6)
    if last:
        made_ref, made_x_ref, before_gates_ref, before_across_ref = take(4)
    else:
        (apart_ref,) = take(1)
    grad_current_ref, main_ref, sums_ref, grad_router_ref = take(4)
    if last:
        out_ref, grads_ref, grads_x_ref = take(3)
    grad_attended, grad_queries, grad_keys, grad_values, grad_middle_ref = take(5)
    total_keys, total_values, qkv_ref, proj_ref, sems = take(5)
    loads = load_shared(
        layer, (own_qkv, own_proj), (other_qkv, other_proj), qkv_ref, proj_ref, sems
    )
    tokens, width = normed_ref.shape
    block = tokens // 2
    down = down_ref[...]
    gate0, gate1 = gates_ref[:, 0:1], gates_ref[:, 1:2]
    middle = middle_ref[...]
    seed = seed_ref[...].astype(F32)
    if last:
        one = unpack_from(made_ref, made_x_ref, down, extra, (0,))
        two = unpack_from(made_ref, made_x_ref, down, extra, (1,))
        out_ref[...] = (middle + (gate0 * one + gate1 * two)).astype(BF)
        apart = one - two
    else:
        apart = apart_ref[...]
    gap = gate0 * gate1 * jnp.sum(seed * apart, axis=-1, keepdims=True)
    terms = gap * routed_ref[...].astype(F32)
    high = terms.astype(BF)
    rest = (terms - high.astype(F32)).astype(BF)
    across = across_ref[...]
    rows = lax.broadcasted_iota(jnp.int32, (grad_router_ref.shape[0], tokens), 0)
    signs = (
        (rows == across[4:5]).astype(F32) - (rows == across[5:6]).astype(F32)
    ).astype(BF)
    grad_router_ref[...] = dot(signs, high, NN) + dot(signs, rest, NN)
    grad_routed = unpack_from(back_ref, back_x_ref, down, extra, (0, 1)) + gap * dot(
        signs_down(down).astype(BF), router_ref[...], NT
    )
    scale = inverse_rms(middle)
    unit = middle * scale
    sums_ref[4:5] = jnp.sum(grad_routed * unit, axis=0, keepdims=True)
    scaled = grad_routed * vectors_ref[4:5]
    grad_middle_ref[...] = seed + scale * (
        scaled - unit * jnp.mean(scaled * unit, axis=-1, keepdims=True)
    )
    grad_branch = grad_middle_ref[...].astype(BF)
    sums_ref[2:3] = jnp.sum(grad_branch.astype(F32), axis=0, keepdims=True)
    loads[1].wait()
    grad_attended[...] = dot(grad_branch, proj_ref[...], NT, BF)
    for at in range(0, width, 256):
        span = slice(at, at + 256)
        main_ref[3 * width : 4 * width, span] = dot(
            attended_ref[...], grad_middle_ref[:, span].astype(BF), TN, BF
        )
    lane = lax.broadcasted_iota(jnp.int32, (1, 2 * HD), 1)

    def pair(step, carry):
        span = pl.ds(pl.multiple_of(step * 2 * HD, 2 * HD), 2 * HD)
        for place in range(2):
            rows = slice(place * block, (place + 1) * block)
            reach = slice(0, (place + 1) * block)
            total = jnp.zeros((block, 2 * HD), F32)
            term_keys = term_values = 0.0
            for side in range(2):
                mine = (lane // HD) == side
                queries = jnp.where(mine, queries_ref[rows, span], 0.0).astype(BF)
                grads = jnp.where(mine, grad_attended[rows, span], 0.0).astype(BF)
                scores = causal_weights(dot(keys_ref[reach, span], queries, NT), place, block)
                weights = jnp.exp(scores - log_ref[step, side : side + 1, rows])
                grad_probs = dot(values_ref[reach, span], grads, NT)
                inner = jnp.sum(weights * grad_probs, axis=0, keepdims=True)
                grad_scores = (weights * (grad_probs - inner)).astype(BF)
                keys = jnp.where(mine, keys_ref[reach, span], 0.0).astype(BF)
                total += dot(grad_scores, keys, TN)
                term_values += dot(weights.astype(BF), grads, NN)
                term_keys += dot(grad_scores, queries, NN)
            grad_queries[rows, span] = (total * HD ** (-0.5)).astype(BF)
            if place == 0:
                total_keys[...] = term_keys
                total_values[...] = term_values
            else:
                term_keys = jnp.concatenate(
                    [term_keys[:block] + total_keys[...], term_keys[block:]]
                )
                term_values = jnp.concatenate(
                    [term_values[:block] + total_values[...], term_values[block:]]
                )
                grad_keys[:, span] = (term_keys * HD ** (-0.5)).astype(BF)
                grad_values[:, span] = term_values.astype(BF)
        return carry

    lax.fori_loop(0, width // (2 * HD), pair, 0)
    sums_ref[0:1] = jnp.sum(grad_queries[...].astype(F32), axis=0, keepdims=True)
    sums_ref[1:2] = jnp.sum(grad_values[...].astype(F32), axis=0, keepdims=True)
    loads[0].wait()
    grad_normed = jnp.zeros((tokens, width), F32)
    for which, grads in enumerate((grad_queries, grad_keys, grad_values)):
        for at in range(0, width, 256):
            main_ref[which * width : (which + 1) * width, at : at + 256] = dot(
                normed_ref[...], grads[:, at : at + 256], TN, BF
            )
        grad_normed += dot(grads[...], qkv_ref[:, which * width : (which + 1) * width], NT)
    current = current_ref[...].astype(F32)
    scale = inverse_rms(current)
    unit = current * scale
    sums_ref[3:4] = jnp.sum(grad_normed * unit, axis=0, keepdims=True)
    scaled = grad_normed * vectors_ref[3:4]
    grad_current = grad_middle_ref[...] + scale * (
        scaled - unit * jnp.mean(scaled * unit, axis=-1, keepdims=True)
    )
    if last:
        grad_current = grad_current.astype(BF).astype(F32)
    grad_current_ref[...] = grad_current
    if last:
        before0, before1 = before_gates_ref[:, 0:1], before_gates_ref[:, 1:2]
        pack_into(
            grads_ref, grads_x_ref, before_across_ref[...], extra,
            [(before0 * grad_current).astype(BF), (before1 * grad_current).astype(BF)],
        )


def attend_back(layer, extra, experts, main, weights, kept, seed, back, rest, last):
    own, other, router, vectors, down, across = weights
    tokens, width = kept[0].shape
    wide = jax.ShapeDtypeStruct((tokens, width), F32)
    out_shape = [
        wide,
        jax.ShapeDtypeStruct((4 * width, width), BF),
        jax.ShapeDtypeStruct((5, width), F32),
        jax.ShapeDtypeStruct((experts, width), F32),
    ]
    if last:
        out_shape += [
            jax.ShapeDtypeStruct((tokens, width), BF),
            jax.ShapeDtypeStruct((experts, main, width), BF),
            jax.ShapeDtypeStruct((experts, 16, 256), BF),
        ]
    vmem = pl.BlockSpec(memory_space=pltpu.VMEM)
    hbm = pl.BlockSpec(memory_space=pl.ANY)
    operands = (*kept, seed, *back, *rest)
    return pl.pallas_call(
        functools.partial(attend_back_kernel, layer, extra, last),
        out_shape=out_shape,
        in_specs=[hbm] * 4 + [vmem] * (4 + len(operands)),
        out_specs=[vmem] * len(out_shape),
        scratch_shapes=[pltpu.VMEM((tokens, width), BF)] * 4
        + [pltpu.VMEM((tokens, width), F32)]
        + [pltpu.VMEM((tokens // 2, 2 * HD), F32)] * 2
        + shared_scratch(width),
        compiler_params=pltpu.CompilerParams(vmem_limit_bytes=58 * 2**20),
        cost_estimate=pl.CostEstimate(
            flops=16 * tokens * width * width + 10 * tokens * tokens * width * 4,
            bytes_accessed=24 * 2**20, transcendentals=12 * tokens * tokens,
        ),
        name="attend_back",
    )(*own, *other, vectors, router, down, across, *operands)


def gelu_and_slope(hidden):
    root = 0.7978845608028654
    square = hidden * hidden
    bent = jnp.tanh(hidden * (root + (root * 0.044715) * square))
    half = 0.5 + 0.5 * bent
    slope = half + (0.5 * hidden) * (1.0 - bent * bent) * (root + (root * 0.134145) * square)
    return hidden * half, slope


def moe_kernel(experts, extra, layer, ahead, back, *refs):
    refs = list(refs)

    def take(count):
        taken, refs[:count] = refs[:count], []
        return taken

    rows_in, grads_in, kept_in = [], [], []
    if ahead:
        rows_in = take(2)
    if back:
        grads_in = take(2)
    if back and not ahead:
        kept_in = take(2)
    own_weights = take(2)
    other_weights = take(2) if back else []
    if kept_in:
        take(2)
    produced_out = take(2) if ahead else []
    kept_out = take(2) if ahead and not back else []
    returned_out = take(2) if back else []
    gwin_out, gwout_out = take(2) if back else (None, None)
    if not back:
        other_weights = take(2)
    win, wout, weight_sem = take(3)
    if ahead:
        row_land, row_land_x, row_stage, row_stage_x, row_acc = take(5)
    if back:
        grad_land, grad_land_x, grad_stage, grad_stage_x, grad_acc, gwin, gwout = take(7)
        fold, fold_sem = take(2)
    send_sems, recv_sems, send_x_sems, recv_x_sems = take(4)
    takes_turns = ahead and not back
    if takes_turns:
        turn, push_send, push_recv = take(3)

    per = experts // PLANES
    main = (rows_in or grads_in)[0].shape[1]
    ff = win.shape[1]
    chunks = ff // CHUNK
    me = lax.axis_index("expert")
    plane = me // per
    spot = me % per
    half, low = plane // 2, plane % 2
    order = [
        (1 - half) * 2 + low,
        (1 - half) * 2 + (1 - low),
        half * 2 + (1 - low),
        plane,
    ]

    barrier = pltpu.get_barrier_semaphore()

    def greet(step, carry):
        pl.semaphore_signal(
            barrier, inc=1, device_id={"expert": (me + step) % experts}, device_id_type=MESH
        )
        return carry

    if back:
        gwin_out, gwout_out = gwin_out.at[layer], gwout_out.at[layer]

    def load(weights):
        pltpu.make_async_copy(weights[0], win, weight_sem.at[0]).start()
        pltpu.make_async_copy(weights[1], wout, weight_sem.at[1]).start()

    section = lax.axis_index("section")
    pl.when(section == layer)(lambda: load(own_weights))
    if back:
        pl.when(section != layer)(lambda: load(other_weights))
    lax.fori_loop(1, experts, greet, 0)
    if takes_turns:
        pl.semaphore_signal(
            barrier, inc=1, device_id={"section": 1 - section}, device_id_type=MESH
        )
        pl.semaphore_wait(barrier, experts)
        for lane in range(2):
            pltpu.make_async_remote_copy(
                src_ref=own_weights[lane],
                dst_ref=other_weights[lane],
                send_sem=push_send.at[lane],
                recv_sem=push_recv.at[lane],
                device_id={"section": 1 - section},
                device_id_type=MESH,
            ).start()

        def pushed():
            for lane, ref in enumerate(other_weights):
                pltpu.make_async_copy(ref, ref, push_recv.at[lane]).wait()

        @pl.when(section != layer)
        def _():
            pushed()
            load(other_weights)

        pl.when(section == 1)(lambda: pl.semaphore_wait(turn, 1))
    else:
        pl.semaphore_wait(barrier, experts - 1)

    def send(source, target, lane, peer, to_plane):
        pltpu.make_async_remote_copy(
            src_ref=source.at[peer],
            dst_ref=target.at[me],
            send_sem=send_sems.at[lane],
            recv_sem=recv_sems.at[lane, plane],
            device_id={"expert": peer},
            device_id_type=MESH,
        ).start()

    def send_x(source, target, lane, peer):
        pltpu.make_async_remote_copy(
            src_ref=source.at[peer],
            dst_ref=target.at[me],
            send_sem=send_x_sems.at[lane],
            recv_sem=recv_x_sems.at[lane],
            device_id={"expert": peer},
            device_id_type=MESH,
        ).start()

    def own(source, target, sem):
        pltpu.make_async_copy(source.at[me], target.at[me], sem).start()

    def send_all_x(pairs):
        def one(step, carry):
            for source, target, lane in pairs:
                send_x(source, target, lane, (me + step) % experts)
            return carry

        lax.fori_loop(1, experts, one, 0)
        for source, target, lane in pairs:
            own(source, target, recv_x_sems.at[lane])

    def send_plane(pairs, to_plane, is_own):
        def one(step, carry):
            for source, target, lane in pairs:
                send(source, target, lane, to_plane * per + (spot + step) % per, to_plane)
            return carry

        lax.fori_loop(1 if is_own else 0, per, one, 0)
        if is_own:
            for source, target, lane in pairs:
                own(source, target, recv_sems.at[lane, plane])

    def wait_plane(target, lane, from_plane):
        part = target.at[pl.ds(from_plane * per, per)]
        pltpu.make_async_copy(part, part, recv_sems.at[lane, from_plane]).wait()

    def wait_x(target, lane):
        pltpu.make_async_copy(target, target, recv_x_sems.at[lane]).wait()

    def wait_sent(source, lane):
        part = source.at[pl.ds(0, experts - 1)]
        pltpu.make_async_copy(part, part, send_sems.at[lane]).wait()

    def wait_sent_x(source, lane):
        part = source.at[pl.ds(0, experts - 1)]
        pltpu.make_async_copy(part, part, send_x_sems.at[lane]).wait()

    first_pairs, first_x = [], []
    if ahead:
        first_pairs.append((rows_in[0], row_land, 0))
        first_x.append((rows_in[1], row_land_x, 0))
    if back:
        first_pairs.append((grads_in[0], grad_land, 1))
        first_x.append((grads_in[1], grad_land_x, 1))
    send_all_x(first_x)
    for at, to_plane in enumerate(order):
        send_plane(first_pairs, to_plane, at == 3)

    tall = experts * 16
    tile_rows = lax.broadcasted_iota(jnp.int32, (experts * extra, tall), 0)
    tile_cols = lax.broadcasted_iota(jnp.int32, (experts * extra, tall), 1)
    parts = win.shape[0] // 256
    picks = [
        (tile_cols == (tile_rows // extra) * 16 + q * extra + tile_rows % extra).astype(BF)
        for q in range(parts)
    ]

    def gather_x(landed):
        flat = landed[...].reshape(tall, 256)
        return jnp.concatenate([dot(pick, flat, NN, BF) for pick in picks], axis=1)

    def spread_x(values):
        total = dot(picks[0], values[:, :256], TN)
        for q in range(1, parts):
            total += dot(picks[q], values[:, q * 256 : (q + 1) * 256], TN)
        return total.astype(BF).reshape(experts, 16, 256)

    def run(rows, grads, is_first):
        count = (rows if rows is not None else grads).shape[0]

        def one(step, carry):
            cols = pl.ds(pl.multiple_of(step * CHUNK, CHUNK), CHUNK)
            wide = win[:, cols]
            deep = wout[cols, :]
            active, slope = gelu_and_slope(dot(rows, wide, NN))
            active = active.astype(BF)
            if ahead:
                row_acc[pl.ds(0, count)] += dot(active, deep, NN)
            if back:
                grad_hidden = (dot(grads, deep, NT) * slope).astype(BF)
                grad_acc[pl.ds(0, count)] += dot(grad_hidden, wide, NT)
                term_in = dot(rows, grad_hidden, TN)
                term_out = dot(active, grads, TN)
                if is_first:
                    gwin[:, cols] = term_in
                    gwout[cols, :] = term_out
                else:
                    gwin[:, cols] += term_in
                    gwout[cols, :] += term_out
            return carry

        if ahead:
            row_acc[pl.ds(0, count)] = jnp.zeros((count, row_acc.shape[1]), F32)
        if back:
            grad_acc[pl.ds(0, count)] = jnp.zeros((count, grad_acc.shape[1]), F32)
        lax.fori_loop(0, chunks, one, 0)

    last_pairs, last_x = [], []
    if ahead:
        last_pairs.append((row_stage, produced_out[0], 2))
        last_x.append((row_stage_x, produced_out[1], 2))
        wait_x(row_land_x, 0)
    if back:
        last_pairs.append((grad_stage, returned_out[0], 3))
        last_x.append((grad_stage_x, returned_out[1], 3))
        wait_x(grad_land_x, 1)
    pltpu.make_async_copy(win, win, weight_sem.at[0]).wait()
    pltpu.make_async_copy(wout, wout, weight_sem.at[1]).wait()

    few = experts * extra
    if ahead:
        rows_x = gather_x(row_land_x)
        if kept_out:
            kept_out[1][...] = rows_x
    else:
        rows_x = kept_in[1][...]
    grads_x = gather_x(grad_land_x) if back else None
    run(rows_x, grads_x, True)
    if ahead:
        row_stage_x[...] = spread_x(row_acc[pl.ds(0, few)].astype(BF))
    if back:
        grad_stage_x[...] = spread_x(grad_acc[pl.ds(0, few)].astype(BF))
    send_all_x(last_x)

    width = win.shape[0]
    block = per * main
    for at in (3, 0, 1, 2):
        from_plane = order[at]
        places = pl.ds(from_plane * per, per)
        rows = grads = None
        if ahead:
            wait_plane(row_land, 0, from_plane)
            rows = row_land[places].reshape(block, width)
            if kept_out:
                kept_out[0][places] = row_land[places]
        else:
            rows = kept_in[0][places].reshape(block, width)
        if back:
            wait_plane(grad_land, 1, from_plane)
            grads = grad_land[places].reshape(block, width)
        run(rows, grads, False)
        if ahead:
            row_stage[places] = row_acc[...].astype(BF).reshape(per, main, width)
        if back:
            grad_stage[places] = grad_acc[...].astype(BF).reshape(per, main, width)
        send_plane(last_pairs, from_plane, at == 3)

    if takes_turns:
        pl.when(section == 0)(
            lambda: pl.semaphore_signal(
                turn, inc=1, device_id={"section": 1 - section}, device_id_type=MESH
            )
        )
    if back:
        for at in range(chunks):
            slot = at % 2
            span = slice(at * CHUNK, (at + 1) * CHUNK)
            if at >= 2:
                pltpu.make_async_copy(
                    fold.at[slot], gwin_out.at[:, span], fold_sem.at[slot]
                ).wait()
            fold[slot] = gwin[:, span].astype(BF)
            pltpu.make_async_copy(fold.at[slot], gwin_out.at[:, span], fold_sem.at[slot]).start()
        for slot in range(2):
            pltpu.make_async_copy(
                fold.at[slot], gwin_out.at[:, slice(0, CHUNK)], fold_sem.at[slot]
            ).wait()
        rows_of = ff // 6
        for at in range(6):
            span = slice(at * rows_of, (at + 1) * rows_of)
            wout[span, :] = gwout[span, :].astype(BF)
            pltpu.make_async_copy(wout.at[span, :], gwout_out.at[span, :], weight_sem.at[1]).start()
        pltpu.make_async_copy(wout, gwout_out, weight_sem.at[1]).wait()

    if takes_turns:
        pl.when(section == layer)(pushed)
        for lane, ref in enumerate(own_weights):
            pltpu.make_async_copy(ref, ref, push_send.at[lane]).wait()
    for source, target, lane in first_pairs:
        wait_sent(source, lane)
    for source, target, lane in first_x + last_x:
        wait_sent_x(source, lane)
    for source, target, lane in last_pairs:
        wait_sent(source, lane)
        for from_plane in range(PLANES):
            wait_plane(target, lane, from_plane)
    for source, target, lane in last_x:
        wait_x(target, lane)


def moe(ahead, back, collective, extra, layer, rows, grads, kept, own, other, stacked=()):
    lead = rows if ahead else grads
    experts, main, width = lead[0].shape
    ff = own[0].shape[1]
    few = experts * extra
    per = experts // PLANES
    block = per * main
    tall = jax.ShapeDtypeStruct((experts, main, width), BF)
    small = jax.ShapeDtypeStruct((experts, 16, 256), BF)
    vmem = pl.BlockSpec(memory_space=pltpu.VMEM)
    hbm = pl.BlockSpec(memory_space=pl.ANY)
    operands, in_specs = [], []
    for pair in (rows if ahead else (), grads if back else (), kept if back and not ahead else ()):
        operands += list(pair)
        in_specs += [vmem] * len(pair)
    operands += [*own, *other, *stacked]
    in_specs += [hbm] * (len(own) + len(other) + len(stacked))
    out_shape, out_specs = [], []
    if ahead:
        out_shape += [tall, small]
        out_specs += [vmem, vmem]
        if not back:
            out_shape += [tall, jax.ShapeDtypeStruct((few, width), BF)]
            out_specs += [vmem, vmem]
    if back:
        out_shape += [tall, small]
        out_specs += [vmem, vmem]
        out_shape += [
            jax.ShapeDtypeStruct((2, width, ff), BF),
            jax.ShapeDtypeStruct((2, ff, width), BF),
        ]
        out_specs += [hbm, hbm]
    if not back:
        out_shape += [jax.ShapeDtypeStruct(part.shape, BF) for part in own]
        out_specs += [hbm, hbm]
    aliases = {}
    if stacked:
        last = len(operands) - 2
        aliases = {last: len(out_shape) - 2, last + 1: len(out_shape) - 1}
    scratch = [
        pltpu.VMEM((width, ff), BF),
        pltpu.VMEM((ff, width), BF),
        pltpu.SemaphoreType.DMA((2,)),
    ]
    work = [
        pltpu.VMEM((experts, main, width), BF),
        pltpu.VMEM((experts, 16, 256), BF),
        pltpu.VMEM((experts, main, width), BF),
        pltpu.VMEM((experts, 16, 256), BF),
        pltpu.VMEM((max(block, few), width), F32),
    ]
    if ahead:
        scratch += work
    if back:
        scratch += work + [
            pltpu.VMEM((width, ff), F32),
            pltpu.VMEM((ff, width), F32),
            pltpu.VMEM((2, width, CHUNK), BF),
            pltpu.SemaphoreType.DMA((2,)),
        ]
    scratch += [
        pltpu.SemaphoreType.DMA((4,)),
        pltpu.SemaphoreType.DMA((4, PLANES)),
        pltpu.SemaphoreType.DMA((4,)),
        pltpu.SemaphoreType.DMA((4,)),
    ]
    if ahead and not back:
        scratch += [
            pltpu.SemaphoreType.REGULAR,
            pltpu.SemaphoreType.DMA((2,)),
            pltpu.SemaphoreType.DMA((2,)),
        ]
    return pl.pallas_call(
        functools.partial(moe_kernel, experts, extra, layer, ahead, back),
        out_shape=out_shape,
        in_specs=in_specs,
        out_specs=out_specs,
        scratch_shapes=scratch,
        input_output_aliases=aliases,
        cost_estimate=pl.CostEstimate(
            flops=(4 * ahead + 6 * back) * experts * main * width * ff,
            bytes_accessed=40 * 2**20 * (ahead + back),
            transcendentals=0,
        ),
        compiler_params=pltpu.CompilerParams(
            collective_id=collective, has_side_effects=True, vmem_limit_bytes=60 * 2**20
        ),
        name="moe_%d%d" % (ahead, back),
    )(*operands)


def pieces_of(experts, rows):
    return 4 if rows % (64 * experts) == 0 else 3


def merge_kernel(
    experts, main0, main1, small0, small1, out0, out1, grad0, grad1, wins, wouts,
    total, total_small, land_in, land_out, grad_in, grad_out, section_out, section_grad,
    own, mate, land1, land2, acc, own_s, mate_s, land1_s, land2_s,
    load_sems, mate_send, mate_recv, mate_recv_s, wide_send, wide_recv, hand_load,
    send_sems, send_s_sems, rs1, rs1_s, rs2, rs2_s, ag2, ag2_s, ag1, ag1_s,
    fold_in, fold_out, fold_loads, fold_stores,
):
    per = experts // PLANES
    me = lax.axis_index("expert")
    section = lax.axis_index("section")
    plane, spot = me // per, me % per
    rows, rows_s = own.shape[0], own_s.shape[0]
    pieces = pieces_of(experts, rows)
    size = rows // pieces
    step_rows = 48 if size % (48 * experts) == 0 else 16
    partner = {"section": 1 - section}

    barrier = pltpu.get_barrier_semaphore()

    def greet(target):
        pl.semaphore_signal(barrier, inc=1, device_id=target, device_id_type=MESH)

    greet(partner)

    def greet_plane(step, carry):
        greet({"expert": plane * per + (spot + step) % per})
        return carry

    def greet_column(step, carry):
        greet({"expert": ((plane + step) % PLANES) * per + spot})
        return carry

    lax.fori_loop(1, per, greet_plane, 0)
    lax.fori_loop(1, PLANES, greet_column, 0)
    pl.semaphore_wait(barrier, per + PLANES - 1)

    def remote(source, target, send, recv, where):
        pltpu.make_async_remote_copy(
            src_ref=source, dst_ref=target, send_sem=send, recv_sem=recv,
            device_id=where, device_id_type=MESH,
        ).start()

    def wait(part, sem):
        pltpu.make_async_copy(part, part, sem).wait()

    def at(start, size):
        return pl.ds(pl.multiple_of(start, 16), size)

    in_plane = lambda j: plane * per + j
    in_column = lambda j: j * per + spot
    by_plane = (per, spot, in_plane, PLANES, plane, in_column)
    by_column = (PLANES, plane, in_column, per, spot, in_plane)
    parts = [(p, p * size) + (by_column if p == 1 else by_plane) for p in range(pieces)]
    lows = [0]
    for part in parts:
        lows.append(lows[-1] + size // part[2])

    def begin(own_main, own_small, own_hand, other_main, other_small, other_hand):
        pltpu.make_async_copy(own_main, own, load_sems.at[0]).start()
        pltpu.make_async_copy(own_small, own_s, load_sems.at[1]).start()
        remote(other_small, mate_s, mate_send.at[1], mate_recv_s.at[0], partner)
        for p, base, n1, i1, _, _, _, _ in parts:
            block = size // n1

            def hand(step, carry):
                j = (i1 + step) % n1
                part = at(base + j * block, block)
                remote(other_main.at[part], mate.at[part], mate_send.at[0],
                       mate_recv.at[p, j], partner)
                return carry

            lax.fori_loop(1, n1 + 1, hand, 0)
        for lane, target in enumerate((section_out, section_grad)):
            mine = target.at[section]
            pltpu.make_async_copy(own_hand[lane], mine, hand_load.at[lane]).start()
            remote(
                other_hand[lane], mine, wide_send.at[2 + lane], wide_recv.at[2 + lane], partner
            )

    first = (main0, small0, (out0, grad0))
    second = (main1, small1, (out1, grad1))
    pl.when(section == 0)(lambda: begin(*first, *second))
    pl.when(section == 1)(lambda: begin(*second, *first))
    remote(wins.at[1 - section], land_in, wide_send.at[0], wide_recv.at[0], partner)
    remote(wouts.at[1 - section], land_out, wide_send.at[1], wide_recv.at[1], partner)
    wait(own, load_sems.at[0])
    wait(own_s, load_sems.at[1])
    wait(mate_s, mate_recv_s.at[0])
    own_s[...] += mate_s[...]

    def stage1(part):
        p, base, n1, i1, peer1, _, _, _ = part
        block, block_s = size // n1, rows_s // n1

        def out1(step, carry):
            j = (i1 + step) % n1
            wait(mate.at[at(base + j * block, block)], mate_recv.at[p, j])

            def fold(step, carry):
                part = at(base + j * block + step * step_rows, step_rows)
                own[part] = (own[part].astype(F32) + mate[part].astype(F32)).astype(BF)
                return carry

            lax.fori_loop(0, block // step_rows, fold, 0)
            where = {"expert": peer1(j)}
            remote(own.at[at(base + j * block, block)], land1.at[at(base + i1 * block, block)],
                   send_sems.at[p, 0], rs1.at[p, i1], where)
            if p == 0:
                remote(own_s.at[at(j * block_s, block_s)], land1_s.at[at(i1 * block_s, block_s)],
                       send_s_sems.at[0], rs1_s.at[i1], where)
            return carry

        lax.fori_loop(1, n1, out1, 0)

    def stage2(part):
        p, base, n1, i1, _, n2, i2, peer2 = part
        block, block_s = size // n1, rows_s // n1
        sub, sub_s = size // (n1 * n2), rows_s // (n1 * n2)
        low = lows[p]
        wait(mate.at[at(base + i1 * block, block)], mate_recv.at[p, i1])

        def in1(step, carry):
            j = (i1 + step) % n1
            wait(land1.at[at(base + j * block, block)], rs1.at[p, j])
            if p == 0:
                wait(land1_s.at[at(j * block_s, block_s)], rs1_s.at[j])
            return carry

        lax.fori_loop(1, n1, in1, 0)

        def sum1(k):
            def one(step, carry):
                place = k * sub + step * step_rows
                part = at(base + i1 * block + place, step_rows)
                value = own[part].astype(F32) + mate[part].astype(F32)

                def add(other, value):
                    far = at(base + ((i1 + other) % n1) * block + place, step_rows)
                    return value + land1[far].astype(F32)

                value = lax.fori_loop(1, n1, add, value)
                own[part] = value.astype(BF)
                acc[at(low + place, step_rows)] = value
                return carry

            lax.fori_loop(0, sub // step_rows, one, 0)
            if p == 0:
                part = at(i1 * block_s + k * sub_s, sub_s)

                def add_s(other, value):
                    far = at(((i1 + other) % n1) * block_s + k * sub_s, sub_s)
                    return value + land1_s[far]

                own_s[part] = lax.fori_loop(1, n1, add_s, own_s[part])

        def out2(step, carry):
            k = (i2 + step) % n2
            sum1(k)
            where = {"expert": peer2(k)}
            remote(own.at[at(base + i1 * block + k * sub, sub)],
                   land2.at[at(low + i2 * sub, sub)], send_sems.at[p, 1], rs2.at[p, i2], where)
            if p == 0:
                remote(own_s.at[at(i1 * block_s + k * sub_s, sub_s)],
                       land2_s.at[at(i2 * sub_s, sub_s)], send_s_sems.at[1], rs2_s.at[i2], where)
            return carry

        lax.fori_loop(1, n2, out2, 0)
        sum1(i2)

    def stage3(part):
        p, base, n1, i1, _, n2, i2, peer2 = part
        block, block_s = size // n1, rows_s // n1
        sub, sub_s = size // (n1 * n2), rows_s // (n1 * n2)
        low = lows[p]

        def in2(step, carry):
            k = (i2 + step) % n2
            wait(land2.at[at(low + k * sub, sub)], rs2.at[p, k])
            if p == 0:
                wait(land2_s.at[at(k * sub_s, sub_s)], rs2_s.at[k])
            return carry

        lax.fori_loop(1, n2, in2, 0)

        def sum2(step, carry):
            place = step * step_rows
            value = acc[at(low + i2 * sub + place, step_rows)]

            def add(other, value):
                far = at(low + ((i2 + other) % n2) * sub + place, step_rows)
                return value + land2[far].astype(F32)

            value = lax.fori_loop(1, n2, add, value)
            total[at(base + i1 * block + i2 * sub + place, step_rows)] = value.astype(BF)
            return carry

        lax.fori_loop(0, sub // step_rows, sum2, 0)
        home = at(base + i1 * block + i2 * sub, sub)
        home_s = at(i1 * block_s + i2 * sub_s, sub_s)
        if p == 0:

            def add2_s(other, value):
                return value + land2_s[at(((i2 + other) % n2) * sub_s, sub_s)]

            total_small[home_s] = lax.fori_loop(1, n2, add2_s, own_s[home_s])

        def share2(step, carry):
            where = {"expert": peer2((i2 + step) % n2)}
            remote(total.at[home], total.at[home], send_sems.at[p, 2], ag2.at[p, i2], where)
            if p == 0:
                remote(total_small.at[home_s], total_small.at[home_s], send_s_sems.at[2],
                       ag2_s.at[i2], where)
            return carry

        lax.fori_loop(1, n2, share2, 0)

    def stage4(part):
        p, base, n1, i1, peer1, n2, i2, _ = part
        block, block_s = size // n1, rows_s // n1
        sub, sub_s = size // (n1 * n2), rows_s // (n1 * n2)

        def share1(step, carry):
            k = (i2 + step) % n2
            home = at(base + i1 * block + k * sub, sub)
            home_s = at(i1 * block_s + k * sub_s, sub_s)

            @pl.when(step > 0)
            def _():
                wait(total.at[home], ag2.at[p, k])
                if p == 0:
                    wait(total_small.at[home_s], ag2_s.at[k])

            def one(jump, carry):
                where = {"expert": peer1((i1 + jump) % n1)}
                remote(total.at[home], total.at[home], send_sems.at[p, 3], ag1.at[p, i1], where)
                if p == 0:
                    remote(total_small.at[home_s], total_small.at[home_s], send_s_sems.at[3],
                           ag1_s.at[i1], where)
                return carry

            lax.fori_loop(1, n1, one, 0)
            return carry

        lax.fori_loop(0, n2, share1, 0)

    def add_terms(which):
        terms, landed, result, fold = (
            (wins, land_in, grad_in, fold_in), (wouts, land_out, grad_out, fold_out)
        )[which]
        wait(landed, wide_recv.at[which])
        height = fold.shape[2]
        steps = landed.shape[0] // height

        def fetch(step):
            slot = step % 2
            part = at(step * height, height)
            pltpu.make_async_copy(
                terms.at[section, part], fold.at[0, slot], fold_loads.at[0, slot]
            ).start()
            pltpu.make_async_copy(
                landed.at[part], fold.at[1, slot], fold_loads.at[1, slot]
            ).start()

        fetch(0)

        def one(step, carry):
            slot = step % 2
            pl.when(step + 1 < steps)(lambda: fetch(step + 1))
            for side in range(2):
                wait(fold.at[side, slot], fold_loads.at[side, slot])
            pl.when(step >= 2)(lambda: wait(fold.at[2, slot], fold_stores.at[slot]))
            fold[2, slot] = (fold[0, slot].astype(F32) + fold[1, slot].astype(F32)).astype(BF)
            pltpu.make_async_copy(
                fold.at[2, slot], result.at[at(step * height, height)], fold_stores.at[slot]
            ).start()
            return carry

        lax.fori_loop(0, steps, one, 0)
        for slot in range(2):
            wait(fold.at[2, slot], fold_stores.at[slot])

    order = [(1, 0), (1, 1), (1, 2), (2, 0), (1, 3), (5, 0), (2, 1), (2, 2), (3, 0), (2, 3),
             (3, 1), (3, 2), (4, 0), (3, 3), (5, 1), (4, 1), (4, 2), (4, 3)]
    stages = (None, stage1, stage2, stage3, stage4)
    for stage, p in order:
        if stage == 5:
            add_terms(p)
        elif p < pieces:
            stages[stage](parts[p])
    for p, base, n1, i1, _, n2, _, _ in parts:
        block, block_s = size // n1, rows_s // n1
        sub, sub_s = size // (n1 * n2), rows_s // (n1 * n2)

        def in_last(step, carry):
            j = (i1 + step) % n1
            wait(total.at[at(base + j * block, block)], ag1.at[p, j])
            if p == 0:
                wait(total_small.at[at(j * block_s, block_s)], ag1_s.at[j])
            return carry

        lax.fori_loop(1, n1, in_last, 0)
        for lane, count, count_s in (
            (0, (n1 - 1) * block, (n1 - 1) * block_s),
            (1, (n2 - 1) * sub, (n2 - 1) * sub_s),
            (2, (n2 - 1) * sub, (n2 - 1) * sub_s),
            (3, (n1 - 1) * block, (n1 - 1) * block_s),
        ):
            wait(own.at[pl.ds(0, count)], send_sems.at[p, lane])
            if p == 0:
                wait(own_s.at[pl.ds(0, count_s)], send_s_sems.at[lane])
    wait(mate, mate_send.at[0])
    wait(mate_s, mate_send.at[1])
    wait(land_in, wide_send.at[0])
    wait(land_out, wide_send.at[1])
    for lane, target in enumerate((section_out, section_grad)):
        wait(target.at[section], hand_load.at[lane])
        wait(target.at[section], wide_send.at[2 + lane])
        wait(target.at[1 - section], wide_recv.at[2 + lane])


def merge(experts, mains, smalls, outs, grads, wins, wouts):
    rows, width = mains[0].shape
    rows_s = smalls[0].shape[0]
    per = experts // PLANES
    most, least = max(per, PLANES), min(per, PLANES)
    pieces = pieces_of(experts, rows)
    seconds = (pieces - 1) * (rows // pieces // per) + rows // pieces // PLANES
    vmem = pl.BlockSpec(memory_space=pltpu.VMEM)
    hbm = pl.BlockSpec(memory_space=pl.ANY)
    sems = lambda *shape: pltpu.SemaphoreType.DMA(shape)
    return pl.pallas_call(
        functools.partial(merge_kernel, experts),
        out_shape=[
            jax.ShapeDtypeStruct((rows, width), BF),
            jax.ShapeDtypeStruct((rows_s, 128), F32),
            jax.ShapeDtypeStruct(wins.shape[1:], BF),
            jax.ShapeDtypeStruct(wouts.shape[1:], BF),
            jax.ShapeDtypeStruct(wins.shape[1:], BF),
            jax.ShapeDtypeStruct(wouts.shape[1:], BF),
            jax.ShapeDtypeStruct((2, *outs[0].shape), BF),
            jax.ShapeDtypeStruct((2, *grads[0].shape), F32),
        ],
        in_specs=[hbm] * 10,
        out_specs=[vmem, vmem, hbm, hbm, hbm, hbm, hbm, hbm],
        scratch_shapes=[
            pltpu.VMEM((rows, width), BF),
            pltpu.VMEM((rows, width), BF),
            pltpu.VMEM((rows, width), BF),
            pltpu.VMEM((seconds, width), BF),
            pltpu.VMEM((seconds, width), F32),
            pltpu.VMEM((rows_s, 128), F32),
            pltpu.VMEM((rows_s, 128), F32),
            pltpu.VMEM((rows_s, 128), F32),
            pltpu.VMEM((rows_s // per, 128), F32),
            sems(2), sems(2), sems(pieces, most), sems(1), sems(4), sems(4), sems(2),
            sems(pieces, 4), sems(4), sems(pieces, most), sems(most), sems(pieces, most), sems(most),
            sems(pieces, most), sems(most), sems(pieces, most), sems(most),
            pltpu.VMEM((3, 2, wins.shape[1] // 8, wins.shape[2]), BF),
            pltpu.VMEM((3, 2, wouts.shape[1] // 8, wouts.shape[2]), BF),
            sems(2, 2), sems(2),
        ],
        compiler_params=pltpu.CompilerParams(
            collective_id=3, has_side_effects=True, vmem_limit_bytes=60 * 2**20
        ),
        name="merge",
    )(*mains, *smalls, *outs, *grads, wins, wouts)


def finish_kernel(q_ref, k_ref, v_ref, p_ref, gqkv_ref, gproj_ref):
    width = gproj_ref.shape[1]
    for at, part in enumerate((q_ref, k_ref, v_ref)):
        gqkv_ref[:, at * width : (at + 1) * width] = part[...].astype(F32)
    gproj_ref[...] = p_ref[...].astype(F32)


def finish(total):
    width = total.shape[1]
    steps = 6
    low = width // steps
    return pl.pallas_call(
        finish_kernel,
        grid=(steps,),
        in_specs=[
            pl.BlockSpec((low, width), functools.partial(lambda k, i: (k * steps + i, 0), k))
            for k in range(4)
        ],
        out_specs=[
            pl.BlockSpec((low, 3 * width), lambda i: (i, 0)),
            pl.BlockSpec((low, width), lambda i: (i, 0)),
        ],
        out_shape=[
            jax.ShapeDtypeStruct((width, 3 * width), F32),
            jax.ShapeDtypeStruct((width, width), F32),
        ],
        compiler_params=pltpu.CompilerParams(vmem_limit_bytes=56 * 2**20),
        name="finish",
    )(*[total] * 4)


def shards(
    block_input, cotangent, expert_ids, qkv_weight, query_bias, value_bias, proj_weight,
    proj_bias, attn_gain, ffn_gain, router_weight, in_weight, out_weight,
):
    section = lax.axis_index("section")
    width = block_input.shape[2]
    experts = router_weight.shape[2]
    tokens = block_input.shape[1]
    capacity = capacity_of(tokens, expert_ids.shape[3], experts)
    extra = capacity % 16

    def swapped(array):
        return lax.ppermute(array, "section", SWAP)

    vectors = jnp.concatenate([query_bias, value_bias, proj_bias, attn_gain, ffn_gain])
    own_shared = (qkv_weight[0], proj_weight[0])
    other_shared = tuple(swapped(part) for part in own_shared)
    vectors_other, router_other = swapped(vectors), swapped(router_weight[0])
    own_experts = (in_weight[0, 0], out_weight[0, 0])
    main = capacity - extra
    ids = lax.dynamic_index_in_dim(expert_ids, section, 1, keepdims=False)
    layers = []
    for l in range(2):
        vector = jnp.where(section == l, vectors, vectors_other)
        router = jnp.where(section == l, router_weight[0], router_other)
        router = jnp.pad(router, ((0, 0), (0, 128 - experts)))
        layers.append(
            (own_shared, other_shared, router, vector, *places_of(ids[l], experts, capacity))
        )
    rows = lax.dynamic_index_in_dim(block_input, section, 0, keepdims=False)
    seed = lax.dynamic_index_in_dim(cotangent, section, 0, keepdims=False)

    *inner0, middle0, routed0, gates0, rows0, rows_x0 = attend(
        0, extra, experts, main, layers[0], current=rows
    )
    done0 = moe(
        True, False, 0, extra, 0, (rows0, rows_x0), None, None, own_experts, ()
    )
    other_experts = done0[4:]
    *inner1, middle1, routed1, gates1, rows1, rows_x1, out0, apart0, grads1, grads_x1 = attend(
        1, extra, experts, main, layers[1],
        chain=(middle0, gates0, layers[0][4], *done0[:2], seed),
    )
    done1 = moe(
        True, True, 1, extra, 1, (rows1, rows_x1), (grads1, grads_x1), None, own_experts,
        other_experts,
    )
    seed0, main1, sums1, grad_router1, out1, grads0, grads_x0 = attend_back(
        1, extra, experts, main, layers[1], (out0, *inner1, middle1, routed1, gates1), seed,
        done1[2:4], (*done1[:2], gates0, layers[0][5]), True,
    )
    back0 = moe(
        False, True, 2, extra, 0, None, (grads0, grads_x0), done0[2:4], own_experts,
        other_experts, done1[4:],
    )
    grad0, main0, sums0, grad_router0 = attend_back(
        0, extra, experts, main, layers[0], (rows, *inner0, middle0, routed0, gates0), seed0,
        back0[:2], (apart0,), False,
    )

    def smalls(sums, grad_router):
        small = jnp.concatenate([sums, grad_router]).reshape(-1, 128)
        return jnp.pad(small, ((0, -small.shape[0] % (16 * experts)), (0, 0)))

    small0, small1 = smalls(sums0, grad_router0), smalls(sums1, grad_router1)
    total, small, _, _, grad_win, grad_wout, section_out, section_grad = merge(
        experts, (main0, main1), (small0, small1), (out0, out1), (grad0, seed0), back0[2],
        back0[3],
    )
    grad_qkv, grad_proj = finish(total)
    small = small[: (5 + experts) * width // 128].reshape(5 + experts, width)
    return (
        section_out[None],
        section_grad[None],
        grad_qkv[None],
        small[0][None],
        small[1][None],
        grad_proj[None],
        small[2][None],
        small[3][None],
        small[4][None],
        small[5:].T[None],
        grad_win[None, None],
        grad_wout[None, None],
    )


def solution(mesh):
    vector, matrix = P("section", None), P("section", None, None)
    expert = P("section", "expert", None, None)
    rows = P("section", None, "expert", None)
    return jax.shard_map(
        shards,
        mesh=mesh,
        in_specs=(
            P(None, "expert", None),
            P(None, "expert", None),
            P(None, None, "expert", None),
            matrix, vector, vector, matrix, vector, vector, vector, matrix, expert, expert,
        ),
        out_specs=(
            rows, rows, matrix, vector, vector, matrix, vector, vector, vector, matrix,
            expert, expert,
        ),
        check_vma=False,
    )
```

```python
import functools

import jax
import jax.numpy as jnp
from jax import lax
from jax.experimental import pallas as pl
from jax.experimental.pallas import tpu as pltpu
from jax.sharding import PartitionSpec as P

HD = 64
EPS = 1e-06
NEG = -1e30
BF = jnp.bfloat16
F32 = jnp.float32
HIGH = lax.Precision.HIGHEST
SWAP = [(0, 1), (1, 0)]
MESH = pl.DeviceIdType.MESH
NN = ((1,), (0,))
NT = ((1,), (1,))
TN = ((0,), (0,))
PLANES = 4
CHUNK = 512


def dot(a, b, dims, kind=F32, precision=None):
    return lax.dot_general(
        a, b, (dims, ((), ())), precision=precision, preferred_element_type=F32
    ).astype(kind)


def capacity_of(tokens, choices, experts):
    return tokens * choices // experts + max(1, tokens * choices // (16 * experts))


def inverse_rms(field):
    return lax.rsqrt(jnp.mean(field * field, axis=-1, keepdims=True) + EPS)


def places_of(route_ids, experts, capacity):
    tokens = route_ids.shape[0]
    main = capacity // 16 * 16
    lanes = jnp.arange(experts, dtype=jnp.int32)[None, :]
    hots = [(route_ids[:, j : j + 1] == lanes).astype(F32) for j in range(2)]
    spots = jnp.arange(tokens, dtype=jnp.int32)
    earlier = (spots[:, None] > spots[None, :]).astype(BF)
    counts = dot(earlier, (hots[0] + hots[1]).astype(BF), NN)
    slots, slots_x = [], []
    for j, hot in enumerate(hots):
        rank = jnp.sum(counts * hot, axis=-1).astype(jnp.int32)
        slots.append(jnp.where(rank < main, route_ids[:, j] * main + rank, -1))
        slots_x.append(
            jnp.where(rank < main, -experts * 16, route_ids[:, j] * 16 + rank - main)
        )
    table = jnp.stack(slots + slots_x + [route_ids[:, 0], route_ids[:, 1]] * 2, axis=1)
    return table, table.T


def pack_into(main_ref, small_ref, across, extra, values):
    experts, main, width = main_ref.shape
    tokens = across.shape[1]
    tall = 256
    each = tall // main

    def hot(rows, slot):
        return (rows == across[slot : slot + 1]).astype(BF)

    def one(step, carry):
        rows = lax.broadcasted_iota(jnp.int32, (tall, tokens), 0) + step * tall
        if len(values) == 1:
            total = dot(hot(rows, 0) + hot(rows, 1), values[0], NN)
        else:
            total = dot(hot(rows, 0), values[0], NN) + dot(hot(rows, 1), values[1], NN)
        main_ref[pl.ds(step * each, each)] = total.astype(BF).reshape(each, main, width)
        return carry

    lax.fori_loop(0, experts * main // tall, one, 0, unroll=2)

    def one_x(step, carry):
        rows = lax.broadcasted_iota(jnp.int32, (tall, tokens), 0) + step * tall
        total = 0.0
        for q in range(width // 256):
            span = slice(q * 256, (q + 1) * 256)
            hots = [hot(rows - q * extra, 2), hot(rows - q * extra, 3)]
            if len(values) == 1:
                total += dot(hots[0] + hots[1], values[0][:, span], NN)
            else:
                total += dot(hots[0], values[0][:, span], NN)
                total += dot(hots[1], values[1][:, span], NN)
        small_ref[pl.ds(step * (tall // 16), tall // 16)] = total.astype(BF).reshape(
            tall // 16, 16, 256
        )
        return carry

    lax.fori_loop(0, experts * 16 // tall, one_x, 0)


def unpack_from(main_ref, small_ref, down, extra, slots):
    experts, main, width = main_ref.shape
    tokens = down.shape[0]
    lanes = lax.broadcasted_iota(jnp.int32, (tokens, experts * main), 1)
    hot = sum((lanes == down[:, j : j + 1]).astype(BF) for j in slots)
    total = dot(hot, main_ref[...].reshape(experts * main, width), NN)
    lanes = lax.broadcasted_iota(jnp.int32, (tokens, experts * 16), 1)
    small = small_ref[...].reshape(experts * 16, 256)
    tail = [
        dot(sum((lanes - q * extra == down[:, 2 + j : 3 + j]).astype(BF) for j in slots), small, NN)
        for q in range(width // 256)
    ]
    return total + jnp.concatenate(tail, axis=1)


def signs_down(down):
    lanes = lax.broadcasted_iota(jnp.int32, (down.shape[0], 128), 1)
    return (lanes == down[:, 4:5]).astype(F32) - (lanes == down[:, 5:6]).astype(F32)


def causal_weights(scores, place, block):
    length = scores.shape[0]
    keys = lax.broadcasted_iota(jnp.int32, scores.shape, 0)
    queries = lax.broadcasted_iota(jnp.int32, scores.shape, 1) + place * block
    return jnp.where(keys <= queries, scores * HD ** (-0.5), NEG)


def load_shared(layer, own, other, qkv_ref, proj_ref, sems):
    section = lax.axis_index("section")

    def load(pair):
        pltpu.make_async_copy(pair[0], qkv_ref, sems.at[0]).start()
        pltpu.make_async_copy(pair[1], proj_ref, sems.at[1]).start()

    pl.when(section == layer)(lambda: load(own))
    pl.when(section != layer)(lambda: load(other))
    return [
        pltpu.make_async_copy(ref, ref, sems.at[at]) for at, ref in enumerate((qkv_ref, proj_ref))
    ]


def attend_kernel(layer, extra, chained, *refs):
    refs = list(refs)

    def take(count):
        taken, refs[:count] = refs[:count], []
        return taken

    own_qkv, own_proj, other_qkv, other_proj = take(4)
    vectors_ref, router_ref, down_ref, across_ref = take(4)
    if chained:
        before_ref, before_gates_ref, before_down_ref, back_ref, back_x_ref, seed_ref = take(6)
    else:
        (current_ref,) = take(1)
    normed_ref, queries_ref, keys_ref, values_ref, log_ref, attended_ref = take(6)
    middle_ref, routed_ref, gates_ref, rows_ref, rows_x_ref = take(5)
    if chained:
        current_ref, apart_ref, grads_ref, grads_x_ref = take(4)
    qkv_ref, proj_ref, sems = take(3)
    loads = load_shared(
        layer, (own_qkv, own_proj), (other_qkv, other_proj), qkv_ref, proj_ref, sems
    )
    if chained:
        down = before_down_ref[...]
        gates = before_gates_ref[...]
        one = unpack_from(back_ref, back_x_ref, down, extra, (0,))
        two = unpack_from(back_ref, back_x_ref, down, extra, (1,))
        apart_ref[...] = one - two
        current_ref[...] = (
            before_ref[...] + (gates[:, 0:1] * one + gates[:, 1:2] * two)
        ).astype(BF)
    tokens, width = normed_ref.shape
    block = tokens // 2
    qbias, vbias, pbias, gain_attn, gain_ffn = (vectors_ref[l : l + 1] for l in range(5))
    current = current_ref[...].astype(F32)
    normed = (current * inverse_rms(current) * gain_attn).astype(BF)
    normed_ref[...] = normed
    loads[0].wait()
    for at in range(0, width, 256):
        span = slice(at, at + 256)
        queries_ref[:, span] = (dot(normed, qkv_ref[:, span], NN) + qbias[:, span]).astype(BF)
        keys_ref[:, span] = dot(normed, qkv_ref[:, width + at : width + at + 256], NN, BF)
        values_ref[:, span] = (
            dot(normed, qkv_ref[:, 2 * width + at : 2 * width + at + 256], NN) + vbias[:, span]
        ).astype(BF)
    lane = lax.broadcasted_iota(jnp.int32, (1, 2 * HD), 1)

    def pair(step, carry):
        span = pl.ds(pl.multiple_of(step * 2 * HD, 2 * HD), 2 * HD)
        for place in range(2):
            rows = slice(place * block, (place + 1) * block)
            reach = slice(0, (place + 1) * block)
            total = jnp.zeros((block, 2 * HD), F32)
            for side in range(2):
                mine = (lane // HD) == side
                queries = jnp.where(mine, queries_ref[rows, span], 0.0).astype(BF)
                scores = causal_weights(dot(keys_ref[reach, span], queries, NT), place, block)
                top = jnp.max(scores, axis=0, keepdims=True)
                weights = jnp.exp(scores - top)
                amount = jnp.sum(weights, axis=0, keepdims=True)
                log_ref[step, side : side + 1, rows] = top + jnp.log(amount)
                probs = (weights * (1.0 / amount)).astype(BF)
                values = jnp.where(mine, values_ref[reach, span], 0.0).astype(BF)
                total += dot(probs, values, TN)
            attended_ref[rows, span] = total.astype(BF)
        return carry

    lax.fori_loop(0, width // (2 * HD), pair, 0, unroll=2)
    loads[1].wait()
    middle = current_ref[...].astype(F32) + (dot(attended_ref[...], proj_ref[...], NN) + pbias)
    middle_ref[...] = middle
    routed = (middle * inverse_rms(middle) * gain_ffn).astype(BF)
    routed_ref[...] = routed
    logits = dot(routed, router_ref[...], NN)
    gap = jnp.sum(logits * signs_down(down_ref[...]), axis=-1, keepdims=True)
    gate0, gate1 = jax.nn.sigmoid(gap), jax.nn.sigmoid(-gap)
    gates_ref[:, 0:1] = gate0
    gates_ref[:, 1:2] = gate1
    across = across_ref[...]
    pack_into(rows_ref, rows_x_ref, across, extra, [routed])
    if chained:
        seed = seed_ref[...].astype(F32)
        pack_into(
            grads_ref, grads_x_ref, across, extra,
            [(gate0 * seed).astype(BF), (gate1 * seed).astype(BF)],
        )


def shared_scratch(width):
    return [
        pltpu.VMEM((width, 3 * width), BF),
        pltpu.VMEM((width, width), BF),
        pltpu.SemaphoreType.DMA((2,)),
    ]


def attend(layer, extra, experts, main, weights, current=None, chain=None):
    own, other, router, vectors, down, across = weights
    tokens, width = (current if chain is None else chain[0]).shape
    low = jax.ShapeDtypeStruct((tokens, width), BF)
    wide = jax.ShapeDtypeStruct((tokens, width), F32)
    rows = [
        jax.ShapeDtypeStruct((experts, main, width), BF),
        jax.ShapeDtypeStruct((experts, 16, 256), BF),
    ]
    out_shape = [low, low, low, low]
    out_shape += [jax.ShapeDtypeStruct((width // (2 * HD), 2, tokens), F32), low, wide, low]
    out_shape += [jax.ShapeDtypeStruct((tokens, 2), F32), *rows]
    if chain is not None:
        out_shape += [low, wide, *rows]
    vmem = pl.BlockSpec(memory_space=pltpu.VMEM)
    hbm = pl.BlockSpec(memory_space=pl.ANY)
    operands = (current,) if chain is None else chain
    return pl.pallas_call(
        functools.partial(attend_kernel, layer, extra, chain is not None),
        out_shape=out_shape,
        in_specs=[hbm] * 4 + [vmem] * (4 + len(operands)),
        out_specs=[vmem] * len(out_shape),
        scratch_shapes=shared_scratch(width),
        compiler_params=pltpu.CompilerParams(vmem_limit_bytes=58 * 2**20),
        cost_estimate=pl.CostEstimate(
            flops=8 * tokens * width * width + 4 * tokens * tokens * width * 4,
            bytes_accessed=16 * 2**20, transcendentals=12 * tokens * tokens,
        ),
        name="attend",
    )(*own, *other, vectors, router, down, across, *operands)


def attend_back_kernel(layer, extra, last, *refs):
    refs = list(refs)

    def take(count):
        taken, refs[:count] = refs[:count], []
        return taken

    own_qkv, own_proj, other_qkv, other_proj = take(4)
    vectors_ref, router_ref, down_ref, across_ref = take(4)
    current_ref, normed_ref, queries_ref, keys_ref, values_ref, log_ref, attended_ref = take(7)
    middle_ref, routed_ref, gates_ref, seed_ref, back_ref, back_x_ref = take(6)
    if last:
        made_ref, made_x_ref, before_gates_ref, before_across_ref = take(4)
    else:
        (apart_ref,) = take(1)
    grad_current_ref, main_ref, sums_ref, grad_router_ref = take(4)
    if last:
        out_ref, grads_ref, grads_x_ref = take(3)
    grad_attended, grad_queries, grad_keys, grad_values, grad_middle_ref = take(5)
    total_keys, total_values, qkv_ref, proj_ref, sems = take(5)
    loads = load_shared(
        layer, (own_qkv, own_proj), (other_qkv, other_proj), qkv_ref, proj_ref, sems
    )
    tokens, width = normed_ref.shape
    block = tokens // 2
    down = down_ref[...]
    gate0, gate1 = gates_ref[:, 0:1], gates_ref[:, 1:2]
    middle = middle_ref[...]
    seed = seed_ref[...].astype(F32)
    if last:
        one = unpack_from(made_ref, made_x_ref, down, extra, (0,))
        two = unpack_from(made_ref, made_x_ref, down, extra, (1,))
        out_ref[...] = (middle + (gate0 * one + gate1 * two)).astype(BF)
        apart = one - two
    else:
        apart = apart_ref[...]
    gap = gate0 * gate1 * jnp.sum(seed * apart, axis=-1, keepdims=True)
    terms = gap * routed_ref[...].astype(F32)
    high = terms.astype(BF)
    rest = (terms - high.astype(F32)).astype(BF)
    across = across_ref[...]
    rows = lax.broadcasted_iota(jnp.int32, (grad_router_ref.shape[0], tokens), 0)
    signs = (
        (rows == across[4:5]).astype(F32) - (rows == across[5:6]).astype(F32)
    ).astype(BF)
    grad_router_ref[...] = dot(signs, high, NN) + dot(signs, rest, NN)
    grad_routed = unpack_from(back_ref, back_x_ref, down, extra, (0, 1)) + gap * dot(
        signs_down(down).astype(BF), router_ref[...], NT
    )
    scale = inverse_rms(middle)
    unit = middle * scale
    sums_ref[4:5] = jnp.sum(grad_routed * unit, axis=0, keepdims=True)
    scaled = grad_routed * vectors_ref[4:5]
    grad_middle_ref[...] = seed + scale * (
        scaled - unit * jnp.mean(scaled * unit, axis=-1, keepdims=True)
    )
    grad_branch = grad_middle_ref[...].astype(BF)
    sums_ref[2:3] = jnp.sum(grad_branch.astype(F32), axis=0, keepdims=True)
    loads[1].wait()
    grad_attended[...] = dot(grad_branch, proj_ref[...], NT, BF)
    for at in range(0, width, 256):
        span = slice(at, at + 256)
        main_ref[3 * width : 4 * width, span] = dot(
            attended_ref[...], grad_middle_ref[:, span].astype(BF), TN, BF
        )
    lane = lax.broadcasted_iota(jnp.int32, (1, 2 * HD), 1)

    def pair(step, carry):
        span = pl.ds(pl.multiple_of(step * 2 * HD, 2 * HD), 2 * HD)
        for place in range(2):
            rows = slice(place * block, (place + 1) * block)
            reach = slice(0, (place + 1) * block)
            total = jnp.zeros((block, 2 * HD), F32)
            term_keys = term_values = 0.0
            for side in range(2):
                mine = (lane // HD) == side
                queries = jnp.where(mine, queries_ref[rows, span], 0.0).astype(BF)
                grads = jnp.where(mine, grad_attended[rows, span], 0.0).astype(BF)
                scores = causal_weights(dot(keys_ref[reach, span], queries, NT), place, block)
                weights = jnp.exp(scores - log_ref[step, side : side + 1, rows])
                grad_probs = dot(values_ref[reach, span], grads, NT)
                inner = jnp.sum(weights * grad_probs, axis=0, keepdims=True)
                grad_scores = (weights * (grad_probs - inner)).astype(BF)
                keys = jnp.where(mine, keys_ref[reach, span], 0.0).astype(BF)
                total += dot(grad_scores, keys, TN)
                term_values += dot(weights.astype(BF), grads, NN)
                term_keys += dot(grad_scores, queries, NN)
            grad_queries[rows, span] = (total * HD ** (-0.5)).astype(BF)
            if place == 0:
                total_keys[...] = term_keys
                total_values[...] = term_values
            else:
                term_keys = jnp.concatenate(
                    [term_keys[:block] + total_keys[...], term_keys[block:]]
                )
                term_values = jnp.concatenate(
                    [term_values[:block] + total_values[...], term_values[block:]]
                )
                grad_keys[:, span] = (term_keys * HD ** (-0.5)).astype(BF)
                grad_values[:, span] = term_values.astype(BF)
        return carry

    lax.fori_loop(0, width // (2 * HD), pair, 0, unroll=2)
    sums_ref[0:1] = jnp.sum(grad_queries[...].astype(F32), axis=0, keepdims=True)
    sums_ref[1:2] = jnp.sum(grad_values[...].astype(F32), axis=0, keepdims=True)
    loads[0].wait()
    grad_normed = jnp.zeros((tokens, width), F32)
    for which, grads in enumerate((grad_queries, grad_keys, grad_values)):
        for at in range(0, width, 256):
            main_ref[which * width : (which + 1) * width, at : at + 256] = dot(
                normed_ref[...], grads[:, at : at + 256], TN, BF
            )
        grad_normed += dot(grads[...], qkv_ref[:, which * width : (which + 1) * width], NT)
    current = current_ref[...].astype(F32)
    scale = inverse_rms(current)
    unit = current * scale
    sums_ref[3:4] = jnp.sum(grad_normed * unit, axis=0, keepdims=True)
    scaled = grad_normed * vectors_ref[3:4]
    grad_current = grad_middle_ref[...] + scale * (
        scaled - unit * jnp.mean(scaled * unit, axis=-1, keepdims=True)
    )
    if last:
        grad_current = grad_current.astype(BF).astype(F32)
    grad_current_ref[...] = grad_current
    if last:
        before0, before1 = before_gates_ref[:, 0:1], before_gates_ref[:, 1:2]
        pack_into(
            grads_ref, grads_x_ref, before_across_ref[...], extra,
            [(before0 * grad_current).astype(BF), (before1 * grad_current).astype(BF)],
        )


def attend_back(layer, extra, experts, main, weights, kept, seed, back, rest, last):
    own, other, router, vectors, down, across = weights
    tokens, width = kept[0].shape
    wide = jax.ShapeDtypeStruct((tokens, width), F32)
    out_shape = [
        wide,
        jax.ShapeDtypeStruct((4 * width, width), BF),
        jax.ShapeDtypeStruct((5, width), F32),
        jax.ShapeDtypeStruct((experts, width), F32),
    ]
    if last:
        out_shape += [
            jax.ShapeDtypeStruct((tokens, width), BF),
            jax.ShapeDtypeStruct((experts, main, width), BF),
            jax.ShapeDtypeStruct((experts, 16, 256), BF),
        ]
    vmem = pl.BlockSpec(memory_space=pltpu.VMEM)
    hbm = pl.BlockSpec(memory_space=pl.ANY)
    operands = (*kept, seed, *back, *rest)
    return pl.pallas_call(
        functools.partial(attend_back_kernel, layer, extra, last),
        out_shape=out_shape,
        in_specs=[hbm] * 4 + [vmem] * (4 + len(operands)),
        out_specs=[vmem] * len(out_shape),
        scratch_shapes=[pltpu.VMEM((tokens, width), BF)] * 4
        + [pltpu.VMEM((tokens, width), F32)]
        + [pltpu.VMEM((tokens // 2, 2 * HD), F32)] * 2
        + shared_scratch(width),
        compiler_params=pltpu.CompilerParams(vmem_limit_bytes=58 * 2**20),
        cost_estimate=pl.CostEstimate(
            flops=16 * tokens * width * width + 10 * tokens * tokens * width * 4,
            bytes_accessed=24 * 2**20, transcendentals=12 * tokens * tokens,
        ),
        name="attend_back",
    )(*own, *other, vectors, router, down, across, *operands)


def gelu_and_slope(hidden):
    root = 0.7978845608028654
    square = hidden * hidden
    bent = jnp.tanh(hidden * (root + (root * 0.044715) * square))
    half = 0.5 + 0.5 * bent
    slope = half + (0.5 * hidden) * (1.0 - bent * bent) * (root + (root * 0.134145) * square)
    return hidden * half, slope


def moe_kernel(experts, extra, layer, ahead, back, *refs):
    refs = list(refs)

    def take(count):
        taken, refs[:count] = refs[:count], []
        return taken

    rows_in, grads_in, kept_in = [], [], []
    if ahead:
        rows_in = take(2)
    if back:
        grads_in = take(2)
    if back and not ahead:
        kept_in = take(2)
    own_weights = take(2)
    other_weights = take(2) if back else []
    if kept_in:
        take(2)
    produced_out = take(2) if ahead else []
    kept_out = take(2) if ahead and not back else []
    returned_out = take(2) if back else []
    gwin_out, gwout_out = take(2) if back else (None, None)
    if not back:
        other_weights = take(2)
    win, wout, weight_sem = take(3)
    if ahead:
        row_land, row_land_x, row_stage, row_stage_x, row_acc = take(5)
    if back:
        grad_land, grad_land_x, grad_stage, grad_stage_x, grad_acc, gwin, gwout = take(7)
        fold, fold_sem = take(2)
    send_sems, recv_sems, send_x_sems, recv_x_sems = take(4)
    takes_turns = ahead and not back
    if takes_turns:
        turn, push_send, push_recv = take(3)

    per = experts // PLANES
    main = (rows_in or grads_in)[0].shape[1]
    ff = win.shape[1]
    chunks = ff // CHUNK
    me = lax.axis_index("expert")
    plane = me // per
    spot = me % per
    half, low = plane // 2, plane % 2
    order = [
        (1 - half) * 2 + low,
        (1 - half) * 2 + (1 - low),
        half * 2 + (1 - low),
        plane,
    ]

    barrier = pltpu.get_barrier_semaphore()

    def greet(step, carry):
        pl.semaphore_signal(
            barrier, inc=1, device_id={"expert": (me + step) % experts}, device_id_type=MESH
        )
        return carry

    if back:
        gwin_out, gwout_out = gwin_out.at[layer], gwout_out.at[layer]

    def load(weights):
        pltpu.make_async_copy(weights[0], win, weight_sem.at[0]).start()
        pltpu.make_async_copy(weights[1], wout, weight_sem.at[1]).start()

    section = lax.axis_index("section")
    pl.when(section == layer)(lambda: load(own_weights))
    if back:
        pl.when(section != layer)(lambda: load(other_weights))
    lax.fori_loop(1, experts, greet, 0)
    if takes_turns:
        pl.semaphore_signal(
            barrier, inc=1, device_id={"section": 1 - section}, device_id_type=MESH
        )
        pl.semaphore_wait(barrier, experts)
        for lane in range(2):
            pltpu.make_async_remote_copy(
                src_ref=own_weights[lane],
                dst_ref=other_weights[lane],
                send_sem=push_send.at[lane],
                recv_sem=push_recv.at[lane],
                device_id={"section": 1 - section},
                device_id_type=MESH,
            ).start()

        def pushed():
            for lane, ref in enumerate(other_weights):
                pltpu.make_async_copy(ref, ref, push_recv.at[lane]).wait()

        @pl.when(section != layer)
        def _():
            pushed()
            load(other_weights)

        pl.when(section == 1)(lambda: pl.semaphore_wait(turn, 1))
    else:
        pl.semaphore_wait(barrier, experts - 1)

    def send(source, target, lane, peer, to_plane):
        pltpu.make_async_remote_copy(
            src_ref=source.at[peer],
            dst_ref=target.at[me],
            send_sem=send_sems.at[lane],
            recv_sem=recv_sems.at[lane, plane],
            device_id={"expert": peer},
            device_id_type=MESH,
        ).start()

    def send_x(source, target, lane, peer):
        pltpu.make_async_remote_copy(
            src_ref=source.at[peer],
            dst_ref=target.at[me],
            send_sem=send_x_sems.at[lane],
            recv_sem=recv_x_sems.at[lane],
            device_id={"expert": peer},
            device_id_type=MESH,
        ).start()

    def own(source, target, sem):
        pltpu.make_async_copy(source.at[me], target.at[me], sem).start()

    def send_all_x(pairs):
        def one(step, carry):
            for source, target, lane in pairs:
                send_x(source, target, lane, (me + step) % experts)
            return carry

        lax.fori_loop(1, experts, one, 0)
        for source, target, lane in pairs:
            own(source, target, recv_x_sems.at[lane])

    def send_plane(pairs, to_plane, is_own):
        def one(step, carry):
            for source, target, lane in pairs:
                send(source, target, lane, to_plane * per + (spot + step) % per, to_plane)
            return carry

        lax.fori_loop(1 if is_own else 0, per, one, 0)
        if is_own:
            for source, target, lane in pairs:
                own(source, target, recv_sems.at[lane, plane])

    def wait_plane(target, lane, from_plane):
        part = target.at[pl.ds(from_plane * per, per)]
        pltpu.make_async_copy(part, part, recv_sems.at[lane, from_plane]).wait()

    def wait_x(target, lane):
        pltpu.make_async_copy(target, target, recv_x_sems.at[lane]).wait()

    def wait_sent(source, lane):
        part = source.at[pl.ds(0, experts - 1)]
        pltpu.make_async_copy(part, part, send_sems.at[lane]).wait()

    def wait_sent_x(source, lane):
        part = source.at[pl.ds(0, experts - 1)]
        pltpu.make_async_copy(part, part, send_x_sems.at[lane]).wait()

    first_pairs, first_x = [], []
    if ahead:
        first_pairs.append((rows_in[0], row_land, 0))
        first_x.append((rows_in[1], row_land_x, 0))
    if back:
        first_pairs.append((grads_in[0], grad_land, 1))
        first_x.append((grads_in[1], grad_land_x, 1))
    send_all_x(first_x)
    for at, to_plane in enumerate(order):
        send_plane(first_pairs, to_plane, at == 3)

    tall = experts * 16
    tile_rows = lax.broadcasted_iota(jnp.int32, (experts * extra, tall), 0)
    tile_cols = lax.broadcasted_iota(jnp.int32, (experts * extra, tall), 1)
    parts = win.shape[0] // 256
    picks = [
        (tile_cols == (tile_rows // extra) * 16 + q * extra + tile_rows % extra).astype(BF)
        for q in range(parts)
    ]

    def gather_x(landed):
        flat = landed[...].reshape(tall, 256)
        return jnp.concatenate([dot(pick, flat, NN, BF) for pick in picks], axis=1)

    def spread_x(values):
        total = dot(picks[0], values[:, :256], TN)
        for q in range(1, parts):
            total += dot(picks[q], values[:, q * 256 : (q + 1) * 256], TN)
        return total.astype(BF).reshape(experts, 16, 256)

    def run(rows, grads, is_first):
        count = (rows if rows is not None else grads).shape[0]

        def one(step, carry):
            cols = pl.ds(pl.multiple_of(step * CHUNK, CHUNK), CHUNK)
            wide = win[:, cols]
            deep = wout[cols, :]
            active, slope = gelu_and_slope(dot(rows, wide, NN))
            active = active.astype(BF)
            if ahead:
                row_acc[pl.ds(0, count)] += dot(active, deep, NN)
            if back:
                grad_hidden = (dot(grads, deep, NT) * slope).astype(BF)
                grad_acc[pl.ds(0, count)] += dot(grad_hidden, wide, NT)
                term_in = dot(rows, grad_hidden, TN)
                term_out = dot(active, grads, TN)
                if is_first:
                    gwin[:, cols] = term_in
                    gwout[cols, :] = term_out
                else:
                    gwin[:, cols] += term_in
                    gwout[cols, :] += term_out
            return carry

        if ahead:
            row_acc[pl.ds(0, count)] = jnp.zeros((count, row_acc.shape[1]), F32)
        if back:
            grad_acc[pl.ds(0, count)] = jnp.zeros((count, grad_acc.shape[1]), F32)
        lax.fori_loop(0, chunks, one, 0)

    last_pairs, last_x = [], []
    if ahead:
        last_pairs.append((row_stage, produced_out[0], 2))
        last_x.append((row_stage_x, produced_out[1], 2))
        wait_x(row_land_x, 0)
    if back:
        last_pairs.append((grad_stage, returned_out[0], 3))
        last_x.append((grad_stage_x, returned_out[1], 3))
        wait_x(grad_land_x, 1)
    pltpu.make_async_copy(win, win, weight_sem.at[0]).wait()
    pltpu.make_async_copy(wout, wout, weight_sem.at[1]).wait()

    few = experts * extra
    if ahead:
        rows_x = gather_x(row_land_x)
        if kept_out:
            kept_out[1][...] = rows_x
    else:
        rows_x = kept_in[1][...]
    grads_x = gather_x(grad_land_x) if back else None
    width = win.shape[0]
    block = per * main
    for at in (3, 0, 1, 2):
        from_plane = order[at]
        places = pl.ds(from_plane * per, per)
        rows = grads = None
        if ahead:
            wait_plane(row_land, 0, from_plane)
            rows = row_land[places].reshape(block, width)
            if kept_out:
                kept_out[0][places] = row_land[places]
        else:
            rows = kept_in[0][places].reshape(block, width)
        if back:
            wait_plane(grad_land, 1, from_plane)
            grads = grad_land[places].reshape(block, width)
        if at == 3:
            rows = jnp.concatenate([rows, rows_x])
            if back:
                grads = jnp.concatenate([grads, grads_x])
        run(rows, grads, at == 3)
        if ahead:
            row_stage[places] = row_acc[:block].astype(BF).reshape(per, main, width)
        if back:
            grad_stage[places] = grad_acc[:block].astype(BF).reshape(per, main, width)
        if at == 3:
            if ahead:
                row_stage_x[...] = spread_x(row_acc[pl.ds(block, few)].astype(BF))
            if back:
                grad_stage_x[...] = spread_x(grad_acc[pl.ds(block, few)].astype(BF))
            send_all_x(last_x)
        send_plane(last_pairs, from_plane, at == 3)

    if takes_turns:
        pl.when(section == 0)(
            lambda: pl.semaphore_signal(
                turn, inc=1, device_id={"section": 1 - section}, device_id_type=MESH
            )
        )
    if back:
        for at in range(chunks):
            slot = at % 2
            span = slice(at * CHUNK, (at + 1) * CHUNK)
            if at >= 2:
                pltpu.make_async_copy(
                    fold.at[slot], gwin_out.at[:, span], fold_sem.at[slot]
                ).wait()
            fold[slot] = gwin[:, span].astype(BF)
            pltpu.make_async_copy(fold.at[slot], gwin_out.at[:, span], fold_sem.at[slot]).start()
        for slot in range(2):
            pltpu.make_async_copy(
                fold.at[slot], gwin_out.at[:, slice(0, CHUNK)], fold_sem.at[slot]
            ).wait()
        rows_of = ff // 6
        for at in range(6):
            span = slice(at * rows_of, (at + 1) * rows_of)
            wout[span, :] = gwout[span, :].astype(BF)
            pltpu.make_async_copy(wout.at[span, :], gwout_out.at[span, :], weight_sem.at[1]).start()
        pltpu.make_async_copy(wout, gwout_out, weight_sem.at[1]).wait()

    if takes_turns:
        pl.when(section == layer)(pushed)
        for lane, ref in enumerate(own_weights):
            pltpu.make_async_copy(ref, ref, push_send.at[lane]).wait()
    for source, target, lane in first_pairs:
        wait_sent(source, lane)
    for source, target, lane in first_x + last_x:
        wait_sent_x(source, lane)
    for source, target, lane in last_pairs:
        wait_sent(source, lane)
        for from_plane in range(PLANES):
            wait_plane(target, lane, from_plane)
    for source, target, lane in last_x:
        wait_x(target, lane)


def moe(ahead, back, collective, extra, layer, rows, grads, kept, own, other, stacked=()):
    lead = rows if ahead else grads
    experts, main, width = lead[0].shape
    ff = own[0].shape[1]
    few = experts * extra
    per = experts // PLANES
    block = per * main
    tall = jax.ShapeDtypeStruct((experts, main, width), BF)
    small = jax.ShapeDtypeStruct((experts, 16, 256), BF)
    vmem = pl.BlockSpec(memory_space=pltpu.VMEM)
    hbm = pl.BlockSpec(memory_space=pl.ANY)
    operands, in_specs = [], []
    for pair in (rows if ahead else (), grads if back else (), kept if back and not ahead else ()):
        operands += list(pair)
        in_specs += [vmem] * len(pair)
    operands += [*own, *other, *stacked]
    in_specs += [hbm] * (len(own) + len(other) + len(stacked))
    out_shape, out_specs = [], []
    if ahead:
        out_shape += [tall, small]
        out_specs += [vmem, vmem]
        if not back:
            out_shape += [tall, jax.ShapeDtypeStruct((few, width), BF)]
            out_specs += [vmem, vmem]
    if back:
        out_shape += [tall, small]
        out_specs += [vmem, vmem]
        out_shape += [
            jax.ShapeDtypeStruct((2, width, ff), BF),
            jax.ShapeDtypeStruct((2, ff, width), BF),
        ]
        out_specs += [hbm, hbm]
    if not back:
        out_shape += [jax.ShapeDtypeStruct(part.shape, BF) for part in own]
        out_specs += [hbm, hbm]
    aliases = {}
    if stacked:
        last = len(operands) - 2
        aliases = {last: len(out_shape) - 2, last + 1: len(out_shape) - 1}
    scratch = [
        pltpu.VMEM((width, ff), BF),
        pltpu.VMEM((ff, width), BF),
        pltpu.SemaphoreType.DMA((2,)),
    ]
    work = [
        pltpu.VMEM((experts, main, width), BF),
        pltpu.VMEM((experts, 16, 256), BF),
        pltpu.VMEM((experts, main, width), BF),
        pltpu.VMEM((experts, 16, 256), BF),
        pltpu.VMEM((block + few, width), F32),
    ]
    if ahead:
        scratch += work
    if back:
        scratch += work + [
            pltpu.VMEM((width, ff), F32),
            pltpu.VMEM((ff, width), F32),
            pltpu.VMEM((2, width, CHUNK), BF),
            pltpu.SemaphoreType.DMA((2,)),
        ]
    scratch += [
        pltpu.SemaphoreType.DMA((4,)),
        pltpu.SemaphoreType.DMA((4, PLANES)),
        pltpu.SemaphoreType.DMA((4,)),
        pltpu.SemaphoreType.DMA((4,)),
    ]
    if ahead and not back:
        scratch += [
            pltpu.SemaphoreType.REGULAR,
            pltpu.SemaphoreType.DMA((2,)),
            pltpu.SemaphoreType.DMA((2,)),
        ]
    return pl.pallas_call(
        functools.partial(moe_kernel, experts, extra, layer, ahead, back),
        out_shape=out_shape,
        in_specs=in_specs,
        out_specs=out_specs,
        scratch_shapes=scratch,
        input_output_aliases=aliases,
        cost_estimate=pl.CostEstimate(
            flops=(4 * ahead + 6 * back) * experts * main * width * ff,
            bytes_accessed=40 * 2**20 * (ahead + back),
            transcendentals=0,
        ),
        compiler_params=pltpu.CompilerParams(
            collective_id=collective, has_side_effects=True, vmem_limit_bytes=60 * 2**20
        ),
        name="moe_%d%d" % (ahead, back),
    )(*operands)


def pieces_of(experts, rows):
    return 4 if rows % (64 * experts) == 0 else 3


def merge_kernel(
    experts, main0, main1, small0, small1, out0, out1, grad0, grad1, wins, wouts,
    total, total_small, land_in, land_out, grad_in, grad_out, section_out, section_grad,
    own, mate, land1, land2, acc, own_s, mate_s, land1_s, land2_s,
    load_sems, mate_send, mate_recv, mate_recv_s, wide_send, wide_recv, hand_load,
    send_sems, send_s_sems, rs1, rs1_s, rs2, rs2_s, ag2, ag2_s, ag1, ag1_s,
    fold_in, fold_out, fold_loads, fold_stores,
):
    per = experts // PLANES
    me = lax.axis_index("expert")
    section = lax.axis_index("section")
    plane, spot = me // per, me % per
    rows, rows_s = own.shape[0], own_s.shape[0]
    pieces = pieces_of(experts, rows)
    size = rows // pieces
    step_rows = 48 if size % (48 * experts) == 0 else 16
    partner = {"section": 1 - section}

    barrier = pltpu.get_barrier_semaphore()

    def greet(target):
        pl.semaphore_signal(barrier, inc=1, device_id=target, device_id_type=MESH)

    greet(partner)

    def greet_plane(step, carry):
        greet({"expert": plane * per + (spot + step) % per})
        return carry

    def greet_column(step, carry):
        greet({"expert": ((plane + step) % PLANES) * per + spot})
        return carry

    lax.fori_loop(1, per, greet_plane, 0)
    lax.fori_loop(1, PLANES, greet_column, 0)
    pl.semaphore_wait(barrier, per + PLANES - 1)

    def remote(source, target, send, recv, where):
        pltpu.make_async_remote_copy(
            src_ref=source, dst_ref=target, send_sem=send, recv_sem=recv,
            device_id=where, device_id_type=MESH,
        ).start()

    def wait(part, sem):
        pltpu.make_async_copy(part, part, sem).wait()

    def at(start, size):
        return pl.ds(pl.multiple_of(start, 16), size)

    in_plane = lambda j: plane * per + j
    in_column = lambda j: j * per + spot
    by_plane = (per, spot, in_plane, PLANES, plane, in_column)
    by_column = (PLANES, plane, in_column, per, spot, in_plane)
    parts = [(p, p * size) + (by_column if p == 1 else by_plane) for p in range(pieces)]
    lows = [0]
    for part in parts:
        lows.append(lows[-1] + size // part[2])

    def begin(own_main, own_small, own_hand, other_main, other_small, other_hand):
        pltpu.make_async_copy(own_main, own, load_sems.at[0]).start()
        pltpu.make_async_copy(own_small, own_s, load_sems.at[1]).start()
        remote(other_small, mate_s, mate_send.at[1], mate_recv_s.at[0], partner)
        for p, base, n1, i1, _, _, _, _ in parts:
            block = size // n1

            def hand(step, carry):
                j = (i1 + step) % n1
                part = at(base + j * block, block)
                remote(other_main.at[part], mate.at[part], mate_send.at[0],
                       mate_recv.at[p, j], partner)
                return carry

            lax.fori_loop(1, n1 + 1, hand, 0)
        for lane, target in enumerate((section_out, section_grad)):
            mine = target.at[section]
            pltpu.make_async_copy(own_hand[lane], mine, hand_load.at[lane]).start()
            remote(
                other_hand[lane], mine, wide_send.at[2 + lane], wide_recv.at[2 + lane], partner
            )

    first = (main0, small0, (out0, grad0))
    second = (main1, small1, (out1, grad1))
    pl.when(section == 0)(lambda: begin(*first, *second))
    pl.when(section == 1)(lambda: begin(*second, *first))
    remote(wins.at[1 - section], land_in, wide_send.at[0], wide_recv.at[0], partner)
    remote(wouts.at[1 - section], land_out, wide_send.at[1], wide_recv.at[1], partner)
    wait(own, load_sems.at[0])
    wait(own_s, load_sems.at[1])
    wait(mate_s, mate_recv_s.at[0])
    own_s[...] += mate_s[...]

    def stage1(part):
        p, base, n1, i1, peer1, _, _, _ = part
        block, block_s = size // n1, rows_s // n1

        def out1(step, carry):
            j = (i1 + step) % n1
            wait(mate.at[at(base + j * block, block)], mate_recv.at[p, j])

            def fold(step, carry):
                part = at(base + j * block + step * step_rows, step_rows)
                own[part] = (own[part].astype(F32) + mate[part].astype(F32)).astype(BF)
                return carry

            lax.fori_loop(0, block // step_rows, fold, 0)
            where = {"expert": peer1(j)}
            remote(own.at[at(base + j * block, block)], land1.at[at(base + i1 * block, block)],
                   send_sems.at[p, 0], rs1.at[p, i1], where)
            if p == 0:
                remote(own_s.at[at(j * block_s, block_s)], land1_s.at[at(i1 * block_s, block_s)],
                       send_s_sems.at[0], rs1_s.at[i1], where)
            return carry

        lax.fori_loop(1, n1, out1, 0)

    def stage2(part):
        p, base, n1, i1, _, n2, i2, peer2 = part
        block, block_s = size // n1, rows_s // n1
        sub, sub_s = size // (n1 * n2), rows_s // (n1 * n2)
        low = lows[p]
        wait(mate.at[at(base + i1 * block, block)], mate_recv.at[p, i1])

        def in1(step, carry):
            j = (i1 + step) % n1
            wait(land1.at[at(base + j * block, block)], rs1.at[p, j])
            if p == 0:
                wait(land1_s.at[at(j * block_s, block_s)], rs1_s.at[j])
            return carry

        lax.fori_loop(1, n1, in1, 0)

        def sum1(k):
            def one(step, carry):
                place = k * sub + step * step_rows
                part = at(base + i1 * block + place, step_rows)
                value = own[part].astype(F32) + mate[part].astype(F32)

                def add(other, value):
                    far = at(base + ((i1 + other) % n1) * block + place, step_rows)
                    return value + land1[far].astype(F32)

                value = lax.fori_loop(1, n1, add, value)
                own[part] = value.astype(BF)
                acc[at(low + place, step_rows)] = value
                return carry

            lax.fori_loop(0, sub // step_rows, one, 0)
            if p == 0:
                part = at(i1 * block_s + k * sub_s, sub_s)

                def add_s(other, value):
                    far = at(((i1 + other) % n1) * block_s + k * sub_s, sub_s)
                    return value + land1_s[far]

                own_s[part] = lax.fori_loop(1, n1, add_s, own_s[part])

        def out2(step, carry):
            k = (i2 + step) % n2
            sum1(k)
            where = {"expert": peer2(k)}
            remote(own.at[at(base + i1 * block + k * sub, sub)],
                   land2.at[at(low + i2 * sub, sub)], send_sems.at[p, 1], rs2.at[p, i2], where)
            if p == 0:
                remote(own_s.at[at(i1 * block_s + k * sub_s, sub_s)],
                       land2_s.at[at(i2 * sub_s, sub_s)], send_s_sems.at[1], rs2_s.at[i2], where)
            return carry

        lax.fori_loop(1, n2, out2, 0)
        sum1(i2)

    def stage3(part):
        p, base, n1, i1, _, n2, i2, peer2 = part
        block, block_s = size // n1, rows_s // n1
        sub, sub_s = size // (n1 * n2), rows_s // (n1 * n2)
        low = lows[p]

        def in2(step, carry):
            k = (i2 + step) % n2
            wait(land2.at[at(low + k * sub, sub)], rs2.at[p, k])
            if p == 0:
                wait(land2_s.at[at(k * sub_s, sub_s)], rs2_s.at[k])
            return carry

        lax.fori_loop(1, n2, in2, 0)

        def sum2(step, carry):
            place = step * step_rows
            value = acc[at(low + i2 * sub + place, step_rows)]

            def add(other, value):
                far = at(low + ((i2 + other) % n2) * sub + place, step_rows)
                return value + land2[far].astype(F32)

            value = lax.fori_loop(1, n2, add, value)
            total[at(base + i1 * block + i2 * sub + place, step_rows)] = value.astype(BF)
            return carry

        lax.fori_loop(0, sub // step_rows, sum2, 0)
        home = at(base + i1 * block + i2 * sub, sub)
        home_s = at(i1 * block_s + i2 * sub_s, sub_s)
        if p == 0:

            def add2_s(other, value):
                return value + land2_s[at(((i2 + other) % n2) * sub_s, sub_s)]

            total_small[home_s] = lax.fori_loop(1, n2, add2_s, own_s[home_s])

        def share2(step, carry):
            where = {"expert": peer2((i2 + step) % n2)}
            remote(total.at[home], total.at[home], send_sems.at[p, 2], ag2.at[p, i2], where)
            if p == 0:
                remote(total_small.at[home_s], total_small.at[home_s], send_s_sems.at[2],
                       ag2_s.at[i2], where)
            return carry

        lax.fori_loop(1, n2, share2, 0)

    def stage4(part):
        p, base, n1, i1, peer1, n2, i2, _ = part
        block, block_s = size // n1, rows_s // n1
        sub, sub_s = size // (n1 * n2), rows_s // (n1 * n2)

        def share1(step, carry):
            k = (i2 + step) % n2
            home = at(base + i1 * block + k * sub, sub)
            home_s = at(i1 * block_s + k * sub_s, sub_s)

            @pl.when(step > 0)
            def _():
                wait(total.at[home], ag2.at[p, k])
                if p == 0:
                    wait(total_small.at[home_s], ag2_s.at[k])

            def one(jump, carry):
                where = {"expert": peer1((i1 + jump) % n1)}
                remote(total.at[home], total.at[home], send_sems.at[p, 3], ag1.at[p, i1], where)
                if p == 0:
                    remote(total_small.at[home_s], total_small.at[home_s], send_s_sems.at[3],
                           ag1_s.at[i1], where)
                return carry

            lax.fori_loop(1, n1, one, 0)
            return carry

        lax.fori_loop(0, n2, share1, 0)

    def add_terms(which):
        terms, landed, result, fold = (
            (wins, land_in, grad_in, fold_in), (wouts, land_out, grad_out, fold_out)
        )[which]
        wait(landed, wide_recv.at[which])
        height = fold.shape[2]
        steps = landed.shape[0] // height

        def fetch(step):
            slot = step % 2
            part = at(step * height, height)
            pltpu.make_async_copy(
                terms.at[section, part], fold.at[0, slot], fold_loads.at[0, slot]
            ).start()
            pltpu.make_async_copy(
                landed.at[part], fold.at[1, slot], fold_loads.at[1, slot]
            ).start()

        fetch(0)

        def one(step, carry):
            slot = step % 2
            pl.when(step + 1 < steps)(lambda: fetch(step + 1))
            for side in range(2):
                wait(fold.at[side, slot], fold_loads.at[side, slot])
            pl.when(step >= 2)(lambda: wait(fold.at[2, slot], fold_stores.at[slot]))
            fold[2, slot] = (fold[0, slot].astype(F32) + fold[1, slot].astype(F32)).astype(BF)
            pltpu.make_async_copy(
                fold.at[2, slot], result.at[at(step * height, height)], fold_stores.at[slot]
            ).start()
            return carry

        lax.fori_loop(0, steps, one, 0)
        for slot in range(2):
            wait(fold.at[2, slot], fold_stores.at[slot])

    order = [(1, 0), (1, 1), (1, 2), (2, 0), (1, 3), (5, 0), (2, 1), (2, 2), (3, 0), (2, 3),
             (3, 1), (3, 2), (4, 0), (3, 3), (5, 1), (4, 1), (4, 2), (4, 3)]
    stages = (None, stage1, stage2, stage3, stage4)
    for stage, p in order:
        if stage == 5:
            add_terms(p)
        elif p < pieces:
            stages[stage](parts[p])
    for p, base, n1, i1, _, n2, _, _ in parts:
        block, block_s = size // n1, rows_s // n1
        sub, sub_s = size // (n1 * n2), rows_s // (n1 * n2)

        def in_last(step, carry):
            j = (i1 + step) % n1
            wait(total.at[at(base + j * block, block)], ag1.at[p, j])
            if p == 0:
                wait(total_small.at[at(j * block_s, block_s)], ag1_s.at[j])
            return carry

        lax.fori_loop(1, n1, in_last, 0)
        for lane, count, count_s in (
            (0, (n1 - 1) * block, (n1 - 1) * block_s),
            (1, (n2 - 1) * sub, (n2 - 1) * sub_s),
            (2, (n2 - 1) * sub, (n2 - 1) * sub_s),
            (3, (n1 - 1) * block, (n1 - 1) * block_s),
        ):
            wait(own.at[pl.ds(0, count)], send_sems.at[p, lane])
            if p == 0:
                wait(own_s.at[pl.ds(0, count_s)], send_s_sems.at[lane])
    wait(mate, mate_send.at[0])
    wait(mate_s, mate_send.at[1])
    wait(land_in, wide_send.at[0])
    wait(land_out, wide_send.at[1])
    for lane, target in enumerate((section_out, section_grad)):
        wait(target.at[section], hand_load.at[lane])
        wait(target.at[section], wide_send.at[2 + lane])
        wait(target.at[1 - section], wide_recv.at[2 + lane])


def merge(experts, mains, smalls, outs, grads, wins, wouts):
    rows, width = mains[0].shape
    rows_s = smalls[0].shape[0]
    per = experts // PLANES
    most, least = max(per, PLANES), min(per, PLANES)
    pieces = pieces_of(experts, rows)
    seconds = (pieces - 1) * (rows // pieces // per) + rows // pieces // PLANES
    vmem = pl.BlockSpec(memory_space=pltpu.VMEM)
    hbm = pl.BlockSpec(memory_space=pl.ANY)
    sems = lambda *shape: pltpu.SemaphoreType.DMA(shape)
    return pl.pallas_call(
        functools.partial(merge_kernel, experts),
        out_shape=[
            jax.ShapeDtypeStruct((rows, width), BF),
            jax.ShapeDtypeStruct((rows_s, 128), F32),
            jax.ShapeDtypeStruct(wins.shape[1:], BF),
            jax.ShapeDtypeStruct(wouts.shape[1:], BF),
            jax.ShapeDtypeStruct(wins.shape[1:], BF),
            jax.ShapeDtypeStruct(wouts.shape[1:], BF),
            jax.ShapeDtypeStruct((2, *outs[0].shape), BF),
            jax.ShapeDtypeStruct((2, *grads[0].shape), F32),
        ],
        in_specs=[hbm] * 10,
        out_specs=[vmem, vmem, hbm, hbm, hbm, hbm, hbm, hbm],
        scratch_shapes=[
            pltpu.VMEM((rows, width), BF),
            pltpu.VMEM((rows, width), BF),
            pltpu.VMEM((rows, width), BF),
            pltpu.VMEM((seconds, width), BF),
            pltpu.VMEM((seconds, width), F32),
            pltpu.VMEM((rows_s, 128), F32),
            pltpu.VMEM((rows_s, 128), F32),
            pltpu.VMEM((rows_s, 128), F32),
            pltpu.VMEM((rows_s // per, 128), F32),
            sems(2), sems(2), sems(pieces, most), sems(1), sems(4), sems(4), sems(2),
            sems(pieces, 4), sems(4), sems(pieces, most), sems(most), sems(pieces, most), sems(most),
            sems(pieces, most), sems(most), sems(pieces, most), sems(most),
            pltpu.VMEM((3, 2, wins.shape[1] // 8, wins.shape[2]), BF),
            pltpu.VMEM((3, 2, wouts.shape[1] // 8, wouts.shape[2]), BF),
            sems(2, 2), sems(2),
        ],
        compiler_params=pltpu.CompilerParams(
            collective_id=3, has_side_effects=True, vmem_limit_bytes=60 * 2**20
        ),
        name="merge",
    )(*mains, *smalls, *outs, *grads, wins, wouts)


def finish_kernel(q_ref, k_ref, v_ref, p_ref, gqkv_ref, gproj_ref):
    width = gproj_ref.shape[1]
    for at, part in enumerate((q_ref, k_ref, v_ref)):
        gqkv_ref[:, at * width : (at + 1) * width] = part[...].astype(F32)
    gproj_ref[...] = p_ref[...].astype(F32)


def finish(total):
    width = total.shape[1]
    steps = 6
    low = width // steps
    return pl.pallas_call(
        finish_kernel,
        grid=(steps,),
        in_specs=[
            pl.BlockSpec((low, width), functools.partial(lambda k, i: (k * steps + i, 0), k))
            for k in range(4)
        ],
        out_specs=[
            pl.BlockSpec((low, 3 * width), lambda i: (i, 0)),
            pl.BlockSpec((low, width), lambda i: (i, 0)),
        ],
        out_shape=[
            jax.ShapeDtypeStruct((width, 3 * width), F32),
            jax.ShapeDtypeStruct((width, width), F32),
        ],
        compiler_params=pltpu.CompilerParams(vmem_limit_bytes=56 * 2**20),
        name="finish",
    )(*[total] * 4)


def shards(
    block_input, cotangent, expert_ids, qkv_weight, query_bias, value_bias, proj_weight,
    proj_bias, attn_gain, ffn_gain, router_weight, in_weight, out_weight,
):
    section = lax.axis_index("section")
    width = block_input.shape[2]
    experts = router_weight.shape[2]
    tokens = block_input.shape[1]
    capacity = capacity_of(tokens, expert_ids.shape[3], experts)
    extra = capacity % 16

    def swapped(array):
        return lax.ppermute(array, "section", SWAP)

    vectors = jnp.concatenate([query_bias, value_bias, proj_bias, attn_gain, ffn_gain])
    own_shared = (qkv_weight[0], proj_weight[0])
    other_shared = tuple(swapped(part) for part in own_shared)
    vectors_other, router_other = swapped(vectors), swapped(router_weight[0])
    own_experts = (in_weight[0, 0], out_weight[0, 0])
    main = capacity - extra
    ids = lax.dynamic_index_in_dim(expert_ids, section, 1, keepdims=False)
    layers = []
    for l in range(2):
        vector = jnp.where(section == l, vectors, vectors_other)
        router = jnp.where(section == l, router_weight[0], router_other)
        router = jnp.pad(router, ((0, 0), (0, 128 - experts)))
        layers.append(
            (own_shared, other_shared, router, vector, *places_of(ids[l], experts, capacity))
        )
    rows = lax.dynamic_index_in_dim(block_input, section, 0, keepdims=False)
    seed = lax.dynamic_index_in_dim(cotangent, section, 0, keepdims=False)

    *inner0, middle0, routed0, gates0, rows0, rows_x0 = attend(
        0, extra, experts, main, layers[0], current=rows
    )
    done0 = moe(
        True, False, 0, extra, 0, (rows0, rows_x0), None, None, own_experts, ()
    )
    other_experts = done0[4:]
    *inner1, middle1, routed1, gates1, rows1, rows_x1, out0, apart0, grads1, grads_x1 = attend(
        1, extra, experts, main, layers[1],
        chain=(middle0, gates0, layers[0][4], *done0[:2], seed),
    )
    done1 = moe(
        True, True, 1, extra, 1, (rows1, rows_x1), (grads1, grads_x1), None, own_experts,
        other_experts,
    )
    seed0, main1, sums1, grad_router1, out1, grads0, grads_x0 = attend_back(
        1, extra, experts, main, layers[1], (out0, *inner1, middle1, routed1, gates1), seed,
        done1[2:4], (*done1[:2], gates0, layers[0][5]), True,
    )
    back0 = moe(
        False, True, 2, extra, 0, None, (grads0, grads_x0), done0[2:4], own_experts,
        other_experts, done1[4:],
    )
    grad0, main0, sums0, grad_router0 = attend_back(
        0, extra, experts, main, layers[0], (rows, *inner0, middle0, routed0, gates0), seed0,
        back0[:2], (apart0,), False,
    )

    def smalls(sums, grad_router):
        small = jnp.concatenate([sums, grad_router]).reshape(-1, 128)
        return jnp.pad(small, ((0, -small.shape[0] % (16 * experts)), (0, 0)))

    small0, small1 = smalls(sums0, grad_router0), smalls(sums1, grad_router1)
    total, small, _, _, grad_win, grad_wout, section_out, section_grad = merge(
        experts, (main0, main1), (small0, small1), (out0, out1), (grad0, seed0), back0[2],
        back0[3],
    )
    grad_qkv, grad_proj = finish(total)
    small = small[: (5 + experts) * width // 128].reshape(5 + experts, width)
    return (
        section_out[None],
        section_grad[None],
        grad_qkv[None],
        small[0][None],
        small[1][None],
        grad_proj[None],
        small[2][None],
        small[3][None],
        small[4][None],
        small[5:].T[None],
        grad_win[None, None],
        grad_wout[None, None],
    )


def solution(mesh):
    vector, matrix = P("section", None), P("section", None, None)
    expert = P("section", "expert", None, None)
    rows = P("section", None, "expert", None)
    return jax.shard_map(
        shards,
        mesh=mesh,
        in_specs=(
            P(None, "expert", None),
            P(None, "expert", None),
            P(None, None, "expert", None),
            matrix, vector, vector, matrix, vector, vector, vector, matrix, expert, expert,
        ),
        out_specs=(
            rows, rows, matrix, vector, vector, matrix, vector, vector, vector, matrix,
            expert, expert,
        ),
        check_vma=False,
    )
```
